32 devices in a mesh: head: 2 (over y), blk: 16 (over z, x, core).
Axes of the slice: x: 2, y: 2, z: 4, core: 2. Of those that a mesh axis runs over, the one named last changes fastest.
Arguments:
- tokens: bfloat16 [2, 2, 1024, 767], P(None, 'head', 'blk'), may hold values from -6 to 6
- segments: int32 [2, 2, 1024], P(None, 'head', 'blk'), may hold values from 0 to 8, as said below
- cotangent: bfloat16 [2, 2, 1024, 767], P(None, 'head', 'blk'), may hold values from -6 to 6
- w_qkv: bfloat16 [768, 2304], P(('head', 'blk')), may hold values from -0.21875 to 0.21875
- w_out: bfloat16 [768, 767], P(('head', 'blk')), may hold values from -1.75 to 1.75
- w_up: bfloat16 [768, 3072], P(('head', 'blk')), may hold values from -0.21875 to 0.21875
- w_down: bfloat16 [3072, 767], P(('head', 'blk')), may hold values from -0.109375 to 0.109375
- gain_one: bfloat16 [768], P(('head', 'blk')), may hold values from 0.5 to 1.5
- gain_two: bfloat16 [768], P(('head', 'blk')), may hold values from 0.5 to 1.5
Outputs:
- mixed: bfloat16 [2, 2, 1024, 767], P(None, 'head', 'blk')
- grad_tokens: float32 [2, 2, 1024, 767], P(None, 'head', 'blk')
- grad_w_qkv: float32 [768, 2304], P(('head', 'blk'))
- grad_w_out: float32 [768, 767], P(('head', 'blk'))
- grad_w_up: float32 [768, 3072], P(('head', 'blk'))
- grad_w_down: float32 [3072, 767], P(('head', 'blk'))
- grad_gain_one: float32 [768], P(('head', 'blk'))
- grad_gain_two: float32 [768], P(('head', 'blk'))
The draws below stay inside these ranges and needn't reach their ends.
Inputs may be any that keep to these rules, and one draw needn't show every extreme that they name: `segments`: in each group positions 0 to 511 carry 0; later positions carry 1 to 8, never falling, every continuation 1024 // 32 positions or more.
All inputs are finite; a program needn't handle non-finite values.
Results may differ from the reference program's by a relative error of at most 0.039.
Values may be sent and summed in bfloat16 or wider, within the bound.
No kernel may reach another device: no remote copies, remote signals or barrier semaphores. Data moves between devices by JAX's collectives and lax.ppermute only.
A program may use at most 384 MiB of HBM per device.

```python
import math
import jax
import jax.numpy as jnp
from jax import lax

D = 768
HEADS = 12
HEAD_DIM = 64
FF = 3072
DR = 767
NC = 8
MICRO = 2
GROUPS = 2
LEN = 1024
PROMPT = 512


def draw_segments(key, part):
    least_len = LEN // 32
    cut_points = jnp.sort(jax.random.randint(key, (MICRO, GROUPS, NC - 1), 0, LEN // 4 + 1), axis=-1)
    cont_starts = PROMPT + least_len * jnp.arange(1, NC, dtype=jnp.int32)[None, None, :] + cut_points
    positions = jnp.arange(LEN, dtype=jnp.int32)
    later = (positions[None, None, :, None] >= cont_starts[:, :, None, :]).astype(jnp.int32)
    in_prompt = (positions >= PROMPT).astype(jnp.int32)[None, None, :]
    return (in_prompt + jnp.sum(later, axis=-1)).astype(jnp.int32)


def levels(own_key, dims, cuts, low, largest):
    def one(dim, shards_of):
        draws = jax.random.uniform(jax.random.fold_in(jax.random.fold_in(own_key, 6), dim), (shards_of,), jnp.float32, low / len(cuts), largest / len(cuts))
        return jnp.repeat(jnp.exp(draws), dims[dim] // shards_of).reshape((-1,) + (1,) * (len(dims) - dim - 1))

    loudness = one(*cuts[0])
    for cut in cuts[1:]:
        loudness = loudness * one(*cut)
    return loudness


def scatter_about(rng, shape, spread, limit, cuts=(), kind=jnp.bfloat16):
    level = levels(rng, shape, cuts, -0.22, 0.18) if cuts else 1.0
    entries = jax.random.normal(rng, shape, jnp.float32) * spread * level
    return jnp.minimum(jnp.maximum(entries, -limit), limit).astype(kind)


def setup_inputs(seed: int = 0) -> dict:
    seeds = jax.random.split(jax.random.key(seed), 10)
    tokens = scatter_about(seeds[0], (MICRO, GROUPS, LEN, DR), 1.0, 6.0, ((1, 2), (2, 16)))
    segments = draw_segments(jax.random.fold_in(seeds[9], 71), 0)
    cotangent = scatter_about(seeds[2], (MICRO, GROUPS, LEN, DR), 1.0, 6.0, ((1, 2), (2, 16)))
    w_qkv = scatter_about(seeds[3], (D, 3 * D), D ** -0.5, 0.21875, ((0, 32),))
    w_out = scatter_about(seeds[4], (D, DR), (max(1, D * 16 // LEN)) ** -0.5, 1.75, ((0, 32),))
    w_up = scatter_about(seeds[5], (D, FF), D ** -0.5, 0.21875, ((0, 32),))
    w_down = scatter_about(seeds[6], (FF, DR), FF ** -0.5, 0.109375, ((0, 32),))
    gain_one = jnp.clip(1.0 + 0.1 * jax.random.normal(seeds[7], (D,), jnp.float32), 0.5, 1.5).astype(jnp.bfloat16)
    gain_two = jnp.clip(1.0 + 0.1 * jax.random.normal(seeds[8], (D,), jnp.float32), 0.5, 1.5).astype(jnp.bfloat16)
    return {"tokens": tokens, "segments": segments, "cotangent": cotangent, "w_qkv": w_qkv, "w_out": w_out, "w_up": w_up, "w_down": w_down, "gain_one": gain_one, "gain_two": gain_two}


@jax.custom_vjp
def low(v):
    return lax.optimization_barrier(v.astype(jnp.bfloat16)).astype(jnp.float32)

@jax.custom_vjp
def low_back(v):
    return v

def low_keep(v):
    return (low(v), None)

def low_pass(kept, grad):
    return (grad,)

def back_keep(v):
    return (v, None)

def back_low(kept, grad):
    return (low(grad),)
low.defvjp(low_keep, low_pass)
low_back.defvjp(back_keep, back_low)

def compress_norm(values, gain):
    total_sum = lax.optimization_barrier(jnp.sum(values, axis=-1, keepdims=True))
    full_vec = jnp.concatenate([values, -total_sum], axis=-1)
    factor = lax.rsqrt(lax.optimization_barrier(jnp.mean(full_vec * full_vec, axis=-1, keepdims=True)) + 1e-05)
    return full_vec * factor * gain

def gelu_tanh(values):
    return jax.nn.gelu(values, approximate=True)

def attention_group(queries, key_rows, value_rows, segment_rows):
    block_rows = min(512, LEN)
    block_count = LEN // block_rows
    score_scale = 1.0 / math.sqrt(HEAD_DIM)
    key_pos = jnp.arange(LEN, dtype=jnp.int32)

    @jax.checkpoint
    def one_block(block_index):
        first_row = block_index * block_rows
        query_block = lax.dynamic_slice_in_dim(queries, first_row, block_rows, 0)
        query_seg = lax.dynamic_slice_in_dim(segment_rows, first_row, block_rows, 0)
        query_pos = first_row + jnp.arange(block_rows, dtype=jnp.int32)
        scores = low_back(score_scale * jnp.einsum('qhd,khd->hqk', query_block, key_rows, precision=lax.Precision.HIGHEST))
        visible = (key_pos[None, :] <= query_pos[:, None]) & ((segment_rows[None, :] == 0) | (segment_rows[None, :] == query_seg[:, None]))
        masked = jnp.where(visible[None], scores, -1e+30)
        row_max = lax.optimization_barrier(jnp.max(masked, axis=-1, keepdims=True))
        exp_terms = jnp.where(visible[None], jnp.exp(masked - row_max), 0.0)
        soft_weights = exp_terms / lax.optimization_barrier(jnp.sum(exp_terms, axis=-1, keepdims=True))
        return jnp.einsum('hqk,khd->qhd', low(soft_weights), value_rows, precision=lax.Precision.HIGHEST)
    outputs = lax.map(one_block, jnp.arange(block_count, dtype=jnp.int32))
    return outputs.reshape(LEN, HEADS, HEAD_DIM)

def layer(token_rows, segment_rows, proj_qkv, proj_out, proj_up, proj_down, norm_one, norm_two):
    normed_one = low(compress_norm(token_rows, norm_one))
    projected = low_back(low(jnp.dot(normed_one, proj_qkv, precision=lax.Precision.HIGHEST)))
    queries = projected[:, :D].reshape(LEN, HEADS, HEAD_DIM)
    key_rows = projected[:, D:2 * D].reshape(LEN, HEADS, HEAD_DIM)
    value_rows = projected[:, 2 * D:].reshape(LEN, HEADS, HEAD_DIM)
    attention = attention_group(queries, key_rows, value_rows, segment_rows).reshape(LEN, D)
    attention = low_back(low(attention))
    residual = token_rows + low_back(jnp.dot(attention, proj_out, precision=lax.Precision.HIGHEST))
    normed_two = low(compress_norm(residual, norm_two))
    hidden = low_back(jnp.dot(normed_two, proj_up, precision=lax.Precision.HIGHEST))
    activated = low(gelu_tanh(hidden))
    return residual + jnp.dot(activated, proj_down, precision=lax.Precision.HIGHEST)

def reference(tokens, segments, cotangent, w_qkv, w_out, w_up, w_down, gain_one, gain_two):
    params = (w_qkv.astype(jnp.float32), w_out.astype(jnp.float32), w_up.astype(jnp.float32), w_down.astype(jnp.float32), gain_one.astype(jnp.float32), gain_two.astype(jnp.float32))
    flat_tokens = tokens.astype(jnp.float32).reshape(MICRO * GROUPS, LEN, DR)
    flat_segments = segments.reshape(MICRO * GROUPS, LEN).astype(jnp.int32)
    flat_cotangent = cotangent.astype(jnp.float32).reshape(MICRO * GROUPS, LEN, DR)

    def one_group(totals, inputs_one):
        token_rows, segment_rows, cotangent_rows = inputs_one

        def forward(token_in, proj_qkv, proj_out, proj_up, proj_down, norm_one, norm_two):
            return layer(token_in, segment_rows, proj_qkv, proj_out, proj_up, proj_down, norm_one, norm_two)
        output, pullback = jax.vjp(forward, token_rows, params[0], params[1], params[2], params[3], params[4], params[5])
        gradients = pullback(cotangent_rows)
        updated = tuple((total + increment for total, increment in zip(totals, gradients[1:])))
        return (updated, (output.astype(jnp.bfloat16), gradients[0]))
    initial = tuple((jnp.zeros_like(matrix) for matrix in params))
    totals, (outputs, token_grads) = lax.scan(one_group, initial, (flat_tokens, flat_segments, flat_cotangent))
    mixed = outputs.reshape(MICRO, GROUPS, LEN, DR)
    grad_tokens = token_grads.reshape(MICRO, GROUPS, LEN, DR)
    return (mixed, grad_tokens, totals[0], totals[1], totals[2], totals[3], totals[4], totals[5])
```

```python
import math

import jax
import jax.numpy as jnp
from jax import lax
from jax.experimental import pallas as pl
from jax.experimental.pallas import tpu as pltpu
from jax.sharding import PartitionSpec as P

HEAD_DIM = 64


def compress_norm(values, gain):
    total_sum = jnp.sum(values, axis=-1, keepdims=True)
    full_vec = jnp.concatenate([values, -total_sum], axis=-1)
    factor = lax.rsqrt(jnp.mean(full_vec * full_vec, axis=-1, keepdims=True) + 1e-05)
    return full_vec * factor * gain


def gelu_tanh(values):
    return jax.nn.gelu(values, approximate=True)


def visibility(query_pos, query_seg, key_pos, key_seg):
    causal = key_pos[:, None, :] <= query_pos[None, :, None]
    shared = (key_seg[:, None, :] == 0) | (key_seg[:, None, :] == query_seg[:, :, None])
    return (causal & shared)[:, :, None, :]


def micro_step(token_block, segment_block, cotangent_block, weights_full, query_pos):
    proj_qkv, proj_out, proj_up, proj_down, norm_one, norm_two = weights_full
    norm_one = norm_one.astype(jnp.float32)
    norm_two = norm_two.astype(jnp.float32)
    group_local, seg_len, resid_width = token_block.shape
    model_width = proj_qkv.shape[0]
    row_count = group_local * seg_len
    score_scale = 1.0 / math.sqrt(HEAD_DIM)
    token_rows = token_block.astype(jnp.float32).reshape(row_count, resid_width)
    normed_f, norm_one_pull = jax.vjp(compress_norm, token_rows, norm_one)
    normed_one = normed_f.astype(jnp.bfloat16)
    projected = jnp.dot(normed_one, proj_qkv, preferred_element_type=jnp.float32).astype(
        jnp.bfloat16
    )
    projected = projected.reshape(group_local, seg_len, 3, model_width)
    head_groups = lax.axis_size("head")
    seg_wide = jnp.broadcast_to(
        segment_block.astype(jnp.bfloat16)[:, :, None, None], (group_local, seg_len, 1, head_groups)
    )
    moved_qkv, moved_seg = (
        lax.all_to_all(projected, "head", split_axis=3, concat_axis=0, tiled=True),
        lax.all_to_all(seg_wide, "head", split_axis=3, concat_axis=0, tiled=True),
    )
    groups = moved_qkv.shape[0]
    head_width = moved_qkv.shape[3]
    heads_here = head_width // HEAD_DIM
    head_shape = (groups, seg_len, heads_here, HEAD_DIM)
    queries = moved_qkv[:, :, 0].reshape(head_shape)
    keys_flat = moved_qkv[:, :, 1]
    values_flat = moved_qkv[:, :, 2]
    keys_local = keys_flat.reshape(head_shape)
    values_local = values_flat.reshape(head_shape)
    seg_bf = moved_seg[:, :, 0, 0]
    seg_here = seg_bf.astype(jnp.int32)
    key_piece = lax.all_gather(keys_flat, "blk", axis=1, tiled=True)
    value_piece = lax.all_gather(values_flat, "blk", axis=1, tiled=True)
    seg_piece = lax.all_gather(seg_bf, "blk", axis=1, tiled=True)
    key_pos = jnp.arange(key_piece.shape[1], dtype=jnp.int32)[None, :]
    running_max = jnp.full((groups, seg_len, heads_here), -1e30, jnp.float32)
    piece_rows = key_piece.shape[1]
    visible = visibility(query_pos, seg_here, key_pos, seg_piece.astype(jnp.int32))
    key_heads = key_piece.reshape(groups, piece_rows, heads_here, HEAD_DIM)
    value_heads = value_piece.reshape(groups, piece_rows, heads_here, HEAD_DIM)
    scores = score_scale * jnp.einsum(
        "gqhd,gkhd->gqhk", queries, key_heads, preferred_element_type=jnp.float32
    )
    masked = jnp.where(visible, scores, -1e30)
    new_max = jnp.maximum(running_max, jnp.max(masked, axis=-1))
    exp_terms = jnp.where(visible, jnp.exp(masked - new_max[..., None]), 0.0)
    new_sum = jnp.sum(exp_terms, axis=-1)
    new_acc = jnp.einsum(
        "gqhk,gkhd->gqhd",
        exp_terms.astype(jnp.bfloat16),
        value_heads,
        preferred_element_type=jnp.float32,
    )
    attn_f = new_acc / new_sum[..., None]
    log_totals = new_max + jnp.log(new_sum)
    attn_heads = attn_f.astype(jnp.bfloat16).reshape(groups, seg_len, head_width)
    attention = lax.all_to_all(attn_heads, "head", split_axis=0, concat_axis=2, tiled=True)
    attn_rows = attention.reshape(row_count, model_width)
    residual = token_rows + jnp.dot(attn_rows, proj_out, preferred_element_type=jnp.float32)
    normed_two_f, norm_two_pull = jax.vjp(compress_norm, residual, norm_two)
    normed_two = normed_two_f.astype(jnp.bfloat16)
    hidden = jnp.dot(normed_two, proj_up, preferred_element_type=jnp.float32)
    activated_f, gelu_pull = jax.vjp(gelu_tanh, hidden)
    activated = activated_f.astype(jnp.bfloat16)
    mixed = (residual + jnp.dot(activated, proj_down, preferred_element_type=jnp.float32)).astype(
        jnp.bfloat16
    )
    cot_rows = cotangent_block.reshape(row_count, resid_width)
    grad_down = jnp.einsum("ra,rb->ab", activated, cot_rows, preferred_element_type=jnp.float32)
    d_activated = jnp.einsum("rb,ab->ra", cot_rows, proj_down, preferred_element_type=jnp.float32)
    (d_hidden,) = gelu_pull(d_activated)
    d_hidden = d_hidden.astype(jnp.bfloat16)
    grad_up = jnp.einsum("ra,rb->ab", normed_two, d_hidden, preferred_element_type=jnp.float32)
    d_normed_two = jnp.einsum("rb,ab->ra", d_hidden, proj_up, preferred_element_type=jnp.float32)
    d_resid_part, grad_gain_two = norm_two_pull(d_normed_two)
    d_residual = cot_rows.astype(jnp.float32) + d_resid_part
    d_sum = d_residual.astype(jnp.bfloat16)
    grad_out = jnp.einsum("ra,rb->ab", attn_rows, d_sum, preferred_element_type=jnp.float32)
    d_attention = jnp.einsum(
        "rb,ab->ra", d_sum, proj_out, preferred_element_type=jnp.float32
    ).astype(jnp.bfloat16)
    d_attention = d_attention.reshape(group_local, seg_len, model_width)
    d_heads_flat = lax.all_to_all(d_attention, "head", split_axis=2, concat_axis=0, tiled=True)
    d_heads = d_heads_flat.reshape(head_shape)
    delta_rows = jnp.sum(d_heads.astype(jnp.float32) * attn_f, axis=-1)
    lse_all, delta_all = (
        lax.all_gather(log_totals, "blk", axis=1, tiled=True),
        lax.all_gather(delta_rows, "blk", axis=1, tiled=True),
    )
    key_piece = lax.all_gather(keys_flat, "blk", axis=1, tiled=True)
    value_piece = lax.all_gather(values_flat, "blk", axis=1, tiled=True)
    seg_piece = lax.all_gather(seg_bf, "blk", axis=1, tiled=True)
    key_pos = jnp.arange(key_piece.shape[1], dtype=jnp.int32)[None, :]
    piece_rows = key_piece.shape[1]
    visible = visibility(query_pos, seg_here, key_pos, seg_piece.astype(jnp.int32))
    key_heads = key_piece.reshape(groups, piece_rows, heads_here, HEAD_DIM)
    value_heads = value_piece.reshape(groups, piece_rows, heads_here, HEAD_DIM)
    scores = score_scale * jnp.einsum(
        "gqhd,gkhd->gqhk", queries, key_heads, preferred_element_type=jnp.float32
    )
    masked = jnp.where(visible, scores, -1e30)
    soft_weights = jnp.where(visible, jnp.exp(masked - log_totals[..., None]), 0.0)
    d_soft = jnp.einsum("gqhd,gkhd->gqhk", d_heads, value_heads, preferred_element_type=jnp.float32)
    d_scores = (soft_weights * (d_soft - delta_rows[..., None])).astype(jnp.bfloat16)
    d_query = score_scale * jnp.einsum(
        "gqhk,gkhd->gqhd", d_scores, key_heads, preferred_element_type=jnp.float32
    )
    queries_flat = moved_qkv[:, :, 0]
    query_piece = lax.all_gather(queries_flat, "blk", axis=1, tiled=True)
    dout_piece = lax.all_gather(d_heads_flat, "blk", axis=1, tiled=True)
    seg_piece = lax.all_gather(seg_bf, "blk", axis=1, tiled=True)
    piece_rows = query_piece.shape[1]
    piece_pos = jnp.arange(piece_rows, dtype=jnp.int32)
    visible = visibility(piece_pos, seg_piece.astype(jnp.int32), query_pos[None, :], seg_here)
    query_heads = query_piece.reshape(groups, piece_rows, heads_here, HEAD_DIM)
    dout_heads = dout_piece.reshape(groups, piece_rows, heads_here, HEAD_DIM)
    scores = score_scale * jnp.einsum(
        "gqhd,gkhd->gqhk", query_heads, keys_local, preferred_element_type=jnp.float32
    )
    masked = jnp.where(visible, scores, -1e30)
    soft_weights = jnp.where(visible, jnp.exp(masked - lse_all[..., None]), 0.0)
    d_soft = jnp.einsum(
        "gqhd,gkhd->gqhk", dout_heads, values_local, preferred_element_type=jnp.float32
    )
    d_scores = (soft_weights * (d_soft - delta_all[..., None])).astype(jnp.bfloat16)
    new_value = jnp.einsum(
        "gqhk,gqhd->gkhd",
        soft_weights.astype(jnp.bfloat16),
        dout_heads,
        preferred_element_type=jnp.float32,
    )
    new_key = score_scale * jnp.einsum(
        "gqhk,gqhd->gkhd", d_scores, query_heads, preferred_element_type=jnp.float32
    )
    d_stacked = (
        jnp.stack([d_query, new_key, new_value], axis=2)
        .astype(jnp.bfloat16)
        .reshape(groups, seg_len, 3, head_width)
    )
    d_projected = lax.all_to_all(d_stacked, "head", split_axis=0, concat_axis=3, tiled=True)
    d_proj_rows = d_projected.reshape(row_count, 3 * model_width)
    grad_qkv = jnp.einsum("ra,rb->ab", normed_one, d_proj_rows, preferred_element_type=jnp.float32)
    d_normed_one = jnp.einsum(
        "rb,ab->ra", d_proj_rows, proj_qkv, preferred_element_type=jnp.float32
    )
    d_token_part, grad_gain_one = norm_one_pull(d_normed_one)
    grad_tokens = (d_residual + d_token_part).reshape(group_local, seg_len, resid_width)
    mixed = mixed.reshape(group_local, seg_len, resid_width)
    return (
        mixed,
        grad_tokens,
        (grad_qkv, grad_out, grad_up, grad_down, grad_gain_one, grad_gain_two),
    )


def on_device(tokens, segments, cotangent, w_qkv, w_out, w_up, w_down, gain_one, gain_two):
    micro_count = tokens.shape[0]
    seg_len = tokens.shape[2]
    query_pos = lax.axis_index("blk") * seg_len + jnp.arange(seg_len, dtype=jnp.int32)
    mixed_list = []
    token_grad_list = []
    grad_terms = []
    for batch_index in range(micro_count):
        weights_full = (
            lax.all_gather(w_qkv, ("head", "blk"), axis=0, tiled=True),
            lax.all_gather(w_out, ("head", "blk"), axis=0, tiled=True),
            lax.all_gather(w_up, ("head", "blk"), axis=0, tiled=True),
            lax.all_gather(w_down, ("head", "blk"), axis=0, tiled=True),
            lax.all_gather(gain_one, ("head", "blk"), axis=0, tiled=True),
            lax.all_gather(gain_two, ("head", "blk"), axis=0, tiled=True),
        )
        mixed, grad_tokens, gradients = micro_step(
            tokens[batch_index],
            segments[batch_index],
            cotangent[batch_index],
            weights_full,
            query_pos,
        )
        mixed_list.append(mixed)
        token_grad_list.append(grad_tokens)
        grad_terms.append(
            (
                lax.psum_scatter(gradients[0], ("head", "blk"), scatter_dimension=0, tiled=True),
                lax.psum_scatter(gradients[1], ("head", "blk"), scatter_dimension=0, tiled=True),
                lax.psum_scatter(gradients[2], ("head", "blk"), scatter_dimension=0, tiled=True),
                lax.psum_scatter(gradients[3], ("head", "blk"), scatter_dimension=0, tiled=True),
                lax.psum_scatter(gradients[4], ("head", "blk"), scatter_dimension=0, tiled=True),
                lax.psum_scatter(gradients[5], ("head", "blk"), scatter_dimension=0, tiled=True),
            )
        )
    summed = grad_terms[0]
    for later_terms in grad_terms[1:]:
        summed = tuple((first + second for first, second in zip(summed, later_terms)))
    mixed_all = jnp.stack(mixed_list, axis=0)
    token_grads = jnp.stack(token_grad_list, axis=0)
    return (
        mixed_all,
        token_grads,
        summed[0],
        summed[1],
        summed[2],
        summed[3],
        summed[4],
        summed[5],
    )


CORE, AXIS_X, AXIS_Z_NEAR, AXIS_Z_FAR, AXIS_Y = 1, 2, 4, 8, 16
DEVICES = 32
WIDTH = 768
HALF = 384
UNITS = 1536
ROWS = 256
POSITIONS = 1024
VMEM_BYTES = 60 * 1024 * 1024


def swap(array, bit, keep=lambda source: True):
    pairs = [(i, i ^ bit) for i in range(DEVICES) if keep(i)]
    return lax.ppermute(array, ("head", "blk"), pairs)


def upward(bit):
    return lambda source: source & bit == 0


def downward(bit):
    return lambda source: source & bit != 0


def dot(a, b):
    return lax.dot_general(a, b, (((1,), (0,)), ((), ())), preferred_element_type=jnp.float32)


def dot_nt(a, b):
    return lax.dot_general(a, b, (((1,), (1,)), ((), ())), preferred_element_type=jnp.float32)


def dot_tn(a, b):
    return lax.dot_general(a, b, (((0,), (0,)), ((), ())), preferred_element_type=jnp.float32)


def run_copies(copies):
    for copy in copies:
        copy.start()
    for copy in copies:
        copy.wait()


def lanes(rows):
    return lax.broadcasted_iota(jnp.int32, (rows, WIDTH), 1)


def norm_rows(values, lane):
    inner = jnp.where(lane < WIDTH - 1, values, 0.0)
    total = jnp.sum(inner, axis=-1, keepdims=True)
    full = jnp.where(lane == WIDTH - 1, -total, inner)
    factor = lax.rsqrt(jnp.mean(full * full, axis=-1, keepdims=True) + 1e-05)
    return full * factor, factor


def norm_rows_back(d_normed, normed, factor, lane):
    inner = jnp.mean(d_normed * normed, axis=-1, keepdims=True)
    d_full = factor * (d_normed - normed * inner)
    last = jnp.sum(jnp.where(lane == WIDTH - 1, d_full, 0.0), axis=-1, keepdims=True)
    return jnp.where(lane < WIDTH - 1, d_full - last, 0.0)


def piece_chip(which, pair, entry):
    z_bits = (entry & 3) << 1
    other = entry >> 2
    return z_bits | ((other | pair << 3) if which == 0 else (other << 3 | pair))


def gather_weights(first, second):
    cut = first.shape[-1]
    joined = jnp.concatenate([first, second], axis=-1)[None]
    two = jnp.concatenate([joined, swap(joined, AXIS_Z_NEAR)], axis=0)
    far = swap(two, AXIS_Z_FAR)
    four_a = jnp.concatenate([two[..., :cut], far[..., :cut]], axis=0)
    four_b = jnp.concatenate([two[..., cut:], far[..., cut:]], axis=0)
    eight_a = jnp.concatenate([four_a, swap(four_a, AXIS_X)], axis=0)
    eight_b = jnp.concatenate([four_b, swap(four_b, AXIS_Y)], axis=0)
    return eight_a, swap(eight_a, AXIS_Y), eight_b, swap(eight_b, AXIS_X)


def reduce_weights(pieces):
    keep_a, send_a, keep_b, send_b = pieces
    eight_a = keep_a.astype(jnp.float32) + swap(send_a, AXIS_Y).astype(jnp.float32)
    eight_b = keep_b.astype(jnp.float32) + swap(send_b, AXIS_X).astype(jnp.float32)
    eight_a = eight_a.astype(jnp.bfloat16)
    eight_b = eight_b.astype(jnp.bfloat16)
    four_a = eight_a[:4].astype(jnp.float32) + swap(eight_a[4:], AXIS_X).astype(jnp.float32)
    four_b = eight_b[:4].astype(jnp.float32) + swap(eight_b[4:], AXIS_Y).astype(jnp.float32)
    four = jnp.concatenate([four_a, four_b], axis=-1).astype(jnp.bfloat16)
    two = four[:2].astype(jnp.float32) + swap(four[2:], AXIS_Z_FAR).astype(jnp.float32)
    two = two.astype(jnp.bfloat16)
    return two[0].astype(jnp.float32) + swap(two[1], AXIS_Z_NEAR).astype(jnp.float32)


def piece_copies(pieces, targets, chip, rows, sem, base, outward=False):
    copies = []
    for which in range(2):
        for pair in range(2):
            source = pieces[which * 2 + pair]
            for entry in range(8):
                block = chip ^ piece_chip(which, pair, entry)
                at = pl.multiple_of(block * rows, 16)
                here = targets[which].at[pl.ds(at, rows), :]
                there = source.at[entry]
                ends = (here, there) if outward else (there, here)
                copies.append(pltpu.make_async_copy(*ends, sem.at[base + len(copies)]))
    return copies


def row_pieces(array, whole, place, core, core_bit, sem, base, outward=False):
    copies = []
    for entry in range(8):
        rel = (entry & 3) << 1 | entry >> 2
        block = (place ^ rel) * 2 + (core ^ core_bit)
        at = pl.multiple_of(block * 64, 64)
        here = whole.at[:, pl.ds(at, 64), :]
        there = array.at[entry]
        ends = (here, there) if outward else (there, here)
        copies.append(pltpu.make_async_copy(*ends, sem.at[base + len(copies)]))
    return copies


def forward_kernel(
    ids, tok_mine, tok_other, w0, w1, w2, w3,
    attn_out, query_out, kv_out, normed_out, soft_out, wqk_out, wvo_out, wout_out, own_out, gains_out,
    tok, bias, sem,
):
    chip, core = ids[0], ids[1]
    place = lax.rem(chip, 8)
    copies = piece_copies((w0, w1, w2, w3), (wqk_out, wvo_out), chip, 48, sem, 0)
    copies += row_pieces(tok_mine, tok, place, core, 0, sem, 32)
    copies += row_pieces(tok_other, tok, place, core, 1, sem, 40)
    run_copies(copies)
    wout_out[...] = wvo_out[:, HALF:]
    picks = lax.broadcasted_iota(jnp.int32, (8, 128), 0) == lax.broadcasted_iota(
        jnp.int32, (8, 128), 1
    )
    gains_out[...] = dot_nt(picks.astype(jnp.bfloat16), wqk_out[:, WIDTH:])
    gain = gains_out[0:1, :]
    lane = lanes(ROWS)
    for micro in range(2):

        def norm_chunk(index, carry, micro=micro):
            at = pl.multiple_of(index * ROWS, ROWS)
            values = tok[micro, pl.ds(at, ROWS), :].astype(jnp.float32)
            normed = (norm_rows(values, lane)[0] * gain).astype(jnp.bfloat16)
            normed_out[micro, pl.ds(at, ROWS), :] = normed
            kv_out[micro, pl.ds(at, ROWS), :HALF] = dot(normed, wqk_out[:, HALF:WIDTH]).astype(
                jnp.bfloat16
            )
            kv_out[micro, pl.ds(at, ROWS), HALF:] = dot(normed, wvo_out[:, :HALF]).astype(
                jnp.bfloat16
            )
            return carry

        lax.fori_loop(0, POSITIONS // ROWS, norm_chunk, 0)
    first_row = pl.multiple_of(place * 128, 128)
    hot = (lax.broadcasted_iota(jnp.int32, (8, WIDTH), 1) == WIDTH - 1).astype(jnp.bfloat16)
    small = lax.broadcasted_iota(jnp.int32, (128, 128), 1) < HEAD_DIM
    for micro in range(2):
        own = tok[micro, pl.ds(first_row, 128), :]
        own_out[micro * 128 : micro * 128 + 128, :] = own
        query = dot(normed_out[micro, pl.ds(first_row, 128), :], wqk_out[:, :HALF])
        query = query.astype(jnp.bfloat16) * jnp.bfloat16(0.125)
        query_out[micro * 128 : micro * 128 + 128, :] = query
        key_seg = dot_nt(hot, tok[micro])[0:1, :]
        query_seg = own[:, WIDTH - 1 :].astype(jnp.float32)
        key_pos = lax.broadcasted_iota(jnp.int32, (128, POSITIONS), 1)
        query_pos = first_row + lax.broadcasted_iota(jnp.int32, (128, POSITIONS), 0)
        seen = (key_pos <= query_pos) & ((key_seg == 0.0) | (key_seg == query_seg))
        bias[...] = jnp.where(seen, 0.0, -1e30)
        for pair in range(3):
            cols = slice(pair * 128, pair * 128 + 128)
            both = query_out[micro * 128 : micro * 128 + 128, cols]
            zero = jnp.zeros_like(both)
            stacked = jnp.concatenate(
                [jnp.where(small, both, zero), jnp.where(small, zero, both)], axis=0
            )
            scores = dot_nt(stacked, kv_out[micro, :, cols])
            scores = scores + jnp.concatenate([bias[...], bias[...]], axis=0)
            top = jnp.max(scores, axis=-1, keepdims=True)
            terms = jnp.exp(scores - top)
            total = jnp.sum(terms, axis=-1, keepdims=True)
            soft = (terms * (1.0 / total)).astype(jnp.bfloat16)
            soft_out[micro * 3 + pair] = soft
            value = kv_out[micro, :, HALF + pair * 128 : HALF + pair * 128 + 128]
            mixed = dot(soft, value)
            attn_out[micro * 128 : micro * 128 + 128, cols] = jnp.where(
                small, mixed[:128], mixed[128:]
            ).astype(jnp.bfloat16)


def feed_kernel(
    ids, gains, attn_mine, attn_other, own, wout_mine, wout_other, cot_mine, cot_other,
    u0, u1, u2, u3, d0, d1, d2, d3,
    attn_out, cot_out, res_out, part_out,
    gu0, gu1, gu2, gu3, gd0, gd1, gd2, gd3,
    wu_a, wu_b, wd_a, wd_b, gu_a, gu_b, gd_a, gd_b, sum_mix, sum_norm, sem,
):
    chip, core = ids[0], ids[1]
    load = piece_copies((u0, u1, u2, u3), (wu_a, wu_b), chip, 48, sem, 0)
    load += piece_copies((d0, d1, d2, d3), (wd_a, wd_b), chip, 96, sem, 32)
    for copy in load:
        copy.start()
    mine_at = pl.multiple_of(core * HALF, 128)
    other_at = pl.multiple_of((1 - core) * HALF, 128)
    attn_out[:, pl.ds(mine_at, HALF)] = attn_mine[...]
    attn_out[:, pl.ds(other_at, HALF)] = attn_other[...]
    for micro in range(2):
        for side, source in ((core, cot_mine), (1 - core, cot_other)):
            at = pl.multiple_of(micro * 128 + side * 64, 64)
            cot_out[pl.ds(at, 64), :] = source[micro]
    lane = lanes(ROWS)
    attn = attn_out[...]
    res_out[:, pl.ds(mine_at, HALF)] = dot(attn, wout_mine[...])
    res_out[:, pl.ds(other_at, HALF)] = dot(attn, wout_other[...])
    own_values = jnp.where(lane < WIDTH - 1, own[...].astype(jnp.float32), 0.0)
    residual = res_out[...] + own_values
    res_out[...] = residual
    normed = (norm_rows(residual, lane)[0] * gains[1:2, :]).astype(jnp.bfloat16)
    cot = cot_out[...]
    for copy in load:
        copy.wait()
    slope = math.sqrt(2.0 / math.pi)
    step = HALF
    sum_mix[...] = jnp.zeros_like(sum_mix)
    sum_norm[...] = jnp.zeros_like(sum_norm)
    for part in range(UNITS // step):
        up, g_up = (wu_a, gu_a) if part < 2 else (wu_b, gu_b)
        cols = slice((part % 2) * step, (part % 2) * step + step)
        rows = slice(part * step, part * step + step)
        hidden = dot(normed, up[:, cols])
        square = hidden * hidden
        wave = jnp.tanh(slope * hidden * (1.0 + 0.044715 * square))
        active = (0.5 * hidden * (1.0 + wave)).astype(jnp.bfloat16)
        grow = 0.5 * (1.0 + wave) + 0.5 * hidden * (1.0 - wave * wave) * slope * (
            1.0 + 3.0 * 0.044715 * square
        )
        d_active = dot_nt(cot[:, :HALF], wd_a[rows, :]) + dot_nt(cot[:, HALF:], wd_b[rows, :])
        d_hidden = (d_active * grow).astype(jnp.bfloat16)
        sum_mix[:, :HALF] += dot(active, wd_a[rows, :])
        sum_mix[:, HALF:] += dot(active, wd_b[rows, :])
        sum_norm[...] += dot_nt(d_hidden, up[:, cols])
        g_up[:, cols] = dot_tn(normed, d_hidden).astype(jnp.bfloat16)
        gd_a[rows, :] = dot_tn(active, cot[:, :HALF]).astype(jnp.bfloat16)
        gd_b[rows, :] = dot_tn(active, cot[:, HALF:]).astype(jnp.bfloat16)
    store = piece_copies((gu0, gu1, gu2, gu3), (gu_a, gu_b), chip, 48, sem, 0, True)
    store += piece_copies((gd0, gd1, gd2, gd3), (gd_a, gd_b), chip, 96, sem, 32, True)
    for copy in store:
        copy.start()
    part_out[:ROWS, :] = sum_mix[...].astype(jnp.bfloat16)
    part_out[ROWS:, :] = sum_norm[...].astype(jnp.bfloat16)
    for copy in store:
        copy.wait()


def backward_kernel(
    ids, gains, residual, part_mine, part_other, cot, attn, wout_mine, wout_other, wqk, wvo,
    query, kv, normed_all, soft,
    mixed_out, dres_out, g0, g1, g2, g3, keep_rows, send_rows,
    g_a, g_b, d_attn, d_kv, d_query, d_rows, d_sum_ref, hold, sem,
):
    chip, core = ids[0], ids[1]
    place = lax.rem(chip, 8)
    first_row = pl.multiple_of(place * 128, 128)
    mine_at = pl.multiple_of(core * HALF, 128)
    other_at = pl.multiple_of((1 - core) * HALF, 128)
    lane = lanes(ROWS)
    res = residual[...]
    mixed = res + part_mine[:ROWS, :].astype(jnp.float32) + part_other[:ROWS, :].astype(jnp.float32)
    hold[...] = mixed
    for micro in range(2):
        at = pl.multiple_of(micro * 128 + core * 64, 64)
        mixed_out[micro] = hold[pl.ds(at, 64), : WIDTH - 1].astype(jnp.bfloat16)
    d_normed = part_mine[ROWS:, :].astype(jnp.float32) + part_other[ROWS:, :].astype(jnp.float32)
    d_normed = d_normed * gains[1:2, :]
    normed_two, factor = norm_rows(res, lane)
    d_res = cot[...].astype(jnp.float32) + norm_rows_back(d_normed, normed_two, factor, lane)
    hold[...] = d_res
    for micro in range(2):
        at = pl.multiple_of(micro * 128 + core * 64, 64)
        dres_out[micro] = hold[pl.ds(at, 64), :]
    d_sum_ref[...] = d_res.astype(jnp.bfloat16)
    d_mine = d_sum_ref[:, pl.ds(mine_at, HALF)]
    d_other = d_sum_ref[:, pl.ds(other_at, HALF)]
    d_heads = dot_nt(d_mine, wout_mine[pl.ds(mine_at, HALF), :]) + dot_nt(
        d_other, wout_other[pl.ds(mine_at, HALF), :]
    )
    d_attn[...] = d_heads.astype(jnp.bfloat16)
    g_b[:, HALF:] = dot_tn(attn[...], d_mine).astype(jnp.bfloat16)
    small = lax.broadcasted_iota(jnp.int32, (128, 128), 1) < HEAD_DIM
    for micro in range(2):
        here = slice(micro * 128, micro * 128 + 128)
        for pair in range(3):
            cols = slice(pair * 128, pair * 128 + 128)
            value_cols = slice(HALF + pair * 128, HALF + pair * 128 + 128)

            def stack(both):
                zero = jnp.zeros_like(both)
                return jnp.concatenate(
                    [jnp.where(small, both, zero), jnp.where(small, zero, both)], axis=0
                )

            d_out = stack(d_attn[here, cols])
            q_both = stack(query[here, cols])
            weights = soft[micro * 3 + pair]
            d_soft = dot_nt(d_out, kv[micro, :, value_cols])
            weights_f = weights.astype(jnp.float32)
            delta = jnp.sum(weights_f * d_soft, axis=-1, keepdims=True)
            d_scores = (weights_f * (d_soft - delta)).astype(jnp.bfloat16)
            d_q = dot(d_scores, kv[micro, :, cols]) * 0.125
            d_query[here, cols] = jnp.where(small, d_q[:128], d_q[128:]).astype(jnp.bfloat16)
            d_kv[micro, :, cols] = dot_tn(d_scores, q_both).astype(jnp.bfloat16)
            d_kv[micro, :, value_cols] = dot_tn(weights, d_out).astype(jnp.bfloat16)
    for micro in range(2):

        def row_chunk(index, carry, micro=micro):
            at = pl.multiple_of(index * ROWS, ROWS)
            d_k = d_kv[micro, pl.ds(at, ROWS), :HALF]
            d_v = d_kv[micro, pl.ds(at, ROWS), HALF:]
            rows = dot_nt(d_k, wqk[:, HALF:WIDTH]) + dot_nt(d_v, wvo[:, :HALF])
            d_rows[micro, pl.ds(at, ROWS), :] = rows.astype(jnp.bfloat16)
            return carry

        lax.fori_loop(0, POSITIONS // ROWS, row_chunk, 0)
        own = d_rows[micro, pl.ds(first_row, 128), :].astype(jnp.float32)
        own = own + dot_nt(d_query[micro * 128 : micro * 128 + 128, :], wqk[:, :HALF])
        d_rows[micro, pl.ds(first_row, 128), :] = own.astype(jnp.bfloat16)
    store = row_pieces(keep_rows, d_rows, place, core, 0, sem, 32, True)
    store += row_pieces(send_rows, d_rows, place, core, 1, sem, 40, True)
    for copy in store:
        copy.start()
    own_0 = normed_all[0, pl.ds(first_row, 128), :]
    own_1 = normed_all[1, pl.ds(first_row, 128), :]
    g_a[:, :HALF] = (dot_tn(own_0, d_query[:128, :]) + dot_tn(own_1, d_query[128:, :])).astype(
        jnp.bfloat16
    )
    g_a[:, HALF:] = (
        dot_tn(normed_all[0], d_kv[0, :, :HALF]) + dot_tn(normed_all[1], d_kv[1, :, :HALF])
    ).astype(jnp.bfloat16)
    g_b[:, :HALF] = (
        dot_tn(normed_all[0], d_kv[0, :, HALF:]) + dot_tn(normed_all[1], d_kv[1, :, HALF:])
    ).astype(jnp.bfloat16)
    run_copies(piece_copies((g0, g1, g2, g3), (g_a, g_b), chip, 48, sem, 0, True))
    for copy in store:
        copy.wait()


def tail_kernel(gains, tokens, d_first, d_second, d_residual, grad_out):
    lane = lanes(128)
    rows = (128, WIDTH)
    values = tokens[...].reshape(rows).astype(jnp.float32)
    normed, factor = norm_rows(values, lane)
    d_normed = d_first[...].reshape(rows).astype(jnp.float32)
    d_normed = d_normed + d_second[...].reshape(rows).astype(jnp.float32)
    d_normed = d_normed * gains[0:1, :]
    out = d_residual[...].reshape(rows) + norm_rows_back(d_normed, normed, factor, lane)
    grad_out[...] = out[:, : WIDTH - 1].reshape(2, 64, WIDTH - 1)


ANY = pl.BlockSpec(memory_space=pl.ANY)
VMEM = pl.BlockSpec(memory_space=pltpu.VMEM)
SMEM = pl.BlockSpec(memory_space=pltpu.SMEM)


def shaped(shape, dtype=jnp.bfloat16):
    return jax.ShapeDtypeStruct(shape, dtype)


def call(kernel, ins, outs, scratch, name):
    return pl.pallas_call(
        kernel,
        in_specs=[spec for spec in ins],
        out_specs=[spec for spec, _ in outs],
        out_shape=[shape for _, shape in outs],
        scratch_shapes=scratch,
        name=name,
        compiler_params=pltpu.CompilerParams(vmem_limit_bytes=VMEM_BYTES),
    )


def pick(core, zero, one):
    return jnp.where(core == 0, zero, one)


def chip_block(core, for_zero, for_one):
    mine = pick(core, for_zero, for_one)
    other = swap(pick(core, for_one, for_zero), CORE)
    return jnp.concatenate([pick(core, mine, other), pick(core, other, mine)], axis=0)


def core_rows(core, block):
    rows = block.shape[0] // 2
    mine = pick(core, block[:rows], block[rows:])
    other = swap(pick(core, block[rows:], block[:rows]), CORE)
    return pick(core, mine, other), pick(core, other, mine)


def on_chip_pair(tokens, segments, cotangent, w_qkv, w_out, w_up, w_down, gain_one, gain_two):
    bf, f32 = jnp.bfloat16, jnp.float32
    device = lax.axis_index("head") * 16 + lax.axis_index("blk")
    core = device % 2
    ids = jnp.stack([device // 2, core]).astype(jnp.int32)
    micro, _, length, narrow = tokens.shape
    own = jnp.concatenate([tokens[:, 0], segments[:, 0, :, None].astype(bf)], axis=-1)
    cot = jnp.pad(cotangent[:, 0], ((0, 0), (0, 0), (0, 1)))
    two = jnp.concatenate([own[None], swap(own, AXIS_Z_NEAR)[None]], axis=0)
    four = jnp.concatenate([two, swap(two, AXIS_Z_FAR, upward(AXIS_Z_FAR))], axis=0)
    eight = jnp.concatenate([four, swap(four, AXIS_X)], axis=0)
    eight_other = swap(eight, CORE)
    out_wide = jnp.pad(w_out, ((0, 0), (0, 1)))
    down_wide = jnp.pad(w_down, ((0, 0), (0, 1)))
    qkv_parts = w_qkv.reshape(-1, 3, 2, HALF)
    attn_halves = [
        jnp.concatenate(
            [qkv_parts[:, 0, k], qkv_parts[:, 1, k], qkv_parts[:, 2, k]]
            + [out_wide[:, k * HALF : k * HALF + HALF]],
            axis=-1,
        )
        for k in range(2)
    ]
    gain_cols = jnp.pad(jnp.stack([gain_one, gain_two], axis=-1), ((0, 0), (0, 126)))
    attn_halves = [
        jnp.concatenate([half[:, :WIDTH], gain_cols, half[:, WIDTH:]], axis=-1)
        for half in attn_halves
    ]
    attn_block = chip_block(core, *attn_halves)
    wide = WIDTH + 128
    unit_rows = w_down.shape[0]
    up_parts = w_up.reshape(w_up.shape[0], -1, 2, unit_rows)
    up_halves = [up_parts[:, :, k].reshape(w_up.shape[0], UNITS) for k in range(2)]
    up_block = chip_block(core, *up_halves)
    attn_pieces = gather_weights(attn_block[:, :wide], attn_block[:, wide:])
    up_pieces = gather_weights(up_block[:, :WIDTH], up_block[:, WIDTH:])
    down_pieces = gather_weights(down_wide[:, :HALF], down_wide[:, HALF:])
    cot_other = swap(cot, CORE)
    attn, query, kv, normed_all, soft, wqk, wvo, wout, own_rows, gains = call(
        forward_kernel,
        [SMEM] + [ANY] * 6,
        [
            (VMEM, shaped((ROWS, HALF))),
            (VMEM, shaped((ROWS, HALF))),
            (VMEM, shaped((2, POSITIONS, WIDTH))),
            (VMEM, shaped((2, POSITIONS, WIDTH))),
            (VMEM, shaped((6, ROWS, POSITIONS))),
            (VMEM, shaped((WIDTH, wide))),
            (VMEM, shaped((WIDTH, WIDTH))),
            (VMEM, shaped((WIDTH, HALF))),
            (VMEM, shaped((ROWS, WIDTH))),
            (VMEM, shaped((8, WIDTH), f32)),
        ],
        [
            pltpu.VMEM((2, POSITIONS, WIDTH), bf),
            pltpu.VMEM((128, POSITIONS), f32),
            pltpu.SemaphoreType.DMA((48,)),
        ],
        "attention_forward",
    )(ids, eight, eight_other, *attn_pieces)
    attn_other = swap(attn, CORE)
    wout_other = swap(wout, CORE)
    outs = call(
        feed_kernel,
        [SMEM] + [VMEM] * 8 + [ANY] * 8,
        [
            (VMEM, shaped((ROWS, WIDTH))),
            (VMEM, shaped((ROWS, WIDTH))),
            (VMEM, shaped((ROWS, WIDTH), f32)),
            (VMEM, shaped((2 * ROWS, WIDTH))),
        ]
        + [(ANY, shaped((8, 48, WIDTH)))] * 4
        + [(ANY, shaped((8, 96, HALF)))] * 4,
        [
            pltpu.VMEM((WIDTH, WIDTH), bf),
            pltpu.VMEM((WIDTH, WIDTH), bf),
            pltpu.VMEM((UNITS, HALF), bf),
            pltpu.VMEM((UNITS, HALF), bf),
            pltpu.VMEM((WIDTH, WIDTH), bf),
            pltpu.VMEM((WIDTH, WIDTH), bf),
            pltpu.VMEM((UNITS, HALF), bf),
            pltpu.VMEM((UNITS, HALF), bf),
            pltpu.VMEM((ROWS, WIDTH), f32),
            pltpu.VMEM((ROWS, WIDTH), f32),
            pltpu.SemaphoreType.DMA((64,)),
        ],
        "feed_forward_and_back",
    )(
        ids, gains, attn, attn_other, own_rows, wout, wout_other, cot, cot_other,
        *up_pieces, *down_pieces,
    )
    attn_all, cot_all, residual, part = outs[:4]
    grad_up_pieces, grad_down_pieces = outs[4:8], outs[8:12]
    part_other = swap(part, CORE)
    outs = call(
        backward_kernel,
        [SMEM] + [VMEM] * 14,
        [(VMEM, shaped((2, 64, WIDTH - 1))), (VMEM, shaped((2, 64, WIDTH), f32))]
        + [(ANY, shaped((8, 48, WIDTH)))] * 4
        + [(ANY, shaped((8, 2, 64, WIDTH)))] * 2,
        [
            pltpu.VMEM((WIDTH, WIDTH), bf),
            pltpu.VMEM((WIDTH, WIDTH), bf),
            pltpu.VMEM((ROWS, HALF), bf),
            pltpu.VMEM((2, POSITIONS, WIDTH), bf),
            pltpu.VMEM((ROWS, HALF), bf),
            pltpu.VMEM((2, POSITIONS, WIDTH), bf),
            pltpu.VMEM((ROWS, WIDTH), bf),
            pltpu.VMEM((ROWS, WIDTH), f32),
            pltpu.SemaphoreType.DMA((48,)),
        ],
        "attention_backward",
    )(
        ids, gains, residual, part, part_other, cot_all, attn_all, wout, wout_other, wqk, wvo,
        query, kv, normed_all, soft,
    )
    mixed, d_residual = outs[:2]
    grad_attn_pieces, keep_rows, send_rows = outs[2:6], outs[6], outs[7]
    up_sum = reduce_weights(grad_up_pieces)
    down_sum = reduce_weights(grad_down_pieces)
    rows_8 = (keep_rows.astype(f32) + swap(send_rows, CORE).astype(f32)).astype(bf)
    rows_4 = (rows_8[:4].astype(f32) + swap(rows_8[4:], AXIS_X).astype(f32)).astype(bf)
    rows_2 = rows_4[:2].astype(f32) + swap(rows_4[2:], AXIS_Z_FAR, downward(AXIS_Z_FAR)).astype(f32)
    rows_2 = rows_2.astype(bf)
    last_rows = swap(rows_2[1], AXIS_Z_NEAR)
    attn_sum = reduce_weights(grad_attn_pieces)
    (grad_tokens,) = call(
        tail_kernel,
        [VMEM] * 5,
        [(VMEM, shaped((2, 64, WIDTH - 1), f32))],
        [],
        "token_gradient",
    )(gains, own, rows_2[0], last_rows, d_residual)
    attn_0, attn_1 = core_rows(core, attn_sum)
    up_0, up_1 = core_rows(core, up_sum)
    grad_qkv = jnp.concatenate(
        [half[:, k * HALF : k * HALF + HALF] for k in range(3) for half in (attn_0, attn_1)],
        axis=-1,
    )
    grad_out = jnp.concatenate([attn_0[:, 3 * HALF :], attn_1[:, 3 * HALF : 4 * HALF - 1]], axis=-1)
    rows = up_0.shape[0]
    grad_up = jnp.stack(
        [up_0.reshape(rows, -1, unit_rows), up_1.reshape(rows, -1, unit_rows)], axis=2
    ).reshape(rows, -1)
    grad_gain_one = jnp.sum(grad_qkv * w_qkv.astype(f32), axis=-1) / gain_one.astype(f32)
    grad_gain_two = jnp.sum(grad_up * w_up.astype(f32), axis=-1) / gain_two.astype(f32)
    return (
        mixed[:, None],
        grad_tokens[:, None],
        grad_qkv,
        grad_out,
        grad_up,
        down_sum[:, : WIDTH - 1],
        grad_gain_one,
        grad_gain_two,
    )


def solution(mesh):
    small_slice = (mesh.shape["head"], mesh.shape["blk"]) == (2, 16)
    placed = (
        P(None, "head", "blk", None),
        P(None, "head", "blk"),
        P(None, "head", "blk", None),
        P(("head", "blk"), None),
        P(("head", "blk"), None),
        P(("head", "blk"), None),
        P(("head", "blk"), None),
        P(("head", "blk")),
        P(("head", "blk")),
    )
    return jax.shard_map(
        on_chip_pair if small_slice else on_device,
        mesh=mesh,
        in_specs=placed,
        out_specs=(
            P(None, "head", "blk", None),
            P(None, "head", "blk", None),
            P(("head", "blk"), None),
            P(("head", "blk"), None),
            P(("head", "blk"), None),
            P(("head", "blk"), None),
            P(("head", "blk")),
            P(("head", "blk")),
        ),
        check_vma=False,
    )
```

```python
import math

import jax
import jax.numpy as jnp
from jax import lax
from jax.experimental import pallas as pl
from jax.experimental.pallas import tpu as pltpu
from jax.sharding import PartitionSpec as P

HEAD_DIM = 64


def compress_norm(values, gain):
    total_sum = jnp.sum(values, axis=-1, keepdims=True)
    full_vec = jnp.concatenate([values, -total_sum], axis=-1)
    factor = lax.rsqrt(jnp.mean(full_vec * full_vec, axis=-1, keepdims=True) + 1e-05)
    return full_vec * factor * gain


def gelu_tanh(values):
    return jax.nn.gelu(values, approximate=True)


def visibility(query_pos, query_seg, key_pos, key_seg):
    causal = key_pos[:, None, :] <= query_pos[None, :, None]
    shared = (key_seg[:, None, :] == 0) | (key_seg[:, None, :] == query_seg[:, :, None])
    return (causal & shared)[:, :, None, :]


def micro_step(token_block, segment_block, cotangent_block, weights_full, query_pos):
    proj_qkv, proj_out, proj_up, proj_down, norm_one, norm_two = weights_full
    norm_one = norm_one.astype(jnp.float32)
    norm_two = norm_two.astype(jnp.float32)
    group_local, seg_len, resid_width = token_block.shape
    model_width = proj_qkv.shape[0]
    row_count = group_local * seg_len
    score_scale = 1.0 / math.sqrt(HEAD_DIM)
    token_rows = token_block.astype(jnp.float32).reshape(row_count, resid_width)
    normed_f, norm_one_pull = jax.vjp(compress_norm, token_rows, norm_one)
    normed_one = normed_f.astype(jnp.bfloat16)
    projected = jnp.dot(normed_one, proj_qkv, preferred_element_type=jnp.float32).astype(
        jnp.bfloat16
    )
    projected = projected.reshape(group_local, seg_len, 3, model_width)
    head_groups = lax.axis_size("head")
    seg_wide = jnp.broadcast_to(
        segment_block.astype(jnp.bfloat16)[:, :, None, None], (group_local, seg_len, 1, head_groups)
    )
    moved_qkv, moved_seg = (
        lax.all_to_all(projected, "head", split_axis=3, concat_axis=0, tiled=True),
        lax.all_to_all(seg_wide, "head", split_axis=3, concat_axis=0, tiled=True),
    )
    groups = moved_qkv.shape[0]
    head_width = moved_qkv.shape[3]
    heads_here = head_width // HEAD_DIM
    head_shape = (groups, seg_len, heads_here, HEAD_DIM)
    queries = moved_qkv[:, :, 0].reshape(head_shape)
    keys_flat = moved_qkv[:, :, 1]
    values_flat = moved_qkv[:, :, 2]
    keys_local = keys_flat.reshape(head_shape)
    values_local = values_flat.reshape(head_shape)
    seg_bf = moved_seg[:, :, 0, 0]
    seg_here = seg_bf.astype(jnp.int32)
    key_piece = lax.all_gather(keys_flat, "blk", axis=1, tiled=True)
    value_piece = lax.all_gather(values_flat, "blk", axis=1, tiled=True)
    seg_piece = lax.all_gather(seg_bf, "blk", axis=1, tiled=True)
    key_pos = jnp.arange(key_piece.shape[1], dtype=jnp.int32)[None, :]
    running_max = jnp.full((groups, seg_len, heads_here), -1e30, jnp.float32)
    piece_rows = key_piece.shape[1]
    visible = visibility(query_pos, seg_here, key_pos, seg_piece.astype(jnp.int32))
    key_heads = key_piece.reshape(groups, piece_rows, heads_here, HEAD_DIM)
    value_heads = value_piece.reshape(groups, piece_rows, heads_here, HEAD_DIM)
    scores = score_scale * jnp.einsum(
        "gqhd,gkhd->gqhk", queries, key_heads, preferred_element_type=jnp.float32
    )
    masked = jnp.where(visible, scores, -1e30)
    new_max = jnp.maximum(running_max, jnp.max(masked, axis=-1))
    exp_terms = jnp.where(visible, jnp.exp(masked - new_max[..., None]), 0.0)
    new_sum = jnp.sum(exp_terms, axis=-1)
    new_acc = jnp.einsum(
        "gqhk,gkhd->gqhd",
        exp_terms.astype(jnp.bfloat16),
        value_heads,
        preferred_element_type=jnp.float32,
    )
    attn_f = new_acc / new_sum[..., None]
    log_totals = new_max + jnp.log(new_sum)
    attn_heads = attn_f.astype(jnp.bfloat16).reshape(groups, seg_len, head_width)
    attention = lax.all_to_all(attn_heads, "head", split_axis=0, concat_axis=2, tiled=True)
    attn_rows = attention.reshape(row_count, model_width)
    residual = token_rows + jnp.dot(attn_rows, proj_out, preferred_element_type=jnp.float32)
    normed_two_f, norm_two_pull = jax.vjp(compress_norm, residual, norm_two)
    normed_two = normed_two_f.astype(jnp.bfloat16)
    hidden = jnp.dot(normed_two, proj_up, preferred_element_type=jnp.float32)
    activated_f, gelu_pull = jax.vjp(gelu_tanh, hidden)
    activated = activated_f.astype(jnp.bfloat16)
    mixed = (residual + jnp.dot(activated, proj_down, preferred_element_type=jnp.float32)).astype(
        jnp.bfloat16
    )
    cot_rows = cotangent_block.reshape(row_count, resid_width)
    grad_down = jnp.einsum("ra,rb->ab", activated, cot_rows, preferred_element_type=jnp.float32)
    d_activated = jnp.einsum("rb,ab->ra", cot_rows, proj_down, preferred_element_type=jnp.float32)
    (d_hidden,) = gelu_pull(d_activated)
    d_hidden = d_hidden.astype(jnp.bfloat16)
    grad_up = jnp.einsum("ra,rb->ab", normed_two, d_hidden, preferred_element_type=jnp.float32)
    d_normed_two = jnp.einsum("rb,ab->ra", d_hidden, proj_up, preferred_element_type=jnp.float32)
    d_resid_part, grad_gain_two = norm_two_pull(d_normed_two)
    d_residual = cot_rows.astype(jnp.float32) + d_resid_part
    d_sum = d_residual.astype(jnp.bfloat16)
    grad_out = jnp.einsum("ra,rb->ab", attn_rows, d_sum, preferred_element_type=jnp.float32)
    d_attention = jnp.einsum(
        "rb,ab->ra", d_sum, proj_out, preferred_element_type=jnp.float32
    ).astype(jnp.bfloat16)
    d_attention = d_attention.reshape(group_local, seg_len, model_width)
    d_heads_flat = lax.all_to_all(d_attention, "head", split_axis=2, concat_axis=0, tiled=True)
    d_heads = d_heads_flat.reshape(head_shape)
    delta_rows = jnp.sum(d_heads.astype(jnp.float32) * attn_f, axis=-1)
    lse_all, delta_all = (
        lax.all_gather(log_totals, "blk", axis=1, tiled=True),
        lax.all_gather(delta_rows, "blk", axis=1, tiled=True),
    )
    key_piece = lax.all_gather(keys_flat, "blk", axis=1, tiled=True)
    value_piece = lax.all_gather(values_flat, "blk", axis=1, tiled=True)
    seg_piece = lax.all_gather(seg_bf, "blk", axis=1, tiled=True)
    key_pos = jnp.arange(key_piece.shape[1], dtype=jnp.int32)[None, :]
    piece_rows = key_piece.shape[1]
    visible = visibility(query_pos, seg_here, key_pos, seg_piece.astype(jnp.int32))
    key_heads = key_piece.reshape(groups, piece_rows, heads_here, HEAD_DIM)
    value_heads = value_piece.reshape(groups, piece_rows, heads_here, HEAD_DIM)
    scores = score_scale * jnp.einsum(
        "gqhd,gkhd->gqhk", queries, key_heads, preferred_element_type=jnp.float32
    )
    masked = jnp.where(visible, scores, -1e30)
    soft_weights = jnp.where(visible, jnp.exp(masked - log_totals[..., None]), 0.0)
    d_soft = jnp.einsum("gqhd,gkhd->gqhk", d_heads, value_heads, preferred_element_type=jnp.float32)
    d_scores = (soft_weights * (d_soft - delta_rows[..., None])).astype(jnp.bfloat16)
    d_query = score_scale * jnp.einsum(
        "gqhk,gkhd->gqhd", d_scores, key_heads, preferred_element_type=jnp.float32
    )
    queries_flat = moved_qkv[:, :, 0]
    query_piece = lax.all_gather(queries_flat, "blk", axis=1, tiled=True)
    dout_piece = lax.all_gather(d_heads_flat, "blk", axis=1, tiled=True)
    seg_piece = lax.all_gather(seg_bf, "blk", axis=1, tiled=True)
    piece_rows = query_piece.shape[1]
    piece_pos = jnp.arange(piece_rows, dtype=jnp.int32)
    visible = visibility(piece_pos, seg_piece.astype(jnp.int32), query_pos[None, :], seg_here)
    query_heads = query_piece.reshape(groups, piece_rows, heads_here, HEAD_DIM)
    dout_heads = dout_piece.reshape(groups, piece_rows, heads_here, HEAD_DIM)
    scores = score_scale * jnp.einsum(
        "gqhd,gkhd->gqhk", query_heads, keys_local, preferred_element_type=jnp.float32
    )
    masked = jnp.where(visible, scores, -1e30)
    soft_weights = jnp.where(visible, jnp.exp(masked - lse_all[..., None]), 0.0)
    d_soft = jnp.einsum(
        "gqhd,gkhd->gqhk", dout_heads, values_local, preferred_element_type=jnp.float32
    )
    d_scores = (soft_weights * (d_soft - delta_all[..., None])).astype(jnp.bfloat16)
    new_value = jnp.einsum(
        "gqhk,gqhd->gkhd",
        soft_weights.astype(jnp.bfloat16),
        dout_heads,
        preferred_element_type=jnp.float32,
    )
    new_key = score_scale * jnp.einsum(
        "gqhk,gqhd->gkhd", d_scores, query_heads, preferred_element_type=jnp.float32
    )
    d_stacked = (
        jnp.stack([d_query, new_key, new_value], axis=2)
        .astype(jnp.bfloat16)
        .reshape(groups, seg_len, 3, head_width)
    )
    d_projected = lax.all_to_all(d_stacked, "head", split_axis=0, concat_axis=3, tiled=True)
    d_proj_rows = d_projected.reshape(row_count, 3 * model_width)
    grad_qkv = jnp.einsum("ra,rb->ab", normed_one, d_proj_rows, preferred_element_type=jnp.float32)
    d_normed_one = jnp.einsum(
        "rb,ab->ra", d_proj_rows, proj_qkv, preferred_element_type=jnp.float32
    )
    d_token_part, grad_gain_one = norm_one_pull(d_normed_one)
    grad_tokens = (d_residual + d_token_part).reshape(group_local, seg_len, resid_width)
    mixed = mixed.reshape(group_local, seg_len, resid_width)
    return (
        mixed,
        grad_tokens,
        (grad_qkv, grad_out, grad_up, grad_down, grad_gain_one, grad_gain_two),
    )


def on_device(tokens, segments, cotangent, w_qkv, w_out, w_up, w_down, gain_one, gain_two):
    micro_count = tokens.shape[0]
    seg_len = tokens.shape[2]
    query_pos = lax.axis_index("blk") * seg_len + jnp.arange(seg_len, dtype=jnp.int32)
    mixed_list = []
    token_grad_list = []
    grad_terms = []
    for batch_index in range(micro_count):
        weights_full = (
            lax.all_gather(w_qkv, ("head", "blk"), axis=0, tiled=True),
            lax.all_gather(w_out, ("head", "blk"), axis=0, tiled=True),
            lax.all_gather(w_up, ("head", "blk"), axis=0, tiled=True),
            lax.all_gather(w_down, ("head", "blk"), axis=0, tiled=True),
            lax.all_gather(gain_one, ("head", "blk"), axis=0, tiled=True),
            lax.all_gather(gain_two, ("head", "blk"), axis=0, tiled=True),
        )
        mixed, grad_tokens, gradients = micro_step(
            tokens[batch_index],
            segments[batch_index],
            cotangent[batch_index],
            weights_full,
            query_pos,
        )
        mixed_list.append(mixed)
        token_grad_list.append(grad_tokens)
        grad_terms.append(
            (
                lax.psum_scatter(gradients[0], ("head", "blk"), scatter_dimension=0, tiled=True),
                lax.psum_scatter(gradients[1], ("head", "blk"), scatter_dimension=0, tiled=True),
                lax.psum_scatter(gradients[2], ("head", "blk"), scatter_dimension=0, tiled=True),
                lax.psum_scatter(gradients[3], ("head", "blk"), scatter_dimension=0, tiled=True),
                lax.psum_scatter(gradients[4], ("head", "blk"), scatter_dimension=0, tiled=True),
                lax.psum_scatter(gradients[5], ("head", "blk"), scatter_dimension=0, tiled=True),
            )
        )
    summed = grad_terms[0]
    for later_terms in grad_terms[1:]:
        summed = tuple((first + second for first, second in zip(summed, later_terms)))
    mixed_all = jnp.stack(mixed_list, axis=0)
    token_grads = jnp.stack(token_grad_list, axis=0)
    return (
        mixed_all,
        token_grads,
        summed[0],
        summed[1],
        summed[2],
        summed[3],
        summed[4],
        summed[5],
    )


CORE, AXIS_X, AXIS_Z_NEAR, AXIS_Z_FAR, AXIS_Y = 1, 2, 4, 8, 16
DEVICES = 32
WIDTH = 768
HALF = 384
UNITS = 1536
ROWS = 256
POSITIONS = 1024
VMEM_BYTES = 60 * 1024 * 1024


def swap(array, bit, keep=lambda source: True):
    pairs = [(i, i ^ bit) for i in range(DEVICES) if keep(i)]
    return lax.ppermute(array, ("head", "blk"), pairs)


def upward(bit):
    return lambda source: source & bit == 0


def downward(bit):
    return lambda source: source & bit != 0


def dot(a, b):
    return lax.dot_general(a, b, (((1,), (0,)), ((), ())), preferred_element_type=jnp.float32)


def dot_nt(a, b):
    return lax.dot_general(a, b, (((1,), (1,)), ((), ())), preferred_element_type=jnp.float32)


def dot_tn(a, b):
    return lax.dot_general(a, b, (((0,), (0,)), ((), ())), preferred_element_type=jnp.float32)


def run_copies(copies):
    for copy in copies:
        copy.start()
    for copy in copies:
        copy.wait()


def lanes(rows):
    return lax.broadcasted_iota(jnp.int32, (rows, WIDTH), 1)


def norm_rows(values, lane):
    inner = jnp.where(lane < WIDTH - 1, values, 0.0)
    total = jnp.sum(inner, axis=-1, keepdims=True)
    full = jnp.where(lane == WIDTH - 1, -total, inner)
    factor = lax.rsqrt(jnp.mean(full * full, axis=-1, keepdims=True) + 1e-05)
    return full * factor, factor


def norm_rows_back(d_normed, normed, factor, lane):
    inner = jnp.mean(d_normed * normed, axis=-1, keepdims=True)
    d_full = factor * (d_normed - normed * inner)
    last = jnp.sum(jnp.where(lane == WIDTH - 1, d_full, 0.0), axis=-1, keepdims=True)
    return jnp.where(lane < WIDTH - 1, d_full - last, 0.0)


def piece_chip(which, pair, entry):
    z_bits = (entry & 3) << 1
    other = entry >> 2
    return z_bits | ((other | pair << 3) if which == 0 else (other << 3 | pair))


def gather_z(block):
    near = swap(block, AXIS_Z_NEAR)
    far = swap(block, AXIS_Z_FAR)
    end = swap(block, AXIS_Z_NEAR | AXIS_Z_FAR)
    return block, near, far, end


def gather_first(four, cut):
    four_a = jnp.stack([array[:, :cut] for array in four])
    four_b = jnp.stack([array[:, cut:] for array in four])
    return four_a, swap(four_a, AXIS_X), four_b, swap(four_b, AXIS_Y)


def gather_second(four_a, got_a, four_b, got_b):
    eight_a = jnp.concatenate([four_a, got_a], axis=0)
    eight_b = jnp.concatenate([four_b, got_b], axis=0)
    return eight_a, swap(eight_a, AXIS_Y), eight_b, swap(eight_b, AXIS_X)


def add(first, *others):
    total = first.astype(jnp.float32)
    for other in others:
        total = total + other.astype(jnp.float32)
    return total


def reduce_start(pieces):
    keep_a, send_a, keep_b, send_b = pieces
    return keep_a, swap(send_a, AXIS_Y), keep_b, swap(send_b, AXIS_X)


def reduce_middle(keep_a, got_a, keep_b, got_b):
    send_a = add(keep_a[4:], got_a[4:]).astype(jnp.bfloat16)
    send_b = add(keep_b[4:], got_b[4:]).astype(jnp.bfloat16)
    left_a = (keep_a[:4], got_a[:4], swap(send_a, AXIS_X))
    left_b = (keep_b[:4], got_b[:4], swap(send_b, AXIS_Y))
    return left_a, left_b


def along_z(four):
    near = swap(four[1], AXIS_Z_NEAR)
    far = swap(four[2], AXIS_Z_FAR)
    end = swap(four[3], AXIS_Z_NEAR | AXIS_Z_FAR)
    return near, far, end


def reduce_z(left_a, left_b):
    four = jnp.concatenate([add(*left_a), add(*left_b)], axis=-1).astype(jnp.bfloat16)
    return (four[0], *along_z(four))


def fence(*arrays):
    return lax.optimization_barrier(arrays)


def piece_copies(pieces, targets, chip, rows, sem, base, outward=False):
    copies = []
    for which in range(2):
        for pair in range(2):
            source = pieces[which * 2 + pair]
            for entry in range(8):
                block = chip ^ piece_chip(which, pair, entry)
                at = pl.multiple_of(block * rows, 16)
                here = targets[which].at[pl.ds(at, rows), :]
                there = source.at[entry]
                ends = (here, there) if outward else (there, here)
                copies.append(pltpu.make_async_copy(*ends, sem.at[base + len(copies)]))
    return copies


def row_pieces(array, whole, place, core, core_bit, sem, base, outward=False):
    copies = []
    for entry in range(8):
        rel = (entry & 3) << 1 | entry >> 2
        block = (place ^ rel) * 2 + (core ^ core_bit)
        at = pl.multiple_of(block * 64, 64)
        here = whole.at[:, pl.ds(at, 64), :]
        there = array.at[entry]
        ends = (here, there) if outward else (there, here)
        copies.append(pltpu.make_async_copy(*ends, sem.at[base + len(copies)]))
    return copies


def forward_kernel(
    ids, tok_mine, tok_other, w0, w1, w2, w3,
    attn_out, query_out, kv_out, normed_out, soft_out, wqkv_out, wout_out, own_out, gains_out,
    tok, bias, sem,
):
    chip, core = ids[0], ids[1]
    place = lax.rem(chip, 8)
    copies = piece_copies((w0, w1, w2, w3), (wqkv_out, wout_out), chip, 48, sem, 0)
    copies += row_pieces(tok_mine, tok, place, core, 0, sem, 32)
    copies += row_pieces(tok_other, tok, place, core, 1, sem, 40)
    run_copies(copies)
    picks = lax.broadcasted_iota(jnp.int32, (8, 128), 0) == lax.broadcasted_iota(
        jnp.int32, (8, 128), 1
    )
    gains_out[...] = dot_nt(picks.astype(jnp.bfloat16), wqkv_out[:, 3 * HALF :])
    gain = gains_out[0:1, :]
    lane = lanes(ROWS)
    for micro in range(2):

        def norm_chunk(index, carry, micro=micro):
            at = pl.multiple_of(index * ROWS, ROWS)
            values = tok[micro, pl.ds(at, ROWS), :].astype(jnp.float32)
            normed = (norm_rows(values, lane)[0] * gain).astype(jnp.bfloat16)
            normed_out[micro, pl.ds(at, ROWS), :] = normed
            kv_out[micro, pl.ds(at, ROWS), :] = dot(normed, wqkv_out[:, HALF : 3 * HALF]).astype(
                jnp.bfloat16
            )
            return carry

        lax.fori_loop(0, POSITIONS // ROWS, norm_chunk, 0)
    first_row = pl.multiple_of(place * 128, 128)
    hot = (lax.broadcasted_iota(jnp.int32, (8, WIDTH), 1) == WIDTH - 1).astype(jnp.bfloat16)
    small = lax.broadcasted_iota(jnp.int32, (128, 128), 1) < HEAD_DIM
    for micro in range(2):
        own = tok[micro, pl.ds(first_row, 128), :]
        own_out[micro * 128 : micro * 128 + 128, :] = own
        query = dot(normed_out[micro, pl.ds(first_row, 128), :], wqkv_out[:, :HALF])
        query = query.astype(jnp.bfloat16) * jnp.bfloat16(0.125)
        query_out[micro * 128 : micro * 128 + 128, :] = query
        key_seg = dot_nt(hot, tok[micro])[0:1, :]
        query_seg = own[:, WIDTH - 1 :].astype(jnp.float32)
        key_pos = lax.broadcasted_iota(jnp.int32, (128, POSITIONS), 1)
        query_pos = first_row + lax.broadcasted_iota(jnp.int32, (128, POSITIONS), 0)
        seen = (key_pos <= query_pos) & ((key_seg == 0.0) | (key_seg == query_seg))
        bias[...] = jnp.where(seen, 0.0, -1e30)
        for pair in range(3):
            cols = slice(pair * 128, pair * 128 + 128)
            both = query_out[micro * 128 : micro * 128 + 128, cols]
            zero = jnp.zeros_like(both)
            stacked = jnp.concatenate(
                [jnp.where(small, both, zero), jnp.where(small, zero, both)], axis=0
            )
            scores = dot_nt(stacked, kv_out[micro, :, cols])
            scores = scores + jnp.concatenate([bias[...], bias[...]], axis=0)
            top = jnp.max(scores, axis=-1, keepdims=True)
            terms = jnp.exp(scores - top)
            total = jnp.sum(terms, axis=-1, keepdims=True)
            soft = (terms * (1.0 / total)).astype(jnp.bfloat16)
            soft_out[micro * 3 + pair] = soft
            value = kv_out[micro, :, HALF + pair * 128 : HALF + pair * 128 + 128]
            mixed = dot(soft, value)
            attn_out[micro * 128 : micro * 128 + 128, cols] = jnp.where(
                small, mixed[:128], mixed[128:]
            ).astype(jnp.bfloat16)


def feed_half(normed, cot, up, down, g_up, g_down, sum_mix, sum_norm):
    slope = math.sqrt(2.0 / math.pi)
    for part in range(2):
        units = slice(part * HALF, part * HALF + HALF)
        hidden = dot(normed, up[:, units])
        square = hidden * hidden
        wave = jnp.tanh(slope * hidden * (1.0 + 0.044715 * square))
        active = (0.5 * hidden * (1.0 + wave)).astype(jnp.bfloat16)
        grow = 0.5 * (1.0 + wave) + 0.5 * hidden * (1.0 - wave * wave) * slope * (
            1.0 + 3.0 * 0.044715 * square
        )
        d_hidden = (dot_nt(cot, down[units, :]) * grow).astype(jnp.bfloat16)
        sum_mix[...] += dot(active, down[units, :])
        sum_norm[...] += dot_nt(d_hidden, up[:, units])
        g_up[:, units] = dot_tn(normed, d_hidden).astype(jnp.bfloat16)
        g_down[units, :] = dot_tn(active, cot).astype(jnp.bfloat16)


def feed_first_kernel(
    ids, gains, attn_mine, attn_other, own, wout_mine, wout_other, cot_mine, cot_other,
    w0, w1, w2, w3,
    attn_out, cot_out, res_out, normed_out, sum_mix, sum_norm, g0, g1, g2, g3,
    up, down, g_up, g_down, sem,
):
    chip, core = ids[0], ids[1]
    load = piece_copies((w0, w1, w2, w3), (up, down), chip, 48, sem, 0)
    for copy in load:
        copy.start()
    mine_at = pl.multiple_of(core * HALF, 128)
    other_at = pl.multiple_of((1 - core) * HALF, 128)
    attn_out[:, pl.ds(mine_at, HALF)] = attn_mine[...]
    attn_out[:, pl.ds(other_at, HALF)] = attn_other[...]
    for micro in range(2):
        for side, source in ((core, cot_mine), (1 - core, cot_other)):
            at = pl.multiple_of(micro * 128 + side * 64, 64)
            cot_out[pl.ds(at, 64), :] = source[micro]
    lane = lanes(ROWS)
    attn = attn_out[...]
    res_out[:, pl.ds(mine_at, HALF)] = dot(attn, wout_mine[...])
    res_out[:, pl.ds(other_at, HALF)] = dot(attn, wout_other[...])
    own_values = jnp.where(lane < WIDTH - 1, own[...].astype(jnp.float32), 0.0)
    residual = res_out[...] + own_values
    res_out[...] = residual
    normed = (norm_rows(residual, lane)[0] * gains[1:2, :]).astype(jnp.bfloat16)
    normed_out[...] = normed
    sum_mix[...] = jnp.zeros_like(sum_mix)
    sum_norm[...] = jnp.zeros_like(sum_norm)
    for copy in load:
        copy.wait()
    feed_half(normed, cot_out[...], up, down, g_up, g_down, sum_mix, sum_norm)
    run_copies(piece_copies((g0, g1, g2, g3), (g_up, g_down), chip, 48, sem, 0, True))


def feed_second_kernel(
    ids, normed, cot, mix_in, norm_in, w0, w1, w2, w3,
    part_out, g0, g1, g2, g3,
    up, down, g_up, g_down, sum_mix, sum_norm, sem,
):
    chip = ids[0]
    load = piece_copies((w0, w1, w2, w3), (up, down), chip, 48, sem, 0)
    for copy in load:
        copy.start()
    sum_mix[...] = mix_in[...]
    sum_norm[...] = norm_in[...]
    for copy in load:
        copy.wait()
    feed_half(normed[...], cot[...], up, down, g_up, g_down, sum_mix, sum_norm)
    store = piece_copies((g0, g1, g2, g3), (g_up, g_down), chip, 48, sem, 0, True)
    for copy in store:
        copy.start()
    part_out[:ROWS, :] = sum_mix[...].astype(jnp.bfloat16)
    part_out[ROWS:, :] = sum_norm[...].astype(jnp.bfloat16)
    for copy in store:
        copy.wait()


def backward_kernel(
    ids, gains, residual, part_mine, part_other, cot, wout_mine, wout_other, wqkv,
    query, kv, soft,
    mixed_out, dres_out, keep_rows, send_rows, d_kv, d_query, d_sum_half,
    d_attn, d_rows, d_sum_ref, hold, sem,
):
    chip, core = ids[0], ids[1]
    place = lax.rem(chip, 8)
    first_row = pl.multiple_of(place * 128, 128)
    mine_at = pl.multiple_of(core * HALF, 128)
    other_at = pl.multiple_of((1 - core) * HALF, 128)
    lane = lanes(ROWS)
    res = residual[...]
    mixed = add(res, part_mine[:ROWS, :], part_other[:ROWS, :])
    hold[...] = mixed
    for micro in range(2):
        at = pl.multiple_of(micro * 128 + core * 64, 64)
        mixed_out[micro] = hold[pl.ds(at, 64), : WIDTH - 1].astype(jnp.bfloat16)
    d_normed = add(part_mine[ROWS:, :], part_other[ROWS:, :]) * gains[1:2, :]
    normed_two, factor = norm_rows(res, lane)
    d_res = cot[...].astype(jnp.float32) + norm_rows_back(d_normed, normed_two, factor, lane)
    hold[...] = d_res
    for micro in range(2):
        at = pl.multiple_of(micro * 128 + core * 64, 64)
        dres_out[micro] = hold[pl.ds(at, 64), :]
    d_sum_ref[...] = d_res.astype(jnp.bfloat16)
    d_mine = d_sum_ref[:, pl.ds(mine_at, HALF)]
    d_other = d_sum_ref[:, pl.ds(other_at, HALF)]
    d_sum_half[...] = d_mine
    d_heads = dot_nt(d_mine, wout_mine[pl.ds(mine_at, HALF), :]) + dot_nt(
        d_other, wout_other[pl.ds(mine_at, HALF), :]
    )
    d_attn[...] = d_heads.astype(jnp.bfloat16)
    small = lax.broadcasted_iota(jnp.int32, (128, 128), 1) < HEAD_DIM
    for micro in range(2):
        here = slice(micro * 128, micro * 128 + 128)
        for pair in range(3):
            cols = slice(pair * 128, pair * 128 + 128)
            value_cols = slice(HALF + pair * 128, HALF + pair * 128 + 128)

            def stack(both):
                zero = jnp.zeros_like(both)
                return jnp.concatenate(
                    [jnp.where(small, both, zero), jnp.where(small, zero, both)], axis=0
                )

            d_out = stack(d_attn[here, cols])
            q_both = stack(query[here, cols])
            weights = soft[micro * 3 + pair]
            d_soft = dot_nt(d_out, kv[micro, :, value_cols])
            weights_f = weights.astype(jnp.float32)
            delta = jnp.sum(weights_f * d_soft, axis=-1, keepdims=True)
            d_scores = (weights_f * (d_soft - delta)).astype(jnp.bfloat16)
            d_q = dot(d_scores, kv[micro, :, cols]) * 0.125
            d_query[here, cols] = jnp.where(small, d_q[:128], d_q[128:]).astype(jnp.bfloat16)
            d_kv[micro, :, cols] = dot_tn(d_scores, q_both).astype(jnp.bfloat16)
            d_kv[micro, :, value_cols] = dot_tn(weights, d_out).astype(jnp.bfloat16)

        def row_chunk(index, carry, micro=micro):
            at = pl.multiple_of(index * ROWS, ROWS)
            rows = dot_nt(d_kv[micro, pl.ds(at, ROWS), :], wqkv[:, HALF : 3 * HALF])
            d_rows[micro, pl.ds(at, ROWS), :] = rows.astype(jnp.bfloat16)
            return carry

        lax.fori_loop(0, POSITIONS // ROWS, row_chunk, 0)
        own = d_rows[micro, pl.ds(first_row, 128), :].astype(jnp.float32)
        own = own + dot_nt(d_query[here, :], wqkv[:, :HALF])
        d_rows[micro, pl.ds(first_row, 128), :] = own.astype(jnp.bfloat16)
    store = row_pieces(keep_rows, d_rows, place, core, 0, sem, 0, True)
    store += row_pieces(send_rows, d_rows, place, core, 1, sem, 8, True)
    run_copies(store)


def gradient_kernel(
    ids, attn, d_sum_half, d_query, d_kv, normed_all, g0, g1, g2, g3, g_a, g_b, sem
):
    chip = ids[0]
    first_row = pl.multiple_of(lax.rem(chip, 8) * 128, 128)
    own_0 = normed_all[0, pl.ds(first_row, 128), :]
    own_1 = normed_all[1, pl.ds(first_row, 128), :]
    g_b[...] = dot_tn(attn[...], d_sum_half[...]).astype(jnp.bfloat16)
    g_a[:, :HALF] = (dot_tn(own_0, d_query[:128, :]) + dot_tn(own_1, d_query[128:, :])).astype(
        jnp.bfloat16
    )
    g_a[:, HALF:] = (dot_tn(normed_all[0], d_kv[0]) + dot_tn(normed_all[1], d_kv[1])).astype(
        jnp.bfloat16
    )
    run_copies(piece_copies((g0, g1, g2, g3), (g_a, g_b), chip, 48, sem, 0, True))


def tail_kernel(gains, tokens, d_0, d_1, d_2, d_3, d_residual, grad_out):
    lane = lanes(128)
    rows = (128, WIDTH)
    values = tokens[...].reshape(rows).astype(jnp.float32)
    normed, factor = norm_rows(values, lane)
    d_normed = add(d_0[...], d_1[...], d_2[...], d_3[...]).reshape(rows) * gains[0:1, :]
    out = d_residual[...].reshape(rows) + norm_rows_back(d_normed, normed, factor, lane)
    grad_out[...] = out[:, : WIDTH - 1].reshape(2, 64, WIDTH - 1)


ANY = pl.BlockSpec(memory_space=pl.ANY)
VMEM = pl.BlockSpec(memory_space=pltpu.VMEM)
SMEM = pl.BlockSpec(memory_space=pltpu.SMEM)


def shaped(shape, dtype=jnp.bfloat16):
    return jax.ShapeDtypeStruct(shape, dtype)


def call(kernel, ins, outs, scratch, name):
    return pl.pallas_call(
        kernel,
        in_specs=[spec for spec in ins],
        out_specs=[spec for spec, _ in outs],
        out_shape=[shape for _, shape in outs],
        scratch_shapes=scratch,
        name=name,
        cost_estimate=pl.CostEstimate(flops=0, transcendentals=0, bytes_accessed=0),
        compiler_params=pltpu.CompilerParams(vmem_limit_bytes=VMEM_BYTES),
    )


def pick(core, zero, one):
    return jnp.where(core == 0, zero, one)


def chip_block(core, for_zero, for_one):
    mine = pick(core, for_zero, for_one)
    other = swap(pick(core, for_one, for_zero), CORE)
    return jnp.concatenate([pick(core, mine, other), pick(core, other, mine)], axis=0)


def core_rows(core, block):
    rows = block.shape[0] // 2
    mine = pick(core, block[:rows], block[rows:])
    other = swap(pick(core, block[rows:], block[:rows]), CORE)
    return pick(core, mine, other), pick(core, other, mine)


def split_units(w_up, blocks):
    rows = w_up.shape[0]
    parts = w_up.reshape(rows, blocks, 2, 2, -1)
    return [parts[:, :, k].swapaxes(1, 2).reshape(rows, -1) for k in range(2)]


def join_units(first, second, blocks):
    rows = first.shape[0]
    parts = [half.reshape(rows, 2, blocks, -1).swapaxes(1, 2) for half in (first, second)]
    return jnp.stack(parts, axis=2).reshape(rows, -1)


def on_chip_pair(tokens, segments, cotangent, w_qkv, w_out, w_up, w_down, gain_one, gain_two):
    bf, f32 = jnp.bfloat16, jnp.float32
    device = lax.axis_index("head") * 16 + lax.axis_index("blk")
    core = device % 2
    ids = jnp.stack([device // 2, core]).astype(jnp.int32)
    own = jnp.concatenate([tokens[:, 0], segments[:, 0, :, None].astype(bf)], axis=-1)
    cot = jnp.pad(cotangent[:, 0], ((0, 0), (0, 0), (0, 1)))
    four = jnp.stack(
        [
            own,
            swap(own, AXIS_Z_NEAR, upward(AXIS_Z_NEAR)),
            swap(own, AXIS_Z_FAR, upward(AXIS_Z_FAR)),
            swap(own, AXIS_Z_NEAR | AXIS_Z_FAR, upward(AXIS_Z_FAR)),
        ]
    )
    eight = jnp.concatenate([four, swap(four, AXIS_X)], axis=0)
    eight_other = swap(eight, CORE)
    gain_cols = jnp.pad(jnp.stack([gain_one, gain_two], axis=-1), ((0, 0), (0, 126)))
    out_wide = jnp.pad(w_out, ((0, 0), (0, 1)))
    down_wide = jnp.pad(w_down, ((0, 0), (0, 1)))
    qkv_parts = w_qkv.reshape(-1, 3, 2, HALF)
    attn_halves = [
        jnp.concatenate(
            [qkv_parts[:, 0, k], qkv_parts[:, 1, k], qkv_parts[:, 2, k], gain_cols]
            + [out_wide[:, k * HALF : k * HALF + HALF]],
            axis=-1,
        )
        for k in range(2)
    ]
    wide = 3 * HALF + 128
    attn_four = gather_z(chip_block(core, *attn_halves))
    attn_first = gather_first(attn_four, wide)
    up_block = chip_block(core, *split_units(w_up, 16))
    feed_blocks = [
        jnp.concatenate(
            [up_block[:, half * WIDTH :][:, :WIDTH], down_wide[half * 48 : half * 48 + 48]], axis=-1
        )
        for half in range(2)
    ]
    four_0 = gather_z(fence(feed_blocks[0], *attn_four[1:])[0])
    four_1 = gather_z(fence(feed_blocks[1], *four_0[1:])[0])
    attn_pieces = gather_second(*attn_first)
    first_0 = gather_first(fence(*four_0, *attn_first)[:4], WIDTH)
    first_1 = gather_first(fence(*four_1, *first_0)[:4], WIDTH)
    pieces_0 = gather_second(*fence(*first_0, *attn_pieces)[:4])
    cot_other = swap(cot, CORE)
    attn, query, kv, normed_all, soft, wqkv, wout, own_rows, gains = call(
        forward_kernel,
        [SMEM] + [ANY] * 6,
        [
            (VMEM, shaped((ROWS, HALF))),
            (VMEM, shaped((ROWS, HALF))),
            (VMEM, shaped((2, POSITIONS, WIDTH))),
            (VMEM, shaped((2, POSITIONS, WIDTH))),
            (VMEM, shaped((6, ROWS, POSITIONS))),
            (VMEM, shaped((WIDTH, wide))),
            (VMEM, shaped((WIDTH, HALF))),
            (VMEM, shaped((ROWS, WIDTH))),
            (VMEM, shaped((8, WIDTH), f32)),
        ],
        [
            pltpu.VMEM((2, POSITIONS, WIDTH), bf),
            pltpu.VMEM((128, POSITIONS), f32),
            pltpu.SemaphoreType.DMA((48,)),
        ],
        "attention_forward",
    )(ids, eight, eight_other, *attn_pieces)
    attn_other = swap(attn, CORE)
    wout_other = swap(wout, CORE)
    pieces_1 = gather_second(*fence(*first_1, *pieces_0, attn)[:4])
    weight_scratch = [pltpu.VMEM((WIDTH, WIDTH), bf)] * 4
    sums_scratch = [pltpu.VMEM((ROWS, WIDTH), f32)] * 2
    piece_shapes = [(ANY, shaped((8, 48, WIDTH)))] * 4
    outs = call(
        feed_first_kernel,
        [SMEM] + [VMEM] * 8 + [ANY] * 4,
        [
            (VMEM, shaped((ROWS, WIDTH))),
            (VMEM, shaped((ROWS, WIDTH))),
            (VMEM, shaped((ROWS, WIDTH), f32)),
            (VMEM, shaped((ROWS, WIDTH))),
            (VMEM, shaped((ROWS, WIDTH), f32)),
            (VMEM, shaped((ROWS, WIDTH), f32)),
        ]
        + piece_shapes,
        weight_scratch + [pltpu.SemaphoreType.DMA((32,))],
        "feed_forward_and_back_first",
    )(
        ids, gains, attn, attn_other, own_rows, wout, wout_other, cot, cot_other, *pieces_0
    )
    attn_all, cot_all, residual, normed_two, sum_mix, sum_norm = outs[:6]
    feed_0 = reduce_start(outs[6:])
    part, *grads_1 = call(
        feed_second_kernel,
        [SMEM] + [VMEM] * 4 + [ANY] * 4,
        [(VMEM, shaped((2 * ROWS, WIDTH)))] + piece_shapes,
        weight_scratch + sums_scratch + [pltpu.SemaphoreType.DMA((32,))],
        "feed_forward_and_back_second",
    )(ids, normed_two, cot_all, sum_mix, sum_norm, *pieces_1)
    feed_0, part, grads_1 = fence(feed_0, part, grads_1)
    part_other = swap(part, CORE)
    feed_0 = reduce_middle(*feed_0)
    feed_1 = reduce_start(grads_1)
    outs = call(
        backward_kernel,
        [SMEM] + [VMEM] * 11,
        [
            (VMEM, shaped((2, 64, WIDTH - 1))),
            (VMEM, shaped((2, 64, WIDTH), f32)),
            (ANY, shaped((8, 2, 64, WIDTH))),
            (ANY, shaped((8, 2, 64, WIDTH))),
            (VMEM, shaped((2, POSITIONS, WIDTH))),
            (VMEM, shaped((ROWS, HALF))),
            (VMEM, shaped((ROWS, HALF))),
        ],
        [
            pltpu.VMEM((ROWS, HALF), bf),
            pltpu.VMEM((2, POSITIONS, WIDTH), bf),
            pltpu.VMEM((ROWS, WIDTH), bf),
            pltpu.VMEM((ROWS, WIDTH), f32),
            pltpu.SemaphoreType.DMA((16,)),
        ],
        "attention_backward",
    )(
        ids, gains, residual, part, part_other, cot_all, wout, wout_other, wqkv,
        query, kv, soft,
    )
    mixed, d_residual, *outs = outs
    outs, feed_0, feed_1 = fence(outs, feed_0, feed_1)
    keep_rows, send_rows, d_kv, d_query, d_sum_half = outs
    feed_0 = reduce_z(*feed_0)
    feed_1 = reduce_middle(*feed_1)
    got_rows = swap(send_rows, CORE)
    grad_attn_pieces = call(
        gradient_kernel,
        [SMEM] + [VMEM] * 5,
        [(ANY, shaped((8, 48, 3 * HALF)))] * 2 + [(ANY, shaped((8, 48, HALF)))] * 2,
        [
            pltpu.VMEM((WIDTH, 3 * HALF), bf),
            pltpu.VMEM((WIDTH, HALF), bf),
            pltpu.SemaphoreType.DMA((32,)),
        ],
        "attention_weight_gradients",
    )(ids, attn_all, d_sum_half, d_query, d_kv, normed_all)
    keep_rows, got_rows, grad_attn_pieces, feed_0, feed_1 = fence(
        keep_rows, got_rows, grad_attn_pieces, feed_0, feed_1
    )
    crossed = swap(add(keep_rows[4:], got_rows[4:]).astype(bf), AXIS_X)
    attn_first = reduce_start(grad_attn_pieces)
    feed_1 = reduce_z(*feed_1)
    feed_1, crossed, attn_first = fence(feed_1, crossed, attn_first)
    rows_4 = add(keep_rows[:4], got_rows[:4], crossed).astype(bf)
    to_near = swap(rows_4[1], AXIS_Z_NEAR, downward(AXIS_Z_NEAR))
    to_far = swap(rows_4[2], AXIS_Z_FAR, downward(AXIS_Z_FAR))
    to_end = swap(rows_4[3], AXIS_Z_NEAR | AXIS_Z_FAR, downward(AXIS_Z_FAR))
    attn_last = reduce_z(*reduce_middle(*attn_first))
    sum_0, sum_1, attn_sum = add(*feed_0), add(*feed_1), add(*attn_last)
    (grad_tokens,) = call(
        tail_kernel,
        [VMEM] * 7,
        [(VMEM, shaped((2, 64, WIDTH - 1), f32))],
        [],
        "token_gradient",
    )(gains, own, rows_4[0], to_near, to_far, to_end, d_residual)
    attn_0, attn_1 = core_rows(core, attn_sum)
    up_sum = jnp.concatenate([sum_0[:, :WIDTH], sum_1[:, :WIDTH]], axis=-1)
    up_0, up_1 = core_rows(core, up_sum)
    grad_qkv = jnp.concatenate(
        [half[:, k * HALF : k * HALF + HALF] for k in range(3) for half in (attn_0, attn_1)],
        axis=-1,
    )
    grad_out = jnp.concatenate([attn_0[:, 3 * HALF :], attn_1[:, 3 * HALF : 4 * HALF - 1]], axis=-1)
    grad_up = join_units(up_0, up_1, 16)
    grad_down = jnp.concatenate([sum_0[:, WIDTH:], sum_1[:, WIDTH:]], axis=0)
    grad_gain_one = jnp.sum(grad_qkv * w_qkv.astype(f32), axis=-1) / gain_one.astype(f32)
    grad_gain_two = jnp.sum(grad_up * w_up.astype(f32), axis=-1) / gain_two.astype(f32)
    return (
        mixed[:, None],
        grad_tokens[:, None],
        grad_qkv,
        grad_out,
        grad_up,
        grad_down[:, : WIDTH - 1],
        grad_gain_one,
        grad_gain_two,
    )


def solution(mesh):
    small_slice = (mesh.shape["head"], mesh.shape["blk"]) == (2, 16)
    placed = (
        P(None, "head", "blk", None),
        P(None, "head", "blk"),
        P(None, "head", "blk", None),
        P(("head", "blk"), None),
        P(("head", "blk"), None),
        P(("head", "blk"), None),
        P(("head", "blk"), None),
        P(("head", "blk")),
        P(("head", "blk")),
    )
    return jax.shard_map(
        on_chip_pair if small_slice else on_device,
        mesh=mesh,
        in_specs=placed,
        out_specs=(
            P(None, "head", "blk", None),
            P(None, "head", "blk", None),
            P(("head", "blk"), None),
            P(("head", "blk"), None),
            P(("head", "blk"), None),
            P(("head", "blk"), None),
            P(("head", "blk")),
            P(("head", "blk")),
        ),
        check_vma=False,
    )
```

```python
import math

import jax
import jax.numpy as jnp
from jax import lax
from jax.experimental import pallas as pl
from jax.experimental.pallas import tpu as pltpu
from jax.sharding import PartitionSpec as P

HEAD_DIM = 64


def compress_norm(values, gain):
    total_sum = jnp.sum(values, axis=-1, keepdims=True)
    full_vec = jnp.concatenate([values, -total_sum], axis=-1)
    factor = lax.rsqrt(jnp.mean(full_vec * full_vec, axis=-1, keepdims=True) + 1e-05)
    return full_vec * factor * gain


def gelu_tanh(values):
    return jax.nn.gelu(values, approximate=True)


def visibility(query_pos, query_seg, key_pos, key_seg):
    causal = key_pos[:, None, :] <= query_pos[None, :, None]
    shared = (key_seg[:, None, :] == 0) | (key_seg[:, None, :] == query_seg[:, :, None])
    return (causal & shared)[:, :, None, :]


def micro_step(token_block, segment_block, cotangent_block, weights_full, query_pos):
    proj_qkv, proj_out, proj_up, proj_down, norm_one, norm_two = weights_full
    norm_one = norm_one.astype(jnp.float32)
    norm_two = norm_two.astype(jnp.float32)
    group_local, seg_len, resid_width = token_block.shape
    model_width = proj_qkv.shape[0]
    row_count = group_local * seg_len
    score_scale = 1.0 / math.sqrt(HEAD_DIM)
    token_rows = token_block.astype(jnp.float32).reshape(row_count, resid_width)
    normed_f, norm_one_pull = jax.vjp(compress_norm, token_rows, norm_one)
    normed_one = normed_f.astype(jnp.bfloat16)
    projected = jnp.dot(normed_one, proj_qkv, preferred_element_type=jnp.float32).astype(
        jnp.bfloat16
    )
    projected = projected.reshape(group_local, seg_len, 3, model_width)
    head_groups = lax.axis_size("head")
    seg_wide = jnp.broadcast_to(
        segment_block.astype(jnp.bfloat16)[:, :, None, None], (group_local, seg_len, 1, head_groups)
    )
    moved_qkv, moved_seg = (
        lax.all_to_all(projected, "head", split_axis=3, concat_axis=0, tiled=True),
        lax.all_to_all(seg_wide, "head", split_axis=3, concat_axis=0, tiled=True),
    )
    groups = moved_qkv.shape[0]
    head_width = moved_qkv.shape[3]
    heads_here = head_width // HEAD_DIM
    head_shape = (groups, seg_len, heads_here, HEAD_DIM)
    queries = moved_qkv[:, :, 0].reshape(head_shape)
    keys_flat = moved_qkv[:, :, 1]
    values_flat = moved_qkv[:, :, 2]
    keys_local = keys_flat.reshape(head_shape)
    values_local = values_flat.reshape(head_shape)
    seg_bf = moved_seg[:, :, 0, 0]
    seg_here = seg_bf.astype(jnp.int32)
    key_piece = lax.all_gather(keys_flat, "blk", axis=1, tiled=True)
    value_piece = lax.all_gather(values_flat, "blk", axis=1, tiled=True)
    seg_piece = lax.all_gather(seg_bf, "blk", axis=1, tiled=True)
    key_pos = jnp.arange(key_piece.shape[1], dtype=jnp.int32)[None, :]
    running_max = jnp.full((groups, seg_len, heads_here), -1e30, jnp.float32)
    piece_rows = key_piece.shape[1]
    visible = visibility(query_pos, seg_here, key_pos, seg_piece.astype(jnp.int32))
    key_heads = key_piece.reshape(groups, piece_rows, heads_here, HEAD_DIM)
    value_heads = value_piece.reshape(groups, piece_rows, heads_here, HEAD_DIM)
    scores = score_scale * jnp.einsum(
        "gqhd,gkhd->gqhk", queries, key_heads, preferred_element_type=jnp.float32
    )
    masked = jnp.where(visible, scores, -1e30)
    new_max = jnp.maximum(running_max, jnp.max(masked, axis=-1))
    exp_terms = jnp.where(visible, jnp.exp(masked - new_max[..., None]), 0.0)
    new_sum = jnp.sum(exp_terms, axis=-1)
    new_acc = jnp.einsum(
        "gqhk,gkhd->gqhd",
        exp_terms.astype(jnp.bfloat16),
        value_heads,
        preferred_element_type=jnp.float32,
    )
    attn_f = new_acc / new_sum[..., None]
    log_totals = new_max + jnp.log(new_sum)
    attn_heads = attn_f.astype(jnp.bfloat16).reshape(groups, seg_len, head_width)
    attention = lax.all_to_all(attn_heads, "head", split_axis=0, concat_axis=2, tiled=True)
    attn_rows = attention.reshape(row_count, model_width)
    residual = token_rows + jnp.dot(attn_rows, proj_out, preferred_element_type=jnp.float32)
    normed_two_f, norm_two_pull = jax.vjp(compress_norm, residual, norm_two)
    normed_two = normed_two_f.astype(jnp.bfloat16)
    hidden = jnp.dot(normed_two, proj_up, preferred_element_type=jnp.float32)
    activated_f, gelu_pull = jax.vjp(gelu_tanh, hidden)
    activated = activated_f.astype(jnp.bfloat16)
    mixed = (residual + jnp.dot(activated, proj_down, preferred_element_type=jnp.float32)).astype(
        jnp.bfloat16
    )
    cot_rows = cotangent_block.reshape(row_count, resid_width)
    grad_down = jnp.einsum("ra,rb->ab", activated, cot_rows, preferred_element_type=jnp.float32)
    d_activated = jnp.einsum("rb,ab->ra", cot_rows, proj_down, preferred_element_type=jnp.float32)
    (d_hidden,) = gelu_pull(d_activated)
    d_hidden = d_hidden.astype(jnp.bfloat16)
    grad_up = jnp.einsum("ra,rb->ab", normed_two, d_hidden, preferred_element_type=jnp.float32)
    d_normed_two = jnp.einsum("rb,ab->ra", d_hidden, proj_up, preferred_element_type=jnp.float32)
    d_resid_part, grad_gain_two = norm_two_pull(d_normed_two)
    d_residual = cot_rows.astype(jnp.float32) + d_resid_part
    d_sum = d_residual.astype(jnp.bfloat16)
    grad_out = jnp.einsum("ra,rb->ab", attn_rows, d_sum, preferred_element_type=jnp.float32)
    d_attention = jnp.einsum(
        "rb,ab->ra", d_sum, proj_out, preferred_element_type=jnp.float32
    ).astype(jnp.bfloat16)
    d_attention = d_attention.reshape(group_local, seg_len, model_width)
    d_heads_flat = lax.all_to_all(d_attention, "head", split_axis=2, concat_axis=0, tiled=True)
    d_heads = d_heads_flat.reshape(head_shape)
    delta_rows = jnp.sum(d_heads.astype(jnp.float32) * attn_f, axis=-1)
    lse_all, delta_all = (
        lax.all_gather(log_totals, "blk", axis=1, tiled=True),
        lax.all_gather(delta_rows, "blk", axis=1, tiled=True),
    )
    key_piece = lax.all_gather(keys_flat, "blk", axis=1, tiled=True)
    value_piece = lax.all_gather(values_flat, "blk", axis=1, tiled=True)
    seg_piece = lax.all_gather(seg_bf, "blk", axis=1, tiled=True)
    key_pos = jnp.arange(key_piece.shape[1], dtype=jnp.int32)[None, :]
    piece_rows = key_piece.shape[1]
    visible = visibility(query_pos, seg_here, key_pos, seg_piece.astype(jnp.int32))
    key_heads = key_piece.reshape(groups, piece_rows, heads_here, HEAD_DIM)
    value_heads = value_piece.reshape(groups, piece_rows, heads_here, HEAD_DIM)
    scores = score_scale * jnp.einsum(
        "gqhd,gkhd->gqhk", queries, key_heads, preferred_element_type=jnp.float32
    )
    masked = jnp.where(visible, scores, -1e30)
    soft_weights = jnp.where(visible, jnp.exp(masked - log_totals[..., None]), 0.0)
    d_soft = jnp.einsum("gqhd,gkhd->gqhk", d_heads, value_heads, preferred_element_type=jnp.float32)
    d_scores = (soft_weights * (d_soft - delta_rows[..., None])).astype(jnp.bfloat16)
    d_query = score_scale * jnp.einsum(
        "gqhk,gkhd->gqhd", d_scores, key_heads, preferred_element_type=jnp.float32
    )
    queries_flat = moved_qkv[:, :, 0]
    query_piece = lax.all_gather(queries_flat, "blk", axis=1, tiled=True)
    dout_piece = lax.all_gather(d_heads_flat, "blk", axis=1, tiled=True)
    seg_piece = lax.all_gather(seg_bf, "blk", axis=1, tiled=True)
    piece_rows = query_piece.shape[1]
    piece_pos = jnp.arange(piece_rows, dtype=jnp.int32)
    visible = visibility(piece_pos, seg_piece.astype(jnp.int32), query_pos[None, :], seg_here)
    query_heads = query_piece.reshape(groups, piece_rows, heads_here, HEAD_DIM)
    dout_heads = dout_piece.reshape(groups, piece_rows, heads_here, HEAD_DIM)
    scores = score_scale * jnp.einsum(
        "gqhd,gkhd->gqhk", query_heads, keys_local, preferred_element_type=jnp.float32
    )
    masked = jnp.where(visible, scores, -1e30)
    soft_weights = jnp.where(visible, jnp.exp(masked - lse_all[..., None]), 0.0)
    d_soft = jnp.einsum(
        "gqhd,gkhd->gqhk", dout_heads, values_local, preferred_element_type=jnp.float32
    )
    d_scores = (soft_weights * (d_soft - delta_all[..., None])).astype(jnp.bfloat16)
    new_value = jnp.einsum(
        "gqhk,gqhd->gkhd",
        soft_weights.astype(jnp.bfloat16),
        dout_heads,
        preferred_element_type=jnp.float32,
    )
    new_key = score_scale * jnp.einsum(
        "gqhk,gqhd->gkhd", d_scores, query_heads, preferred_element_type=jnp.float32
    )
    d_stacked = (
        jnp.stack([d_query, new_key, new_value], axis=2)
        .astype(jnp.bfloat16)
        .reshape(groups, seg_len, 3, head_width)
    )
    d_projected = lax.all_to_all(d_stacked, "head", split_axis=0, concat_axis=3, tiled=True)
    d_proj_rows = d_projected.reshape(row_count, 3 * model_width)
    grad_qkv = jnp.einsum("ra,rb->ab", normed_one, d_proj_rows, preferred_element_type=jnp.float32)
    d_normed_one = jnp.einsum(
        "rb,ab->ra", d_proj_rows, proj_qkv, preferred_element_type=jnp.float32
    )
    d_token_part, grad_gain_one = norm_one_pull(d_normed_one)
    grad_tokens = (d_residual + d_token_part).reshape(group_local, seg_len, resid_width)
    mixed = mixed.reshape(group_local, seg_len, resid_width)
    return (
        mixed,
        grad_tokens,
        (grad_qkv, grad_out, grad_up, grad_down, grad_gain_one, grad_gain_two),
    )


def on_device(tokens, segments, cotangent, w_qkv, w_out, w_up, w_down, gain_one, gain_two):
    micro_count = tokens.shape[0]
    seg_len = tokens.shape[2]
    query_pos = lax.axis_index("blk") * seg_len + jnp.arange(seg_len, dtype=jnp.int32)
    mixed_list = []
    token_grad_list = []
    grad_terms = []
    for batch_index in range(micro_count):
        weights_full = (
            lax.all_gather(w_qkv, ("head", "blk"), axis=0, tiled=True),
            lax.all_gather(w_out, ("head", "blk"), axis=0, tiled=True),
            lax.all_gather(w_up, ("head", "blk"), axis=0, tiled=True),
            lax.all_gather(w_down, ("head", "blk"), axis=0, tiled=True),
            lax.all_gather(gain_one, ("head", "blk"), axis=0, tiled=True),
            lax.all_gather(gain_two, ("head", "blk"), axis=0, tiled=True),
        )
        mixed, grad_tokens, gradients = micro_step(
            tokens[batch_index],
            segments[batch_index],
            cotangent[batch_index],
            weights_full,
            query_pos,
        )
        mixed_list.append(mixed)
        token_grad_list.append(grad_tokens)
        grad_terms.append(
            (
                lax.psum_scatter(gradients[0], ("head", "blk"), scatter_dimension=0, tiled=True),
                lax.psum_scatter(gradients[1], ("head", "blk"), scatter_dimension=0, tiled=True),
                lax.psum_scatter(gradients[2], ("head", "blk"), scatter_dimension=0, tiled=True),
                lax.psum_scatter(gradients[3], ("head", "blk"), scatter_dimension=0, tiled=True),
                lax.psum_scatter(gradients[4], ("head", "blk"), scatter_dimension=0, tiled=True),
                lax.psum_scatter(gradients[5], ("head", "blk"), scatter_dimension=0, tiled=True),
            )
        )
    summed = grad_terms[0]
    for later_terms in grad_terms[1:]:
        summed = tuple((first + second for first, second in zip(summed, later_terms)))
    mixed_all = jnp.stack(mixed_list, axis=0)
    token_grads = jnp.stack(token_grad_list, axis=0)
    return (
        mixed_all,
        token_grads,
        summed[0],
        summed[1],
        summed[2],
        summed[3],
        summed[4],
        summed[5],
    )


CORE, AXIS_X, AXIS_Z_NEAR, AXIS_Z_FAR, AXIS_Y = 1, 2, 4, 8, 16
DEVICES = 32
WIDTH = 768
HALF = 384
UNITS = 1536
ROWS = 256
POSITIONS = 1024
MIB = 1024 * 1024


def swap(array, bit, keep=lambda source: True):
    pairs = [(i, i ^ bit) for i in range(DEVICES) if keep(i)]
    return lax.ppermute(array, ("head", "blk"), pairs)


def upward(bit):
    return lambda source: source & bit == 0


def downward(bit):
    return lambda source: source & bit != 0


def dot(a, b):
    return lax.dot_general(a, b, (((1,), (0,)), ((), ())), preferred_element_type=jnp.float32)


def dot_nt(a, b):
    return lax.dot_general(a, b, (((1,), (1,)), ((), ())), preferred_element_type=jnp.float32)


def dot_tn(a, b):
    return lax.dot_general(a, b, (((0,), (0,)), ((), ())), preferred_element_type=jnp.float32)


def lanes(rows):
    return lax.broadcasted_iota(jnp.int32, (rows, WIDTH), 1)


def norm_rows(values, lane):
    inner = jnp.where(lane < WIDTH - 1, values, 0.0)
    total = jnp.sum(inner, axis=-1, keepdims=True)
    full = jnp.where(lane == WIDTH - 1, -total, inner)
    factor = lax.rsqrt(jnp.mean(full * full, axis=-1, keepdims=True) + 1e-05)
    return full * factor, factor


def norm_rows_back(d_normed, normed, factor, lane):
    inner = jnp.mean(d_normed * normed, axis=-1, keepdims=True)
    d_full = factor * (d_normed - normed * inner)
    last = jnp.sum(jnp.where(lane == WIDTH - 1, d_full, 0.0), axis=-1, keepdims=True)
    return jnp.where(lane < WIDTH - 1, d_full - last, 0.0)


def piece_chip(which, pair, entry):
    z_bits = (entry & 3) << 1
    other = entry >> 2
    return z_bits | ((other | pair << 3) if which == 0 else (other << 3 | pair))


def gather_z(block):
    near = swap(block, AXIS_Z_NEAR)
    far = swap(block, AXIS_Z_FAR)
    end = swap(block, AXIS_Z_NEAR | AXIS_Z_FAR)
    return block, near, far, end


def gather_first(four, cut):
    four_a = jnp.stack([array[:, :cut] for array in four])
    four_b = jnp.stack([array[:, cut:] for array in four])
    return four_a, swap(four_a, AXIS_X), four_b, swap(four_b, AXIS_Y)


def gather_second(four_a, got_a, four_b, got_b):
    eight_a = jnp.concatenate([four_a, got_a], axis=0)
    eight_b = jnp.concatenate([four_b, got_b], axis=0)
    return eight_a, swap(eight_a, AXIS_Y), eight_b, swap(eight_b, AXIS_X)


def add(first, *others):
    total = first.astype(jnp.float32)
    for other in others:
        total = total + other.astype(jnp.float32)
    return total


def reduce_start(pieces):
    keep_a, send_a, keep_b, send_b = pieces
    return keep_a, swap(send_a, AXIS_Y), keep_b, swap(send_b, AXIS_X)


def reduce_middle(keep_a, got_a, keep_b, got_b):
    send_a = add(keep_a[4:], got_a[4:]).astype(jnp.bfloat16)
    send_b = add(keep_b[4:], got_b[4:]).astype(jnp.bfloat16)
    left_a = (keep_a[:4], got_a[:4], swap(send_a, AXIS_X))
    left_b = (keep_b[:4], got_b[:4], swap(send_b, AXIS_Y))
    return left_a, left_b


def along_z(four):
    near = swap(four[1], AXIS_Z_NEAR)
    far = swap(four[2], AXIS_Z_FAR)
    end = swap(four[3], AXIS_Z_NEAR | AXIS_Z_FAR)
    return near, far, end


def reduce_z(left_a, left_b):
    four = jnp.concatenate([add(*left_a), add(*left_b)], axis=-1).astype(jnp.bfloat16)
    return (four[0], *along_z(four))


def fence(*arrays):
    return lax.optimization_barrier(arrays)


def piece_rows(chip, which, pair, entry):
    return pl.ds(pl.multiple_of((chip ^ piece_chip(which, pair, entry)) * 48, 16), 48)


def take_pieces(pieces, target, chip, which):
    for pair in range(2):
        for entry in range(8):
            target[piece_rows(chip, which, pair, entry), :] = pieces[pair][entry]


def give_pieces(pieces, source, chip, which):
    for pair in range(2):
        for entry in range(8):
            pieces[pair][entry] = source[piece_rows(chip, which, pair, entry), :]


def row_block(entry, place, core):
    rel = (entry & 3) << 1 | entry >> 2
    return pl.ds(pl.multiple_of(((place ^ rel) * 2 + core) * 64, 64), 64)


def split_heads(both):
    small = lax.broadcasted_iota(jnp.int32, both.shape, 1) < HEAD_DIM
    zero = jnp.zeros_like(both)
    return jnp.concatenate([jnp.where(small, both, zero), jnp.where(small, zero, both)], axis=0)


def join_heads(stacked):
    rows = stacked.shape[0] // 2
    small = lax.broadcasted_iota(jnp.int32, (rows, stacked.shape[1]), 1) < HEAD_DIM
    return jnp.where(small, stacked[:rows], stacked[rows:])


def forward_kernel(
    ids, tok_mine, tok_other, w0, w1, w2, w3,
    attn_out, query_out, own_out, gains_out, kv, normed, soft, wqkv, wout,
    tok, bias,
):
    chip, core = ids[0], ids[1]
    place = lax.rem(chip, 8)
    take_pieces((w0, w1), wqkv, chip, 0)
    take_pieces((w2, w3), wout, chip, 1)
    first_row = pl.multiple_of(place * 128, 128)
    lane = lanes(ROWS)
    picks = lax.broadcasted_iota(jnp.int32, (8, 128), 0) == lax.broadcasted_iota(
        jnp.int32, (8, 128), 1
    )
    gains_out[...] = dot_nt(picks.astype(jnp.bfloat16), wqkv[:, 3 * HALF :])
    gain = gains_out[0:1, :]
    for micro in range(2):
        for entry in range(8):
            tok[micro, row_block(entry, place, core), :] = tok_mine[entry, micro]
            tok[micro, row_block(entry, place, 1 - core), :] = tok_other[entry, micro]
        for chunk in range(POSITIONS // ROWS):
            rows = slice(chunk * ROWS, chunk * ROWS + ROWS)
            values = tok[micro, rows, :].astype(jnp.float32)
            rows_normed = (norm_rows(values, lane)[0] * gain).astype(jnp.bfloat16)
            normed[micro, rows, :] = rows_normed
            kv[micro, rows, :] = dot(rows_normed, wqkv[:, HALF : 3 * HALF]).astype(jnp.bfloat16)
    hot = (lax.broadcasted_iota(jnp.int32, (8, WIDTH), 1) == WIDTH - 1).astype(jnp.bfloat16)
    for micro in range(2):
        here = slice(micro * 128, micro * 128 + 128)
        own = tok[micro, pl.ds(first_row, 128), :]
        own_out[here, :] = own
        query = dot(normed[micro, pl.ds(first_row, 128), :], wqkv[:, :HALF])
        query = query.astype(jnp.bfloat16) * jnp.bfloat16(0.125)
        query_out[here, :] = query
        query_seg = dot_nt(hot, own)[0:1, :]
        key_seg = tok[micro, :, WIDTH - 1 :].astype(jnp.float32)
        key_pos = lax.broadcasted_iota(jnp.int32, (POSITIONS, 128), 0)
        query_pos = first_row + lax.broadcasted_iota(jnp.int32, (POSITIONS, 128), 1)
        seen = (key_pos <= query_pos) & ((key_seg == 0.0) | (key_seg == query_seg))
        one = jnp.where(seen, 0.0, -1e30)
        bias[:, :128] = one
        bias[:, 128:] = one
        for pair in range(3):
            cols = slice(pair * 128, pair * 128 + 128)
            stacked = split_heads(query[:, cols])
            scores = dot_nt(kv[micro, :, cols], stacked) + bias[...]
            top = jnp.max(scores, axis=0, keepdims=True)
            terms = jnp.exp(scores - top)
            total = jnp.sum(terms, axis=0, keepdims=True)
            weights = (terms * (1.0 / total)).astype(jnp.bfloat16)
            soft[micro * 3 + pair] = weights
            value = kv[micro, :, HALF + pair * 128 : HALF + pair * 128 + 128]
            mixed = dot_tn(value, weights)
            attn_out[here, cols] = join_heads(mixed.T).astype(jnp.bfloat16)


def feed_half(normed, cot, up, down, g_up, g_down):
    slope = math.sqrt(2.0 / math.pi)
    hidden = dot(normed, up[...])
    square = hidden * hidden
    wave = jnp.tanh(slope * hidden * (1.0 + 0.044715 * square))
    active = (0.5 * hidden * (1.0 + wave)).astype(jnp.bfloat16)
    grow = 0.5 * (1.0 + wave) + 0.5 * hidden * (1.0 - wave * wave) * slope * (
        1.0 + 3.0 * 0.044715 * square
    )
    d_hidden = (dot_nt(cot, down[...]) * grow).astype(jnp.bfloat16)
    g_up[...] = dot_tn(normed, d_hidden).astype(jnp.bfloat16)
    g_down[...] = dot_tn(active, cot).astype(jnp.bfloat16)
    return dot(active, down[...]), dot_nt(d_hidden, up[...])


def feed_first_kernel(
    ids, gains, attn_mine, attn_other, own, wout_mine, wout_other, cot_mine, cot_other,
    w0, w1, w2, w3,
    attn_out, cot_out, res_out, normed_out, sum_mix, sum_norm, g0, g1, g2, g3,
    up, down, g_up, g_down,
):
    chip, core = ids[0], ids[1]
    take_pieces((w0, w1), up, chip, 0)
    take_pieces((w2, w3), down, chip, 1)
    mine_at = pl.multiple_of(core * HALF, 128)
    other_at = pl.multiple_of((1 - core) * HALF, 128)
    attn_out[:, pl.ds(mine_at, HALF)] = attn_mine[...]
    attn_out[:, pl.ds(other_at, HALF)] = attn_other[...]
    for micro in range(2):
        for side, source in ((core, cot_mine), (1 - core, cot_other)):
            at = pl.multiple_of(micro * 128 + side * 64, 64)
            cot_out[pl.ds(at, 64), :] = source[micro]
    lane = lanes(ROWS)
    attn = attn_out[...]
    res_out[:, pl.ds(mine_at, HALF)] = dot(attn, wout_mine[...])
    res_out[:, pl.ds(other_at, HALF)] = dot(attn, wout_other[...])
    own_values = jnp.where(lane < WIDTH - 1, own[...].astype(jnp.float32), 0.0)
    residual = res_out[...] + own_values
    res_out[...] = residual
    normed = (norm_rows(residual, lane)[0] * gains[1:2, :]).astype(jnp.bfloat16)
    normed_out[...] = normed
    mix, norm = feed_half(normed, cot_out[...], up, down, g_up, g_down)
    sum_mix[...] = mix
    sum_norm[...] = norm
    give_pieces((g0, g1), g_up, chip, 0)
    give_pieces((g2, g3), g_down, chip, 1)


def feed_second_kernel(
    ids, normed, cot, mix_in, norm_in, w0, w1, w2, w3,
    part_out, g0, g1, g2, g3,
    up, down, g_up, g_down,
):
    chip = ids[0]
    take_pieces((w0, w1), up, chip, 0)
    take_pieces((w2, w3), down, chip, 1)
    mix, norm = feed_half(normed[...], cot[...], up, down, g_up, g_down)
    part_out[:ROWS, :] = (mix_in[...] + mix).astype(jnp.bfloat16)
    part_out[ROWS:, :] = (norm_in[...] + norm).astype(jnp.bfloat16)
    give_pieces((g0, g1), g_up, chip, 0)
    give_pieces((g2, g3), g_down, chip, 1)


def backward_kernel(
    ids, gains, residual, part_mine, part_other, cot, wout_mine, wout_other, query,
    wqkv, kv, soft,
    mixed_out, dres_out, d_query, d_sum_half, keep_rows, send_rows, d_kv,
    d_attn, d_rows, d_sum_ref, hold,
):
    chip, core = ids[0], ids[1]
    place = lax.rem(chip, 8)
    first_row = pl.multiple_of(place * 128, 128)
    mine_at = pl.multiple_of(core * HALF, 128)
    other_at = pl.multiple_of((1 - core) * HALF, 128)
    lane = lanes(ROWS)
    res = residual[...]
    hold[...] = add(res, part_mine[:ROWS, :], part_other[:ROWS, :])
    for micro in range(2):
        at = pl.multiple_of(micro * 128 + core * 64, 64)
        mixed_out[micro] = hold[pl.ds(at, 64), : WIDTH - 1].astype(jnp.bfloat16)
    d_normed = add(part_mine[ROWS:, :], part_other[ROWS:, :]) * gains[1:2, :]
    normed_two, factor = norm_rows(res, lane)
    d_res = cot[...].astype(jnp.float32) + norm_rows_back(d_normed, normed_two, factor, lane)
    hold[...] = d_res
    for micro in range(2):
        at = pl.multiple_of(micro * 128 + core * 64, 64)
        dres_out[micro] = hold[pl.ds(at, 64), :]
    d_sum_ref[...] = d_res.astype(jnp.bfloat16)
    d_mine = d_sum_ref[:, pl.ds(mine_at, HALF)]
    d_other = d_sum_ref[:, pl.ds(other_at, HALF)]
    d_sum_half[...] = d_mine
    d_heads = dot_nt(d_mine, wout_mine[pl.ds(mine_at, HALF), :]) + dot_nt(
        d_other, wout_other[pl.ds(mine_at, HALF), :]
    )
    d_attn[...] = d_heads.astype(jnp.bfloat16)
    for micro in range(2):
        here = slice(micro * 128, micro * 128 + 128)
        for pair in range(3):
            cols = slice(pair * 128, pair * 128 + 128)
            value_cols = slice(HALF + pair * 128, HALF + pair * 128 + 128)
            d_out = split_heads(d_attn[here, cols])
            weights = soft[micro * 3 + pair]
            d_soft = dot_nt(kv[micro, :, value_cols], d_out)
            weights_f = weights.astype(jnp.float32)
            delta = jnp.sum(weights_f * d_soft, axis=0, keepdims=True)
            d_scores = (weights_f * (d_soft - delta)).astype(jnp.bfloat16)
            d_q = dot_tn(kv[micro, :, cols], d_scores) * 0.125
            d_query[here, cols] = join_heads(d_q.T).astype(jnp.bfloat16)
            d_kv[micro, :, cols] = dot(d_scores, split_heads(query[here, cols])).astype(
                jnp.bfloat16
            )
            d_kv[micro, :, value_cols] = dot(weights, d_out).astype(jnp.bfloat16)
        for chunk in range(POSITIONS // ROWS):
            at = slice(chunk * ROWS, chunk * ROWS + ROWS)
            rows = dot_nt(d_kv[micro, at, :], wqkv[:, HALF : 3 * HALF])
            d_rows[micro, at, :] = rows.astype(jnp.bfloat16)
        own = d_rows[micro, pl.ds(first_row, 128), :].astype(jnp.float32)
        own = own + dot_nt(d_query[here, :], wqkv[:, :HALF])
        d_rows[micro, pl.ds(first_row, 128), :] = own.astype(jnp.bfloat16)
        for entry in range(8):
            keep_rows[entry, micro] = d_rows[micro, row_block(entry, place, core), :]
            send_rows[entry, micro] = d_rows[micro, row_block(entry, place, 1 - core), :]


def gradient_kernel(
    ids, attn, d_sum_half, d_query, d_kv, normed, g0, g1, g2, g3, g_a, g_b
):
    chip = ids[0]
    first_row = pl.multiple_of(lax.rem(chip, 8) * 128, 128)
    g_b[...] = dot_tn(attn[...], d_sum_half[...]).astype(jnp.bfloat16)
    own_0 = normed[0, pl.ds(first_row, 128), :]
    own_1 = normed[1, pl.ds(first_row, 128), :]
    g_a[:, :HALF] = (dot_tn(own_0, d_query[:128, :]) + dot_tn(own_1, d_query[128:, :])).astype(
        jnp.bfloat16
    )
    g_a[:, HALF:] = (dot_tn(normed[0], d_kv[0]) + dot_tn(normed[1], d_kv[1])).astype(jnp.bfloat16)
    give_pieces((g0, g1), g_a, chip, 0)
    give_pieces((g2, g3), g_b, chip, 1)


def tail_kernel(gains, tokens, d_0, d_1, d_2, d_3, d_residual, grad_out):
    lane = lanes(128)
    rows = (128, WIDTH)
    values = tokens[...].reshape(rows).astype(jnp.float32)
    normed, factor = norm_rows(values, lane)
    d_normed = add(d_0[...], d_1[...], d_2[...], d_3[...]).reshape(rows) * gains[0:1, :]
    out = d_residual[...].reshape(rows) + norm_rows_back(d_normed, normed, factor, lane)
    grad_out[...] = out[:, : WIDTH - 1].reshape(2, 64, WIDTH - 1)


VMEM = pl.BlockSpec(memory_space=pltpu.VMEM)
SMEM = pl.BlockSpec(memory_space=pltpu.SMEM)


def shaped(shape, dtype=jnp.bfloat16):
    return jax.ShapeDtypeStruct(shape, dtype)


def call(kernel, ins, outs, scratch, name, mib):
    return pl.pallas_call(
        kernel,
        in_specs=[spec for spec in ins],
        out_specs=[spec for spec, _ in outs],
        out_shape=[shape for _, shape in outs],
        scratch_shapes=scratch,
        name=name,
        cost_estimate=pl.CostEstimate(flops=0, transcendentals=0, bytes_accessed=0),
        compiler_params=pltpu.CompilerParams(vmem_limit_bytes=mib * MIB),
    )


def pick(core, zero, one):
    return jnp.where(core == 0, zero, one)


def chip_block(core, for_zero, for_one):
    mine = pick(core, for_zero, for_one)
    other = swap(pick(core, for_one, for_zero), CORE)
    return jnp.concatenate([pick(core, mine, other), pick(core, other, mine)], axis=0)


def core_rows(core, block):
    rows = block.shape[0] // 2
    mine = pick(core, block[:rows], block[rows:])
    other = swap(pick(core, block[rows:], block[:rows]), CORE)
    return pick(core, mine, other), pick(core, other, mine)


def split_units(w_up, blocks):
    rows = w_up.shape[0]
    parts = w_up.reshape(rows, blocks, 2, 2, -1)
    return [parts[:, :, k].swapaxes(1, 2).reshape(rows, -1) for k in range(2)]


def join_units(first, second, blocks):
    rows = first.shape[0]
    parts = [half.reshape(rows, 2, blocks, -1).swapaxes(1, 2) for half in (first, second)]
    return jnp.stack(parts, axis=2).reshape(rows, -1)


def on_chip_pair(tokens, segments, cotangent, w_qkv, w_out, w_up, w_down, gain_one, gain_two):
    bf, f32 = jnp.bfloat16, jnp.float32
    device = lax.axis_index("head") * 16 + lax.axis_index("blk")
    core = device % 2
    ids = jnp.stack([device // 2, core]).astype(jnp.int32)
    own = jnp.concatenate([tokens[:, 0], segments[:, 0, :, None].astype(bf)], axis=-1)
    cot = jnp.pad(cotangent[:, 0], ((0, 0), (0, 0), (0, 1)))
    four = jnp.stack(
        [
            own,
            swap(own, AXIS_Z_NEAR, upward(AXIS_Z_NEAR)),
            swap(own, AXIS_Z_FAR, upward(AXIS_Z_FAR)),
            swap(own, AXIS_Z_NEAR | AXIS_Z_FAR, upward(AXIS_Z_FAR)),
        ]
    )
    eight = jnp.concatenate([four, swap(four, AXIS_X)], axis=0)
    eight_other = swap(eight, CORE)
    gain_cols = jnp.pad(jnp.stack([gain_one, gain_two], axis=-1), ((0, 0), (0, 126)))
    out_wide = jnp.pad(w_out, ((0, 0), (0, 1)))
    down_wide = jnp.pad(w_down, ((0, 0), (0, 1)))
    qkv_parts = w_qkv.reshape(-1, 3, 2, HALF)
    attn_halves = [
        jnp.concatenate(
            [qkv_parts[:, 0, k], qkv_parts[:, 1, k], qkv_parts[:, 2, k], gain_cols]
            + [out_wide[:, k * HALF : k * HALF + HALF]],
            axis=-1,
        )
        for k in range(2)
    ]
    wide = 3 * HALF + 128
    attn_four = gather_z(chip_block(core, *attn_halves))
    attn_first = gather_first(attn_four, wide)
    up_block = chip_block(core, *split_units(w_up, 16))
    feed_blocks = [
        jnp.concatenate(
            [up_block[:, half * WIDTH :][:, :WIDTH], down_wide[half * 48 : half * 48 + 48]], axis=-1
        )
        for half in range(2)
    ]
    four_0 = gather_z(fence(feed_blocks[0], *attn_four[1:])[0])
    four_1 = gather_z(fence(feed_blocks[1], *four_0[1:])[0])
    attn_pieces = gather_second(*attn_first)
    first_0 = gather_first(fence(*four_0, *attn_first)[:4], WIDTH)
    first_1 = gather_first(fence(*four_1, *first_0)[:4], WIDTH)
    pieces_0 = gather_second(*fence(*first_0, *attn_pieces)[:4])
    cot_other = swap(cot, CORE)
    rows_shape = shaped((2, POSITIONS, WIDTH))
    attn, query, own_rows, gains, kv, normed_all, soft, wqkv, wout = call(
        forward_kernel,
        [SMEM] + [VMEM] * 6,
        [
            (VMEM, shaped((ROWS, HALF))),
            (VMEM, shaped((ROWS, HALF))),
            (VMEM, shaped((ROWS, WIDTH))),
            (VMEM, shaped((8, WIDTH), f32)),
            (VMEM, rows_shape),
            (VMEM, rows_shape),
            (VMEM, shaped((6, POSITIONS, ROWS))),
            (VMEM, shaped((WIDTH, wide))),
            (VMEM, shaped((WIDTH, HALF))),
        ],
        [
            pltpu.VMEM((2, POSITIONS, WIDTH), bf),
            pltpu.VMEM((POSITIONS, ROWS), f32),
        ],
        "attention_forward",
        30,
    )(ids, eight, eight_other, *attn_pieces)
    attn_other = swap(attn, CORE)
    wout_other = swap(wout, CORE)
    pieces_1 = gather_second(*fence(*first_1, *pieces_0, attn)[:4])
    weight_scratch = [pltpu.VMEM((WIDTH, WIDTH), bf)] * 4
    piece_shapes = [(VMEM, shaped((8, 48, WIDTH)))] * 4
    outs = call(
        feed_first_kernel,
        [SMEM] + [VMEM] * 8 + [VMEM] * 4,
        [
            (VMEM, shaped((ROWS, WIDTH))),
            (VMEM, shaped((ROWS, WIDTH))),
            (VMEM, shaped((ROWS, WIDTH), f32)),
            (VMEM, shaped((ROWS, WIDTH))),
            (VMEM, shaped((ROWS, WIDTH), f32)),
            (VMEM, shaped((ROWS, WIDTH), f32)),
        ]
        + piece_shapes,
        weight_scratch,
        "feed_forward_and_back_first",
        20,
    )(
        ids, gains, attn, attn_other, own_rows, wout, wout_other, cot, cot_other, *pieces_0
    )
    attn_all, cot_all, residual, normed_two, sum_mix, sum_norm = outs[:6]
    feed_0 = reduce_start(outs[6:])
    part, *grads_1 = call(
        feed_second_kernel,
        [SMEM] + [VMEM] * 4 + [VMEM] * 4,
        [(VMEM, shaped((2 * ROWS, WIDTH)))] + piece_shapes,
        weight_scratch,
        "feed_forward_and_back_second",
        20,
    )(ids, normed_two, cot_all, sum_mix, sum_norm, *pieces_1)
    feed_0, part, grads_1 = fence(feed_0, part, grads_1)
    part_other = swap(part, CORE)
    feed_0 = reduce_middle(*feed_0)
    feed_1 = reduce_start(grads_1)
    outs = call(
        backward_kernel,
        [SMEM] + [VMEM] * 11,
        [
            (VMEM, shaped((2, 64, WIDTH - 1))),
            (VMEM, shaped((2, 64, WIDTH), f32)),
            (VMEM, shaped((ROWS, HALF))),
            (VMEM, shaped((ROWS, HALF))),
            (VMEM, shaped((8, 2, 64, WIDTH))),
            (VMEM, shaped((8, 2, 64, WIDTH))),
            (VMEM, rows_shape),
        ],
        [
            pltpu.VMEM((ROWS, HALF), bf),
            pltpu.VMEM((2, POSITIONS, WIDTH), bf),
            pltpu.VMEM((ROWS, WIDTH), bf),
            pltpu.VMEM((ROWS, WIDTH), f32),
        ],
        "attention_backward",
        30,
    )(
        ids, gains, residual, part, part_other, cot_all, wout, wout_other, query,
        wqkv, kv, soft,
    )
    mixed, d_residual, *outs = outs
    outs, feed_0, feed_1 = fence(outs, feed_0, feed_1)
    d_query, d_sum_half, keep_rows, send_rows, d_kv = outs
    feed_0 = reduce_z(*feed_0)
    feed_1 = reduce_middle(*feed_1)
    got_rows = swap(send_rows, CORE)
    grad_attn_pieces = call(
        gradient_kernel,
        [SMEM] + [VMEM] * 5,
        [(VMEM, shaped((8, 48, 3 * HALF)))] * 2 + [(VMEM, shaped((8, 48, HALF)))] * 2,
        [
            pltpu.VMEM((WIDTH, 3 * HALF), bf),
            pltpu.VMEM((WIDTH, HALF), bf),
        ],
        "attention_weight_gradients",
        20,
    )(ids, attn_all, d_sum_half, d_query, d_kv, normed_all)
    keep_rows, got_rows, grad_attn_pieces, feed_0, feed_1 = fence(
        keep_rows, got_rows, grad_attn_pieces, feed_0, feed_1
    )
    crossed = swap(add(keep_rows[4:], got_rows[4:]).astype(bf), AXIS_X)
    attn_first = reduce_start(grad_attn_pieces)
    feed_1 = reduce_z(*feed_1)
    feed_1, crossed, attn_first = fence(feed_1, crossed, attn_first)
    rows_4 = add(keep_rows[:4], got_rows[:4], crossed).astype(bf)
    to_near = swap(rows_4[1], AXIS_Z_NEAR, downward(AXIS_Z_NEAR))
    to_far = swap(rows_4[2], AXIS_Z_FAR, downward(AXIS_Z_FAR))
    to_end = swap(rows_4[3], AXIS_Z_NEAR | AXIS_Z_FAR, downward(AXIS_Z_FAR))
    attn_last = reduce_z(*reduce_middle(*attn_first))
    sum_0, sum_1, attn_sum = add(*feed_0), add(*feed_1), add(*attn_last)
    (grad_tokens,) = call(
        tail_kernel,
        [VMEM] * 7,
        [(VMEM, shaped((2, 64, WIDTH - 1), f32))],
        [],
        "token_gradient",
        8,
    )(gains, own, rows_4[0], to_near, to_far, to_end, d_residual)
    attn_0, attn_1 = core_rows(core, attn_sum)
    up_sum = jnp.concatenate([sum_0[:, :WIDTH], sum_1[:, :WIDTH]], axis=-1)
    up_0, up_1 = core_rows(core, up_sum)
    grad_qkv = jnp.concatenate(
        [half[:, k * HALF : k * HALF + HALF] for k in range(3) for half in (attn_0, attn_1)],
        axis=-1,
    )
    grad_out = jnp.concatenate([attn_0[:, 3 * HALF :], attn_1[:, 3 * HALF : 4 * HALF - 1]], axis=-1)
    grad_up = join_units(up_0, up_1, 16)
    grad_down = jnp.concatenate([sum_0[:, WIDTH:], sum_1[:, WIDTH:]], axis=0)
    grad_gain_one = jnp.sum(grad_qkv * w_qkv.astype(f32), axis=-1) / gain_one.astype(f32)
    grad_gain_two = jnp.sum(grad_up * w_up.astype(f32), axis=-1) / gain_two.astype(f32)
    return (
        mixed[:, None],
        grad_tokens[:, None],
        grad_qkv,
        grad_out,
        grad_up,
        grad_down[:, : WIDTH - 1],
        grad_gain_one,
        grad_gain_two,
    )


def solution(mesh):
    small_slice = (mesh.shape["head"], mesh.shape["blk"]) == (2, 16)
    placed = (
        P(None, "head", "blk", None),
        P(None, "head", "blk"),
        P(None, "head", "blk", None),
        P(("head", "blk"), None),
        P(("head", "blk"), None),
        P(("head", "blk"), None),
        P(("head", "blk"), None),
        P(("head", "blk")),
        P(("head", "blk")),
    )
    return jax.shard_map(
        on_chip_pair if small_slice else on_device,
        mesh=mesh,
        in_specs=placed,
        out_specs=(
            P(None, "head", "blk", None),
            P(None, "head", "blk", None),
            P(("head", "blk"), None),
            P(("head", "blk"), None),
            P(("head", "blk"), None),
            P(("head", "blk"), None),
            P(("head", "blk")),
            P(("head", "blk")),
        ),
        check_vma=False,
    )
```

```python
import math

import jax
import jax.numpy as jnp
from jax import lax
from jax.experimental import pallas as pl
from jax.experimental.pallas import tpu as pltpu
from jax.sharding import PartitionSpec as P

HEAD_DIM = 64


def compress_norm(values, gain):
    total_sum = jnp.sum(values, axis=-1, keepdims=True)
    full_vec = jnp.concatenate([values, -total_sum], axis=-1)
    factor = lax.rsqrt(jnp.mean(full_vec * full_vec, axis=-1, keepdims=True) + 1e-05)
    return full_vec * factor * gain


def gelu_tanh(values):
    return jax.nn.gelu(values, approximate=True)


def visibility(query_pos, query_seg, key_pos, key_seg):
    causal = key_pos[:, None, :] <= query_pos[None, :, None]
    shared = (key_seg[:, None, :] == 0) | (key_seg[:, None, :] == query_seg[:, :, None])
    return (causal & shared)[:, :, None, :]


def micro_step(token_block, segment_block, cotangent_block, weights_full, query_pos):
    proj_qkv, proj_out, proj_up, proj_down, norm_one, norm_two = weights_full
    norm_one = norm_one.astype(jnp.float32)
    norm_two = norm_two.astype(jnp.float32)
    group_local, seg_len, resid_width = token_block.shape
    model_width = proj_qkv.shape[0]
    row_count = group_local * seg_len
    score_scale = 1.0 / math.sqrt(HEAD_DIM)
    token_rows = token_block.astype(jnp.float32).reshape(row_count, resid_width)
    normed_f, norm_one_pull = jax.vjp(compress_norm, token_rows, norm_one)
    normed_one = normed_f.astype(jnp.bfloat16)
    projected = jnp.dot(normed_one, proj_qkv, preferred_element_type=jnp.float32).astype(
        jnp.bfloat16
    )
    projected = projected.reshape(group_local, seg_len, 3, model_width)
    head_groups = lax.axis_size("head")
    seg_wide = jnp.broadcast_to(
        segment_block.astype(jnp.bfloat16)[:, :, None, None], (group_local, seg_len, 1, head_groups)
    )
    moved_qkv, moved_seg = (
        lax.all_to_all(projected, "head", split_axis=3, concat_axis=0, tiled=True),
        lax.all_to_all(seg_wide, "head", split_axis=3, concat_axis=0, tiled=True),
    )
    groups = moved_qkv.shape[0]
    head_width = moved_qkv.shape[3]
    heads_here = head_width // HEAD_DIM
    head_shape = (groups, seg_len, heads_here, HEAD_DIM)
    queries = moved_qkv[:, :, 0].reshape(head_shape)
    keys_flat = moved_qkv[:, :, 1]
    values_flat = moved_qkv[:, :, 2]
    keys_local = keys_flat.reshape(head_shape)
    values_local = values_flat.reshape(head_shape)
    seg_bf = moved_seg[:, :, 0, 0]
    seg_here = seg_bf.astype(jnp.int32)
    key_piece = lax.all_gather(keys_flat, "blk", axis=1, tiled=True)
    value_piece = lax.all_gather(values_flat, "blk", axis=1, tiled=True)
    seg_piece = lax.all_gather(seg_bf, "blk", axis=1, tiled=True)
    key_pos = jnp.arange(key_piece.shape[1], dtype=jnp.int32)[None, :]
    running_max = jnp.full((groups, seg_len, heads_here), -1e30, jnp.float32)
    piece_rows = key_piece.shape[1]
    visible = visibility(query_pos, seg_here, key_pos, seg_piece.astype(jnp.int32))
    key_heads = key_piece.reshape(groups, piece_rows, heads_here, HEAD_DIM)
    value_heads = value_piece.reshape(groups, piece_rows, heads_here, HEAD_DIM)
    scores = score_scale * jnp.einsum(
        "gqhd,gkhd->gqhk", queries, key_heads, preferred_element_type=jnp.float32
    )
    masked = jnp.where(visible, scores, -1e30)
    new_max = jnp.maximum(running_max, jnp.max(masked, axis=-1))
    exp_terms = jnp.where(visible, jnp.exp(masked - new_max[..., None]), 0.0)
    new_sum = jnp.sum(exp_terms, axis=-1)
    new_acc = jnp.einsum(
        "gqhk,gkhd->gqhd",
        exp_terms.astype(jnp.bfloat16),
        value_heads,
        preferred_element_type=jnp.float32,
    )
    attn_f = new_acc / new_sum[..., None]
    log_totals = new_max + jnp.log(new_sum)
    attn_heads = attn_f.astype(jnp.bfloat16).reshape(groups, seg_len, head_width)
    attention = lax.all_to_all(attn_heads, "head", split_axis=0, concat_axis=2, tiled=True)
    attn_rows = attention.reshape(row_count, model_width)
    residual = token_rows + jnp.dot(attn_rows, proj_out, preferred_element_type=jnp.float32)
    normed_two_f, norm_two_pull = jax.vjp(compress_norm, residual, norm_two)
    normed_two = normed_two_f.astype(jnp.bfloat16)
    hidden = jnp.dot(normed_two, proj_up, preferred_element_type=jnp.float32)
    activated_f, gelu_pull = jax.vjp(gelu_tanh, hidden)
    activated = activated_f.astype(jnp.bfloat16)
    mixed = (residual + jnp.dot(activated, proj_down, preferred_element_type=jnp.float32)).astype(
        jnp.bfloat16
    )
    cot_rows = cotangent_block.reshape(row_count, resid_width)
    grad_down = jnp.einsum("ra,rb->ab", activated, cot_rows, preferred_element_type=jnp.float32)
    d_activated = jnp.einsum("rb,ab->ra", cot_rows, proj_down, preferred_element_type=jnp.float32)
    (d_hidden,) = gelu_pull(d_activated)
    d_hidden = d_hidden.astype(jnp.bfloat16)
    grad_up = jnp.einsum("ra,rb->ab", normed_two, d_hidden, preferred_element_type=jnp.float32)
    d_normed_two = jnp.einsum("rb,ab->ra", d_hidden, proj_up, preferred_element_type=jnp.float32)
    d_resid_part, grad_gain_two = norm_two_pull(d_normed_two)
    d_residual = cot_rows.astype(jnp.float32) + d_resid_part
    d_sum = d_residual.astype(jnp.bfloat16)
    grad_out = jnp.einsum("ra,rb->ab", attn_rows, d_sum, preferred_element_type=jnp.float32)
    d_attention = jnp.einsum(
        "rb,ab->ra", d_sum, proj_out, preferred_element_type=jnp.float32
    ).astype(jnp.bfloat16)
    d_attention = d_attention.reshape(group_local, seg_len, model_width)
    d_heads_flat = lax.all_to_all(d_attention, "head", split_axis=2, concat_axis=0, tiled=True)
    d_heads = d_heads_flat.reshape(head_shape)
    delta_rows = jnp.sum(d_heads.astype(jnp.float32) * attn_f, axis=-1)
    lse_all, delta_all = (
        lax.all_gather(log_totals, "blk", axis=1, tiled=True),
        lax.all_gather(delta_rows, "blk", axis=1, tiled=True),
    )
    key_piece = lax.all_gather(keys_flat, "blk", axis=1, tiled=True)
    value_piece = lax.all_gather(values_flat, "blk", axis=1, tiled=True)
    seg_piece = lax.all_gather(seg_bf, "blk", axis=1, tiled=True)
    key_pos = jnp.arange(key_piece.shape[1], dtype=jnp.int32)[None, :]
    piece_rows = key_piece.shape[1]
    visible = visibility(query_pos, seg_here, key_pos, seg_piece.astype(jnp.int32))
    key_heads = key_piece.reshape(groups, piece_rows, heads_here, HEAD_DIM)
    value_heads = value_piece.reshape(groups, piece_rows, heads_here, HEAD_DIM)
    scores = score_scale * jnp.einsum(
        "gqhd,gkhd->gqhk", queries, key_heads, preferred_element_type=jnp.float32
    )
    masked = jnp.where(visible, scores, -1e30)
    soft_weights = jnp.where(visible, jnp.exp(masked - log_totals[..., None]), 0.0)
    d_soft = jnp.einsum("gqhd,gkhd->gqhk", d_heads, value_heads, preferred_element_type=jnp.float32)
    d_scores = (soft_weights * (d_soft - delta_rows[..., None])).astype(jnp.bfloat16)
    d_query = score_scale * jnp.einsum(
        "gqhk,gkhd->gqhd", d_scores, key_heads, preferred_element_type=jnp.float32
    )
    queries_flat = moved_qkv[:, :, 0]
    query_piece = lax.all_gather(queries_flat, "blk", axis=1, tiled=True)
    dout_piece = lax.all_gather(d_heads_flat, "blk", axis=1, tiled=True)
    seg_piece = lax.all_gather(seg_bf, "blk", axis=1, tiled=True)
    piece_rows = query_piece.shape[1]
    piece_pos = jnp.arange(piece_rows, dtype=jnp.int32)
    visible = visibility(piece_pos, seg_piece.astype(jnp.int32), query_pos[None, :], seg_here)
    query_heads = query_piece.reshape(groups, piece_rows, heads_here, HEAD_DIM)
    dout_heads = dout_piece.reshape(groups, piece_rows, heads_here, HEAD_DIM)
    scores = score_scale * jnp.einsum(
        "gqhd,gkhd->gqhk", query_heads, keys_local, preferred_element_type=jnp.float32
    )
    masked = jnp.where(visible, scores, -1e30)
    soft_weights = jnp.where(visible, jnp.exp(masked - lse_all[..., None]), 0.0)
    d_soft = jnp.einsum(
        "gqhd,gkhd->gqhk", dout_heads, values_local, preferred_element_type=jnp.float32
    )
    d_scores = (soft_weights * (d_soft - delta_all[..., None])).astype(jnp.bfloat16)
    new_value = jnp.einsum(
        "gqhk,gqhd->gkhd",
        soft_weights.astype(jnp.bfloat16),
        dout_heads,
        preferred_element_type=jnp.float32,
    )
    new_key = score_scale * jnp.einsum(
        "gqhk,gqhd->gkhd", d_scores, query_heads, preferred_element_type=jnp.float32
    )
    d_stacked = (
        jnp.stack([d_query, new_key, new_value], axis=2)
        .astype(jnp.bfloat16)
        .reshape(groups, seg_len, 3, head_width)
    )
    d_projected = lax.all_to_all(d_stacked, "head", split_axis=0, concat_axis=3, tiled=True)
    d_proj_rows = d_projected.reshape(row_count, 3 * model_width)
    grad_qkv = jnp.einsum("ra,rb->ab", normed_one, d_proj_rows, preferred_element_type=jnp.float32)
    d_normed_one = jnp.einsum(
        "rb,ab->ra", d_proj_rows, proj_qkv, preferred_element_type=jnp.float32
    )
    d_token_part, grad_gain_one = norm_one_pull(d_normed_one)
    grad_tokens = (d_residual + d_token_part).reshape(group_local, seg_len, resid_width)
    mixed = mixed.reshape(group_local, seg_len, resid_width)
    return (
        mixed,
        grad_tokens,
        (grad_qkv, grad_out, grad_up, grad_down, grad_gain_one, grad_gain_two),
    )


def on_device(tokens, segments, cotangent, w_qkv, w_out, w_up, w_down, gain_one, gain_two):
    micro_count = tokens.shape[0]
    seg_len = tokens.shape[2]
    query_pos = lax.axis_index("blk") * seg_len + jnp.arange(seg_len, dtype=jnp.int32)
    mixed_list = []
    token_grad_list = []
    grad_terms = []
    for batch_index in range(micro_count):
        weights_full = (
            lax.all_gather(w_qkv, ("head", "blk"), axis=0, tiled=True),
            lax.all_gather(w_out, ("head", "blk"), axis=0, tiled=True),
            lax.all_gather(w_up, ("head", "blk"), axis=0, tiled=True),
            lax.all_gather(w_down, ("head", "blk"), axis=0, tiled=True),
            lax.all_gather(gain_one, ("head", "blk"), axis=0, tiled=True),
            lax.all_gather(gain_two, ("head", "blk"), axis=0, tiled=True),
        )
        mixed, grad_tokens, gradients = micro_step(
            tokens[batch_index],
            segments[batch_index],
            cotangent[batch_index],
            weights_full,
            query_pos,
        )
        mixed_list.append(mixed)
        token_grad_list.append(grad_tokens)
        grad_terms.append(
            (
                lax.psum_scatter(gradients[0], ("head", "blk"), scatter_dimension=0, tiled=True),
                lax.psum_scatter(gradients[1], ("head", "blk"), scatter_dimension=0, tiled=True),
                lax.psum_scatter(gradients[2], ("head", "blk"), scatter_dimension=0, tiled=True),
                lax.psum_scatter(gradients[3], ("head", "blk"), scatter_dimension=0, tiled=True),
                lax.psum_scatter(gradients[4], ("head", "blk"), scatter_dimension=0, tiled=True),
                lax.psum_scatter(gradients[5], ("head", "blk"), scatter_dimension=0, tiled=True),
            )
        )
    summed = grad_terms[0]
    for later_terms in grad_terms[1:]:
        summed = tuple((first + second for first, second in zip(summed, later_terms)))
    mixed_all = jnp.stack(mixed_list, axis=0)
    token_grads = jnp.stack(token_grad_list, axis=0)
    return (
        mixed_all,
        token_grads,
        summed[0],
        summed[1],
        summed[2],
        summed[3],
        summed[4],
        summed[5],
    )


CORE, AXIS_X, AXIS_Z_NEAR, AXIS_Z_FAR, AXIS_Y = 1, 2, 4, 8, 16
DEVICES = 32
WIDTH = 768
HALF = 384
UNITS = 1536
ROWS = 256
POSITIONS = 1024
MIB = 1024 * 1024


def swap(array, bit, keep=lambda source: True):
    pairs = [(i, i ^ bit) for i in range(DEVICES) if keep(i)]
    return lax.ppermute(array, ("head", "blk"), pairs)


def upward(bit):
    return lambda source: source & bit == 0


def downward(bit):
    return lambda source: source & bit != 0


def dot(a, b):
    return lax.dot_general(a, b, (((1,), (0,)), ((), ())), preferred_element_type=jnp.float32)


def dot_nt(a, b):
    return lax.dot_general(a, b, (((1,), (1,)), ((), ())), preferred_element_type=jnp.float32)


def dot_tn(a, b):
    return lax.dot_general(a, b, (((0,), (0,)), ((), ())), preferred_element_type=jnp.float32)


def lanes(rows):
    return lax.broadcasted_iota(jnp.int32, (rows, WIDTH), 1)


def norm_rows(values, lane):
    inner = jnp.where(lane < WIDTH - 1, values, 0.0)
    total = jnp.sum(inner, axis=-1, keepdims=True)
    full = jnp.where(lane == WIDTH - 1, -total, inner)
    factor = lax.rsqrt(jnp.mean(full * full, axis=-1, keepdims=True) + 1e-05)
    return full * factor, factor


def norm_rows_back(d_normed, normed, factor, lane):
    inner = jnp.mean(d_normed * normed, axis=-1, keepdims=True)
    d_full = factor * (d_normed - normed * inner)
    last = jnp.sum(jnp.where(lane == WIDTH - 1, d_full, 0.0), axis=-1, keepdims=True)
    return jnp.where(lane < WIDTH - 1, d_full - last, 0.0)


def piece_chip(which, pair, entry):
    z_bits = (entry & 3) << 1
    other = entry >> 2
    return z_bits | ((other | pair << 3) if which == 0 else (other << 3 | pair))


def gather_z(block):
    near = swap(block, AXIS_Z_NEAR)
    far = swap(block, AXIS_Z_FAR)
    end = swap(block, AXIS_Z_NEAR | AXIS_Z_FAR)
    return block, near, far, end


def gather_first(four, cut):
    four_a = jnp.stack([array[:, :cut] for array in four])
    four_b = jnp.stack([array[:, cut:] for array in four])
    return four_a, swap(four_a, AXIS_X), four_b, swap(four_b, AXIS_Y)


def gather_second(four_a, got_a, four_b, got_b):
    eight_a = jnp.concatenate([four_a, got_a], axis=0)
    eight_b = jnp.concatenate([four_b, got_b], axis=0)
    return eight_a, swap(eight_a, AXIS_Y), eight_b, swap(eight_b, AXIS_X)


def add(first, *others):
    total = first.astype(jnp.float32)
    for other in others:
        total = total + other.astype(jnp.float32)
    return total


def reduce_start(pieces):
    keep_a, send_a, keep_b, send_b = pieces
    return keep_a, swap(send_a, AXIS_Y), keep_b, swap(send_b, AXIS_X)


def reduce_middle(keep_a, got_a, keep_b, got_b):
    send_a = add(keep_a[4:], got_a[4:]).astype(jnp.bfloat16)
    send_b = add(keep_b[4:], got_b[4:]).astype(jnp.bfloat16)
    left_a = (keep_a[:4], got_a[:4], swap(send_a, AXIS_X))
    left_b = (keep_b[:4], got_b[:4], swap(send_b, AXIS_Y))
    return left_a, left_b


def along_z(four):
    near = swap(four[1], AXIS_Z_NEAR)
    far = swap(four[2], AXIS_Z_FAR)
    end = swap(four[3], AXIS_Z_NEAR | AXIS_Z_FAR)
    return near, far, end


def reduce_z(left_a, left_b):
    four = jnp.concatenate([add(*left_a), add(*left_b)], axis=-1).astype(jnp.bfloat16)
    return (four[0], *along_z(four))


def fence(*arrays):
    return lax.optimization_barrier(arrays)


def piece_rows(chip, which, pair, entry):
    return pl.ds(pl.multiple_of((chip ^ piece_chip(which, pair, entry)) * 48, 16), 48)


def take_pieces(pieces, target, chip, which):
    def move(entry, carry):
        for pair in range(2):
            target[piece_rows(chip, which, pair, entry), :] = pieces[pair][entry]
        return carry

    lax.fori_loop(0, 8, move, 0)


def give_pieces(pieces, source, chip, which):
    def move(entry, carry):
        for pair in range(2):
            pieces[pair][entry] = source[piece_rows(chip, which, pair, entry), :]
        return carry

    lax.fori_loop(0, 8, move, 0)


def row_block(entry, place, core):
    rel = (entry & 3) << 1 | entry >> 2
    return pl.ds(pl.multiple_of(((place ^ rel) * 2 + core) * 64, 64), 64)


def split_heads(both):
    small = lax.broadcasted_iota(jnp.int32, both.shape, 1) < HEAD_DIM
    zero = jnp.zeros_like(both)
    return jnp.concatenate([jnp.where(small, both, zero), jnp.where(small, zero, both)], axis=0)


def join_heads(stacked):
    rows = stacked.shape[0] // 2
    small = lax.broadcasted_iota(jnp.int32, (rows, stacked.shape[1]), 1) < HEAD_DIM
    return jnp.where(small, stacked[:rows], stacked[rows:])


def forward_kernel(
    ids, tok_mine, tok_other, w0, w1, w2, w3,
    attn_out, query_out, own_out, gains_out, kv, normed, soft, wqkv, wout,
    tok, bias,
):
    chip, core = ids[0], ids[1]
    place = lax.rem(chip, 8)
    take_pieces((w0, w1), wqkv, chip, 0)
    take_pieces((w2, w3), wout, chip, 1)
    first_row = pl.multiple_of(place * 128, 128)
    lane = lanes(ROWS)
    picks = lax.broadcasted_iota(jnp.int32, (8, 128), 0) == lax.broadcasted_iota(
        jnp.int32, (8, 128), 1
    )
    gains_out[...] = dot_nt(picks.astype(jnp.bfloat16), wqkv[:, 3 * HALF :])
    gain = gains_out[0:1, :]
    for micro in range(2):
        def move(entry, carry, micro=micro):
            tok[micro, row_block(entry, place, core), :] = tok_mine[entry, micro]
            tok[micro, row_block(entry, place, 1 - core), :] = tok_other[entry, micro]
            return carry

        lax.fori_loop(0, 8, move, 0)

        def norm_chunk(chunk, carry, micro=micro):
            rows = pl.ds(pl.multiple_of(chunk * ROWS, ROWS), ROWS)
            values = tok[micro, rows, :].astype(jnp.float32)
            rows_normed = (norm_rows(values, lane)[0] * gain).astype(jnp.bfloat16)
            normed[micro, rows, :] = rows_normed
            kv[micro, rows, :] = dot(rows_normed, wqkv[:, HALF : 3 * HALF]).astype(jnp.bfloat16)
            return carry

        lax.fori_loop(0, POSITIONS // ROWS, norm_chunk, 0)
    hot = (lax.broadcasted_iota(jnp.int32, (8, WIDTH), 1) == WIDTH - 1).astype(jnp.bfloat16)
    for micro in range(2):
        here = slice(micro * 128, micro * 128 + 128)
        own = tok[micro, pl.ds(first_row, 128), :]
        own_out[here, :] = own
        query = dot(normed[micro, pl.ds(first_row, 128), :], wqkv[:, :HALF])
        query = query.astype(jnp.bfloat16) * jnp.bfloat16(0.125)
        query_out[here, :] = query
        query_seg = dot_nt(hot, own)[0:1, :]
        key_seg = tok[micro, :, WIDTH - 1 :].astype(jnp.float32)
        key_pos = lax.broadcasted_iota(jnp.int32, (POSITIONS, 128), 0)
        query_pos = first_row + lax.broadcasted_iota(jnp.int32, (POSITIONS, 128), 1)
        seen = (key_pos <= query_pos) & ((key_seg == 0.0) | (key_seg == query_seg))
        one = jnp.where(seen, 0.0, -1e30)
        bias[:, :128] = one
        bias[:, 128:] = one
        for pair in range(3):
            cols = slice(pair * 128, pair * 128 + 128)
            stacked = split_heads(query[:, cols])
            scores = dot_nt(kv[micro, :, cols], stacked) + bias[...]
            top = jnp.max(scores, axis=0, keepdims=True)
            terms = jnp.exp(scores - top)
            total = jnp.sum(terms, axis=0, keepdims=True)
            weights = (terms * (1.0 / total)).astype(jnp.bfloat16)
            soft[micro * 3 + pair] = weights
            value = kv[micro, :, HALF + pair * 128 : HALF + pair * 128 + 128]
            mixed = dot_tn(value, weights)
            attn_out[here, cols] = join_heads(mixed.T).astype(jnp.bfloat16)


def feed_half(normed, cot, up, down, g_up, g_down):
    slope = math.sqrt(2.0 / math.pi)
    hidden = dot(normed, up[...])
    square = hidden * hidden
    wave = jnp.tanh(slope * hidden * (1.0 + 0.044715 * square))
    active = (0.5 * hidden * (1.0 + wave)).astype(jnp.bfloat16)
    grow = 0.5 * (1.0 + wave) + 0.5 * hidden * (1.0 - wave * wave) * slope * (
        1.0 + 3.0 * 0.044715 * square
    )
    d_hidden = (dot_nt(cot, down[...]) * grow).astype(jnp.bfloat16)
    g_up[...] = dot_tn(normed, d_hidden).astype(jnp.bfloat16)
    g_down[...] = dot_tn(active, cot).astype(jnp.bfloat16)
    return dot(active, down[...]), dot_nt(d_hidden, up[...])


def feed_first_kernel(
    ids, gains, attn_mine, attn_other, own, wout_mine, wout_other, cot_mine, cot_other,
    w0, w1, w2, w3,
    attn_out, cot_out, res_out, normed_out, sum_mix, sum_norm, g0, g1, g2, g3,
    up, down, g_up, g_down,
):
    chip, core = ids[0], ids[1]
    take_pieces((w0, w1), up, chip, 0)
    take_pieces((w2, w3), down, chip, 1)
    mine_at = pl.multiple_of(core * HALF, 128)
    other_at = pl.multiple_of((1 - core) * HALF, 128)
    attn_out[:, pl.ds(mine_at, HALF)] = attn_mine[...]
    attn_out[:, pl.ds(other_at, HALF)] = attn_other[...]
    for micro in range(2):
        for side, source in ((core, cot_mine), (1 - core, cot_other)):
            at = pl.multiple_of(micro * 128 + side * 64, 64)
            cot_out[pl.ds(at, 64), :] = source[micro]
    lane = lanes(ROWS)
    attn = attn_out[...]
    res_out[:, pl.ds(mine_at, HALF)] = dot(attn, wout_mine[...])
    res_out[:, pl.ds(other_at, HALF)] = dot(attn, wout_other[...])
    own_values = jnp.where(lane < WIDTH - 1, own[...].astype(jnp.float32), 0.0)
    residual = res_out[...] + own_values
    res_out[...] = residual
    normed = (norm_rows(residual, lane)[0] * gains[1:2, :]).astype(jnp.bfloat16)
    normed_out[...] = normed
    mix, norm = feed_half(normed, cot_out[...], up, down, g_up, g_down)
    sum_mix[...] = mix
    sum_norm[...] = norm
    give_pieces((g0, g1), g_up, chip, 0)
    give_pieces((g2, g3), g_down, chip, 1)


def feed_second_kernel(
    ids, normed, cot, mix_in, norm_in, w0, w1, w2, w3,
    part_out, g0, g1, g2, g3,
    up, down, g_up, g_down,
):
    chip = ids[0]
    take_pieces((w0, w1), up, chip, 0)
    take_pieces((w2, w3), down, chip, 1)
    mix, norm = feed_half(normed[...], cot[...], up, down, g_up, g_down)
    part_out[:ROWS, :] = (mix_in[...] + mix).astype(jnp.bfloat16)
    part_out[ROWS:, :] = (norm_in[...] + norm).astype(jnp.bfloat16)
    give_pieces((g0, g1), g_up, chip, 0)
    give_pieces((g2, g3), g_down, chip, 1)


def backward_kernel(
    ids, gains, residual, part_mine, part_other, cot, wout_mine, wout_other, query,
    wqkv, kv, soft,
    mixed_out, dres_out, d_query, d_sum_half, keep_rows, send_rows, d_kv,
    d_attn, d_rows, d_sum_ref, hold,
):
    chip, core = ids[0], ids[1]
    place = lax.rem(chip, 8)
    first_row = pl.multiple_of(place * 128, 128)
    mine_at = pl.multiple_of(core * HALF, 128)
    other_at = pl.multiple_of((1 - core) * HALF, 128)
    lane = lanes(ROWS)
    res = residual[...]
    hold[...] = add(res, part_mine[:ROWS, :], part_other[:ROWS, :])
    for micro in range(2):
        at = pl.multiple_of(micro * 128 + core * 64, 64)
        mixed_out[micro] = hold[pl.ds(at, 64), : WIDTH - 1].astype(jnp.bfloat16)
    d_normed = add(part_mine[ROWS:, :], part_other[ROWS:, :]) * gains[1:2, :]
    normed_two, factor = norm_rows(res, lane)
    d_res = cot[...].astype(jnp.float32) + norm_rows_back(d_normed, normed_two, factor, lane)
    hold[...] = d_res
    for micro in range(2):
        at = pl.multiple_of(micro * 128 + core * 64, 64)
        dres_out[micro] = hold[pl.ds(at, 64), :]
    d_sum_ref[...] = d_res.astype(jnp.bfloat16)
    d_mine = d_sum_ref[:, pl.ds(mine_at, HALF)]
    d_other = d_sum_ref[:, pl.ds(other_at, HALF)]
    d_sum_half[...] = d_mine
    d_heads = dot_nt(d_mine, wout_mine[pl.ds(mine_at, HALF), :]) + dot_nt(
        d_other, wout_other[pl.ds(mine_at, HALF), :]
    )
    d_attn[...] = d_heads.astype(jnp.bfloat16)
    for micro in range(2):
        here = slice(micro * 128, micro * 128 + 128)
        for pair in range(3):
            cols = slice(pair * 128, pair * 128 + 128)
            value_cols = slice(HALF + pair * 128, HALF + pair * 128 + 128)
            d_out = split_heads(d_attn[here, cols])
            weights = soft[micro * 3 + pair]
            d_soft = dot_nt(kv[micro, :, value_cols], d_out)
            weights_f = weights.astype(jnp.float32)
            delta = jnp.sum(weights_f * d_soft, axis=0, keepdims=True)
            d_scores = (weights_f * (d_soft - delta)).astype(jnp.bfloat16)
            d_q = dot_tn(kv[micro, :, cols], d_scores) * 0.125
            d_query[here, cols] = join_heads(d_q.T).astype(jnp.bfloat16)
            d_kv[micro, :, cols] = dot(d_scores, split_heads(query[here, cols])).astype(
                jnp.bfloat16
            )
            d_kv[micro, :, value_cols] = dot(weights, d_out).astype(jnp.bfloat16)
        def row_chunk(chunk, carry, micro=micro):
            at = pl.ds(pl.multiple_of(chunk * ROWS, ROWS), ROWS)
            rows = dot_nt(d_kv[micro, at, :], wqkv[:, HALF : 3 * HALF])
            d_rows[micro, at, :] = rows.astype(jnp.bfloat16)
            return carry

        lax.fori_loop(0, POSITIONS // ROWS, row_chunk, 0)
        own = d_rows[micro, pl.ds(first_row, 128), :].astype(jnp.float32)
        own = own + dot_nt(d_query[here, :], wqkv[:, :HALF])
        d_rows[micro, pl.ds(first_row, 128), :] = own.astype(jnp.bfloat16)
        def part_rows(entry, carry, micro=micro):
            keep_rows[entry, micro] = d_rows[micro, row_block(entry, place, core), :]
            send_rows[entry, micro] = d_rows[micro, row_block(entry, place, 1 - core), :]
            return carry

        lax.fori_loop(0, 8, part_rows, 0)


def gradient_kernel(
    ids, attn, d_sum_half, d_query, d_kv, normed, g0, g1, g2, g3, g_a, g_b
):
    chip = ids[0]
    first_row = pl.multiple_of(lax.rem(chip, 8) * 128, 128)
    g_b[...] = dot_tn(attn[...], d_sum_half[...]).astype(jnp.bfloat16)
    own_0 = normed[0, pl.ds(first_row, 128), :]
    own_1 = normed[1, pl.ds(first_row, 128), :]
    g_a[:, :HALF] = (dot_tn(own_0, d_query[:128, :]) + dot_tn(own_1, d_query[128:, :])).astype(
        jnp.bfloat16
    )
    g_a[:, HALF:] = (dot_tn(normed[0], d_kv[0]) + dot_tn(normed[1], d_kv[1])).astype(jnp.bfloat16)
    give_pieces((g0, g1), g_a, chip, 0)
    give_pieces((g2, g3), g_b, chip, 1)


def tail_kernel(gains, tokens, d_0, d_1, d_2, d_3, d_residual, grad_out):
    lane = lanes(128)
    rows = (128, WIDTH)
    values = tokens[...].reshape(rows).astype(jnp.float32)
    normed, factor = norm_rows(values, lane)
    d_normed = add(d_0[...], d_1[...], d_2[...], d_3[...]).reshape(rows) * gains[0:1, :]
    out = d_residual[...].reshape(rows) + norm_rows_back(d_normed, normed, factor, lane)
    grad_out[...] = out[:, : WIDTH - 1].reshape(2, 64, WIDTH - 1)


VMEM = pl.BlockSpec(memory_space=pltpu.VMEM)
SMEM = pl.BlockSpec(memory_space=pltpu.SMEM)


def shaped(shape, dtype=jnp.bfloat16):
    return jax.ShapeDtypeStruct(shape, dtype)


def call(kernel, ins, outs, scratch, name, mib, flops=0, bytes_accessed=0):
    return pl.pallas_call(
        kernel,
        in_specs=[spec for spec in ins],
        out_specs=[spec for spec, _ in outs],
        out_shape=[shape for _, shape in outs],
        scratch_shapes=scratch,
        name=name,
        cost_estimate=pl.CostEstimate(
            flops=flops, transcendentals=0, bytes_accessed=bytes_accessed
        ),
        compiler_params=pltpu.CompilerParams(vmem_limit_bytes=mib * MIB),
    )


def pick(core, zero, one):
    return jnp.where(core == 0, zero, one)


def chip_block(core, for_zero, for_one):
    mine = pick(core, for_zero, for_one)
    other = swap(pick(core, for_one, for_zero), CORE)
    return jnp.concatenate([pick(core, mine, other), pick(core, other, mine)], axis=0)


def core_rows(core, block):
    rows = block.shape[0] // 2
    mine = pick(core, block[:rows], block[rows:])
    other = swap(pick(core, block[rows:], block[:rows]), CORE)
    return pick(core, mine, other), pick(core, other, mine)


def split_units(w_up, blocks):
    rows = w_up.shape[0]
    parts = w_up.reshape(rows, blocks, 2, 2, -1)
    return [parts[:, :, k].swapaxes(1, 2).reshape(rows, -1) for k in range(2)]


def join_units(first, second, blocks):
    rows = first.shape[0]
    parts = [half.reshape(rows, 2, blocks, -1).swapaxes(1, 2) for half in (first, second)]
    return jnp.stack(parts, axis=2).reshape(rows, -1)


def on_chip_pair(tokens, segments, cotangent, w_qkv, w_out, w_up, w_down, gain_one, gain_two):
    bf, f32 = jnp.bfloat16, jnp.float32
    device = lax.axis_index("head") * 16 + lax.axis_index("blk")
    core = device % 2
    ids = jnp.stack([device // 2, core]).astype(jnp.int32)
    own = jnp.concatenate([tokens[:, 0], segments[:, 0, :, None].astype(bf)], axis=-1)
    cot = jnp.pad(cotangent[:, 0], ((0, 0), (0, 0), (0, 1)))
    four = jnp.stack(
        [
            own,
            swap(own, AXIS_Z_NEAR, upward(AXIS_Z_NEAR)),
            swap(own, AXIS_Z_FAR, upward(AXIS_Z_FAR)),
            swap(own, AXIS_Z_NEAR | AXIS_Z_FAR, upward(AXIS_Z_FAR)),
        ]
    )
    got_x = swap(four, AXIS_X)
    eight = jnp.concatenate([four, got_x], axis=0)
    eight_other = swap(eight, CORE)
    gain_cols = jnp.pad(jnp.stack([gain_one, gain_two], axis=-1), ((0, 0), (0, 126)))
    out_wide = jnp.pad(w_out, ((0, 0), (0, 1)))
    down_wide = jnp.pad(w_down, ((0, 0), (0, 1)))
    qkv_parts = w_qkv.reshape(-1, 3, 2, HALF)
    attn_halves = [
        jnp.concatenate(
            [qkv_parts[:, 0, k], qkv_parts[:, 1, k], qkv_parts[:, 2, k], gain_cols]
            + [out_wide[:, k * HALF : k * HALF + HALF]],
            axis=-1,
        )
        for k in range(2)
    ]
    wide = 3 * HALF + 128
    attn_four = gather_z(chip_block(core, *attn_halves))
    attn_four = fence(*attn_four, got_x)[:4]
    attn_first = gather_first(attn_four, wide)
    up_block = chip_block(core, *split_units(w_up, 16))
    feed_blocks = [
        jnp.concatenate(
            [up_block[:, half * WIDTH :][:, :WIDTH], down_wide[half * 48 : half * 48 + 48]], axis=-1
        )
        for half in range(2)
    ]
    four_0 = gather_z(fence(feed_blocks[0], *attn_four[1:])[0])
    four_1 = gather_z(fence(feed_blocks[1], *four_0[1:])[0])
    attn_pieces = gather_second(*attn_first)
    first_0 = gather_first(fence(*four_0, *attn_first)[:4], WIDTH)
    first_1 = gather_first(fence(*four_1, *first_0)[:4], WIDTH)
    pieces_0 = gather_second(*first_0)
    cot_other = swap(cot, CORE)
    rows_shape = shaped((2, POSITIONS, WIDTH))
    attn, query, own_rows, gains, kv, normed_all, soft, wqkv, wout = call(
        forward_kernel,
        [SMEM] + [VMEM] * 6,
        [
            (VMEM, shaped((ROWS, HALF))),
            (VMEM, shaped((ROWS, HALF))),
            (VMEM, shaped((ROWS, WIDTH))),
            (VMEM, shaped((8, WIDTH), f32)),
            (VMEM, rows_shape),
            (VMEM, rows_shape),
            (VMEM, shaped((6, POSITIONS, ROWS))),
            (VMEM, shaped((WIDTH, wide))),
            (VMEM, shaped((WIDTH, HALF))),
        ],
        [
            pltpu.VMEM((2, POSITIONS, WIDTH), bf),
            pltpu.VMEM((POSITIONS, ROWS), f32),
        ],
        "attention_forward",
        30,
    )(ids, eight, eight_other, *attn_pieces)
    attn_other = swap(attn, CORE)
    wout_other = swap(wout, CORE)
    pieces_1 = gather_second(*first_1)
    weight_scratch = [pltpu.VMEM((WIDTH, WIDTH), bf)] * 4
    piece_shapes = [(VMEM, shaped((8, 48, WIDTH)))] * 4
    outs = call(
        feed_first_kernel,
        [SMEM] + [VMEM] * 8 + [VMEM] * 4,
        [
            (VMEM, shaped((ROWS, WIDTH))),
            (VMEM, shaped((ROWS, WIDTH))),
            (VMEM, shaped((ROWS, WIDTH), f32)),
            (VMEM, shaped((ROWS, WIDTH))),
            (VMEM, shaped((ROWS, WIDTH), f32)),
            (VMEM, shaped((ROWS, WIDTH), f32)),
        ]
        + piece_shapes,
        weight_scratch,
        "feed_forward_and_back_first",
        20,
    )(
        ids, gains, attn, attn_other, own_rows, wout, wout_other, cot, cot_other, *pieces_0
    )
    attn_all, cot_all, residual, normed_two, sum_mix, sum_norm = outs[:6]
    feed_0 = reduce_start(outs[6:])
    part, *grads_1 = call(
        feed_second_kernel,
        [SMEM] + [VMEM] * 4 + [VMEM] * 4,
        [(VMEM, shaped((2 * ROWS, WIDTH)))] + piece_shapes,
        weight_scratch,
        "feed_forward_and_back_second",
        20,
        2 * 10**10,
        10**8,
    )(ids, normed_two, cot_all, sum_mix, sum_norm, *pieces_1)
    part_other = swap(part, CORE)
    feed_0 = reduce_middle(*feed_0)
    feed_1 = reduce_start(grads_1)
    outs = call(
        backward_kernel,
        [SMEM] + [VMEM] * 11,
        [
            (VMEM, shaped((2, 64, WIDTH - 1))),
            (VMEM, shaped((2, 64, WIDTH), f32)),
            (VMEM, shaped((ROWS, HALF))),
            (VMEM, shaped((ROWS, HALF))),
            (VMEM, shaped((8, 2, 64, WIDTH))),
            (VMEM, shaped((8, 2, 64, WIDTH))),
            (VMEM, rows_shape),
        ],
        [
            pltpu.VMEM((ROWS, HALF), bf),
            pltpu.VMEM((2, POSITIONS, WIDTH), bf),
            pltpu.VMEM((ROWS, WIDTH), bf),
            pltpu.VMEM((ROWS, WIDTH), f32),
        ],
        "attention_backward",
        30,
    )(
        ids, gains, residual, part, part_other, cot_all, wout, wout_other, query,
        wqkv, kv, soft,
    )
    mixed, d_residual, *outs = outs
    outs, feed_0, feed_1 = fence(outs, feed_0, feed_1)
    d_query, d_sum_half, keep_rows, send_rows, d_kv = outs
    feed_0 = reduce_z(*feed_0)
    feed_1 = reduce_middle(*feed_1)
    got_rows = swap(send_rows, CORE)
    grad_attn_pieces = call(
        gradient_kernel,
        [SMEM] + [VMEM] * 5,
        [(VMEM, shaped((8, 48, 3 * HALF)))] * 2 + [(VMEM, shaped((8, 48, HALF)))] * 2,
        [
            pltpu.VMEM((WIDTH, 3 * HALF), bf),
            pltpu.VMEM((WIDTH, HALF), bf),
        ],
        "attention_weight_gradients",
        20,
    )(ids, attn_all, d_sum_half, d_query, d_kv, normed_all)
    keep_rows, got_rows, grad_attn_pieces, feed_1 = fence(
        keep_rows, got_rows, grad_attn_pieces, feed_1
    )
    crossed = swap(add(keep_rows[4:], got_rows[4:]).astype(bf), AXIS_X)
    attn_first = reduce_start(grad_attn_pieces)
    feed_1 = reduce_z(*feed_1)
    feed_1, crossed, attn_first = fence(feed_1, crossed, attn_first)
    rows_4 = add(keep_rows[:4], got_rows[:4], crossed).astype(bf)
    to_near = swap(rows_4[1], AXIS_Z_NEAR, downward(AXIS_Z_NEAR))
    to_far = swap(rows_4[2], AXIS_Z_FAR, downward(AXIS_Z_FAR))
    to_end = swap(rows_4[3], AXIS_Z_NEAR | AXIS_Z_FAR, downward(AXIS_Z_FAR))
    attn_last = reduce_z(*reduce_middle(*attn_first))
    sum_0, sum_1, attn_sum = add(*feed_0), add(*feed_1), add(*attn_last)
    (grad_tokens,) = call(
        tail_kernel,
        [VMEM] * 7,
        [(VMEM, shaped((2, 64, WIDTH - 1), f32))],
        [],
        "token_gradient",
        8,
        2 * 10**10,
        10**8,
    )(gains, own, rows_4[0], to_near, to_far, to_end, d_residual)
    attn_0, attn_1 = core_rows(core, attn_sum)
    up_sum = jnp.concatenate([sum_0[:, :WIDTH], sum_1[:, :WIDTH]], axis=-1)
    up_0, up_1 = core_rows(core, up_sum)
    grad_qkv = jnp.concatenate(
        [half[:, k * HALF : k * HALF + HALF] for k in range(3) for half in (attn_0, attn_1)],
        axis=-1,
    )
    grad_out = jnp.concatenate([attn_0[:, 3 * HALF :], attn_1[:, 3 * HALF : 4 * HALF - 1]], axis=-1)
    grad_up = join_units(up_0, up_1, 16)
    grad_down = jnp.concatenate([sum_0[:, WIDTH:], sum_1[:, WIDTH:]], axis=0)
    grad_gain_one = jnp.sum(grad_qkv * w_qkv.astype(f32), axis=-1) / gain_one.astype(f32)
    grad_gain_two = jnp.sum(grad_up * w_up.astype(f32), axis=-1) / gain_two.astype(f32)
    return (
        mixed[:, None],
        grad_tokens[:, None],
        grad_qkv,
        grad_out,
        grad_up,
        grad_down[:, : WIDTH - 1],
        grad_gain_one,
        grad_gain_two,
    )


def solution(mesh):
    small_slice = (mesh.shape["head"], mesh.shape["blk"]) == (2, 16)
    placed = (
        P(None, "head", "blk", None),
        P(None, "head", "blk"),
        P(None, "head", "blk", None),
        P(("head", "blk"), None),
        P(("head", "blk"), None),
        P(("head", "blk"), None),
        P(("head", "blk"), None),
        P(("head", "blk")),
        P(("head", "blk")),
    )
    return jax.shard_map(
        on_chip_pair if small_slice else on_device,
        mesh=mesh,
        in_specs=placed,
        out_specs=(
            P(None, "head", "blk", None),
            P(None, "head", "blk", None),
            P(("head", "blk"), None),
            P(("head", "blk"), None),
            P(("head", "blk"), None),
            P(("head", "blk"), None),
            P(("head", "blk")),
            P(("head", "blk")),
        ),
        check_vma=False,
    )
```

```python
import math

import jax
import jax.numpy as jnp
from jax import lax
from jax.experimental import pallas as pl
from jax.experimental.pallas import tpu as pltpu
from jax.sharding import PartitionSpec as P

HEAD_DIM = 64


def compress_norm(values, gain):
    total_sum = jnp.sum(values, axis=-1, keepdims=True)
    full_vec = jnp.concatenate([values, -total_sum], axis=-1)
    factor = lax.rsqrt(jnp.mean(full_vec * full_vec, axis=-1, keepdims=True) + 1e-05)
    return full_vec * factor * gain


def gelu_tanh(values):
    return jax.nn.gelu(values, approximate=True)


def visibility(query_pos, query_seg, key_pos, key_seg):
    causal = key_pos[:, None, :] <= query_pos[None, :, None]
    shared = (key_seg[:, None, :] == 0) | (key_seg[:, None, :] == query_seg[:, :, None])
    return (causal & shared)[:, :, None, :]


def micro_step(token_block, segment_block, cotangent_block, weights_full, query_pos):
    proj_qkv, proj_out, proj_up, proj_down, norm_one, norm_two = weights_full
    norm_one = norm_one.astype(jnp.float32)
    norm_two = norm_two.astype(jnp.float32)
    group_local, seg_len, resid_width = token_block.shape
    model_width = proj_qkv.shape[0]
    row_count = group_local * seg_len
    score_scale = 1.0 / math.sqrt(HEAD_DIM)
    token_rows = token_block.astype(jnp.float32).reshape(row_count, resid_width)
    normed_f, norm_one_pull = jax.vjp(compress_norm, token_rows, norm_one)
    normed_one = normed_f.astype(jnp.bfloat16)
    projected = jnp.dot(normed_one, proj_qkv, preferred_element_type=jnp.float32).astype(
        jnp.bfloat16
    )
    projected = projected.reshape(group_local, seg_len, 3, model_width)
    head_groups = lax.axis_size("head")
    seg_wide = jnp.broadcast_to(
        segment_block.astype(jnp.bfloat16)[:, :, None, None], (group_local, seg_len, 1, head_groups)
    )
    moved_qkv, moved_seg = (
        lax.all_to_all(projected, "head", split_axis=3, concat_axis=0, tiled=True),
        lax.all_to_all(seg_wide, "head", split_axis=3, concat_axis=0, tiled=True),
    )
    groups = moved_qkv.shape[0]
    head_width = moved_qkv.shape[3]
    heads_here = head_width // HEAD_DIM
    head_shape = (groups, seg_len, heads_here, HEAD_DIM)
    queries = moved_qkv[:, :, 0].reshape(head_shape)
    keys_flat = moved_qkv[:, :, 1]
    values_flat = moved_qkv[:, :, 2]
    keys_local = keys_flat.reshape(head_shape)
    values_local = values_flat.reshape(head_shape)
    seg_bf = moved_seg[:, :, 0, 0]
    seg_here = seg_bf.astype(jnp.int32)
    key_piece = lax.all_gather(keys_flat, "blk", axis=1, tiled=True)
    value_piece = lax.all_gather(values_flat, "blk", axis=1, tiled=True)
    seg_piece = lax.all_gather(seg_bf, "blk", axis=1, tiled=True)
    key_pos = jnp.arange(key_piece.shape[1], dtype=jnp.int32)[None, :]
    running_max = jnp.full((groups, seg_len, heads_here), -1e30, jnp.float32)
    piece_rows = key_piece.shape[1]
    visible = visibility(query_pos, seg_here, key_pos, seg_piece.astype(jnp.int32))
    key_heads = key_piece.reshape(groups, piece_rows, heads_here, HEAD_DIM)
    value_heads = value_piece.reshape(groups, piece_rows, heads_here, HEAD_DIM)
    scores = score_scale * jnp.einsum(
        "gqhd,gkhd->gqhk", queries, key_heads, preferred_element_type=jnp.float32
    )
    masked = jnp.where(visible, scores, -1e30)
    new_max = jnp.maximum(running_max, jnp.max(masked, axis=-1))
    exp_terms = jnp.where(visible, jnp.exp(masked - new_max[..., None]), 0.0)
    new_sum = jnp.sum(exp_terms, axis=-1)
    new_acc = jnp.einsum(
        "gqhk,gkhd->gqhd",
        exp_terms.astype(jnp.bfloat16),
        value_heads,
        preferred_element_type=jnp.float32,
    )
    attn_f = new_acc / new_sum[..., None]
    log_totals = new_max + jnp.log(new_sum)
    attn_heads = attn_f.astype(jnp.bfloat16).reshape(groups, seg_len, head_width)
    attention = lax.all_to_all(attn_heads, "head", split_axis=0, concat_axis=2, tiled=True)
    attn_rows = attention.reshape(row_count, model_width)
    residual = token_rows + jnp.dot(attn_rows, proj_out, preferred_element_type=jnp.float32)
    normed_two_f, norm_two_pull = jax.vjp(compress_norm, residual, norm_two)
    normed_two = normed_two_f.astype(jnp.bfloat16)
    hidden = jnp.dot(normed_two, proj_up, preferred_element_type=jnp.float32)
    activated_f, gelu_pull = jax.vjp(gelu_tanh, hidden)
    activated = activated_f.astype(jnp.bfloat16)
    mixed = (residual + jnp.dot(activated, proj_down, preferred_element_type=jnp.float32)).astype(
        jnp.bfloat16
    )
    cot_rows = cotangent_block.reshape(row_count, resid_width)
    grad_down = jnp.einsum("ra,rb->ab", activated, cot_rows, preferred_element_type=jnp.float32)
    d_activated = jnp.einsum("rb,ab->ra", cot_rows, proj_down, preferred_element_type=jnp.float32)
    (d_hidden,) = gelu_pull(d_activated)
    d_hidden = d_hidden.astype(jnp.bfloat16)
    grad_up = jnp.einsum("ra,rb->ab", normed_two, d_hidden, preferred_element_type=jnp.float32)
    d_normed_two = jnp.einsum("rb,ab->ra", d_hidden, proj_up, preferred_element_type=jnp.float32)
    d_resid_part, grad_gain_two = norm_two_pull(d_normed_two)
    d_residual = cot_rows.astype(jnp.float32) + d_resid_part
    d_sum = d_residual.astype(jnp.bfloat16)
    grad_out = jnp.einsum("ra,rb->ab", attn_rows, d_sum, preferred_element_type=jnp.float32)
    d_attention = jnp.einsum(
        "rb,ab->ra", d_sum, proj_out, preferred_element_type=jnp.float32
    ).astype(jnp.bfloat16)
    d_attention = d_attention.reshape(group_local, seg_len, model_width)
    d_heads_flat = lax.all_to_all(d_attention, "head", split_axis=2, concat_axis=0, tiled=True)
    d_heads = d_heads_flat.reshape(head_shape)
    delta_rows = jnp.sum(d_heads.astype(jnp.float32) * attn_f, axis=-1)
    lse_all, delta_all = (
        lax.all_gather(log_totals, "blk", axis=1, tiled=True),
        lax.all_gather(delta_rows, "blk", axis=1, tiled=True),
    )
    key_piece = lax.all_gather(keys_flat, "blk", axis=1, tiled=True)
    value_piece = lax.all_gather(values_flat, "blk", axis=1, tiled=True)
    seg_piece = lax.all_gather(seg_bf, "blk", axis=1, tiled=True)
    key_pos = jnp.arange(key_piece.shape[1], dtype=jnp.int32)[None, :]
    piece_rows = key_piece.shape[1]
    visible = visibility(query_pos, seg_here, key_pos, seg_piece.astype(jnp.int32))
    key_heads = key_piece.reshape(groups, piece_rows, heads_here, HEAD_DIM)
    value_heads = value_piece.reshape(groups, piece_rows, heads_here, HEAD_DIM)
    scores = score_scale * jnp.einsum(
        "gqhd,gkhd->gqhk", queries, key_heads, preferred_element_type=jnp.float32
    )
    masked = jnp.where(visible, scores, -1e30)
    soft_weights = jnp.where(visible, jnp.exp(masked - log_totals[..., None]), 0.0)
    d_soft = jnp.einsum("gqhd,gkhd->gqhk", d_heads, value_heads, preferred_element_type=jnp.float32)
    d_scores = (soft_weights * (d_soft - delta_rows[..., None])).astype(jnp.bfloat16)
    d_query = score_scale * jnp.einsum(
        "gqhk,gkhd->gqhd", d_scores, key_heads, preferred_element_type=jnp.float32
    )
    queries_flat = moved_qkv[:, :, 0]
    query_piece = lax.all_gather(queries_flat, "blk", axis=1, tiled=True)
    dout_piece = lax.all_gather(d_heads_flat, "blk", axis=1, tiled=True)
    seg_piece = lax.all_gather(seg_bf, "blk", axis=1, tiled=True)
    piece_rows = query_piece.shape[1]
    piece_pos = jnp.arange(piece_rows, dtype=jnp.int32)
    visible = visibility(piece_pos, seg_piece.astype(jnp.int32), query_pos[None, :], seg_here)
    query_heads = query_piece.reshape(groups, piece_rows, heads_here, HEAD_DIM)
    dout_heads = dout_piece.reshape(groups, piece_rows, heads_here, HEAD_DIM)
    scores = score_scale * jnp.einsum(
        "gqhd,gkhd->gqhk", query_heads, keys_local, preferred_element_type=jnp.float32
    )
    masked = jnp.where(visible, scores, -1e30)
    soft_weights = jnp.where(visible, jnp.exp(masked - lse_all[..., None]), 0.0)
    d_soft = jnp.einsum(
        "gqhd,gkhd->gqhk", dout_heads, values_local, preferred_element_type=jnp.float32
    )
    d_scores = (soft_weights * (d_soft - delta_all[..., None])).astype(jnp.bfloat16)
    new_value = jnp.einsum(
        "gqhk,gqhd->gkhd",
        soft_weights.astype(jnp.bfloat16),
        dout_heads,
        preferred_element_type=jnp.float32,
    )
    new_key = score_scale * jnp.einsum(
        "gqhk,gqhd->gkhd", d_scores, query_heads, preferred_element_type=jnp.float32
    )
    d_stacked = (
        jnp.stack([d_query, new_key, new_value], axis=2)
        .astype(jnp.bfloat16)
        .reshape(groups, seg_len, 3, head_width)
    )
    d_projected = lax.all_to_all(d_stacked, "head", split_axis=0, concat_axis=3, tiled=True)
    d_proj_rows = d_projected.reshape(row_count, 3 * model_width)
    grad_qkv = jnp.einsum("ra,rb->ab", normed_one, d_proj_rows, preferred_element_type=jnp.float32)
    d_normed_one = jnp.einsum(
        "rb,ab->ra", d_proj_rows, proj_qkv, preferred_element_type=jnp.float32
    )
    d_token_part, grad_gain_one = norm_one_pull(d_normed_one)
    grad_tokens = (d_residual + d_token_part).reshape(group_local, seg_len, resid_width)
    mixed = mixed.reshape(group_local, seg_len, resid_width)
    return (
        mixed,
        grad_tokens,
        (grad_qkv, grad_out, grad_up, grad_down, grad_gain_one, grad_gain_two),
    )


def on_device(tokens, segments, cotangent, w_qkv, w_out, w_up, w_down, gain_one, gain_two):
    micro_count = tokens.shape[0]
    seg_len = tokens.shape[2]
    query_pos = lax.axis_index("blk") * seg_len + jnp.arange(seg_len, dtype=jnp.int32)
    mixed_list = []
    token_grad_list = []
    grad_terms = []
    for batch_index in range(micro_count):
        weights_full = (
            lax.all_gather(w_qkv, ("head", "blk"), axis=0, tiled=True),
            lax.all_gather(w_out, ("head", "blk"), axis=0, tiled=True),
            lax.all_gather(w_up, ("head", "blk"), axis=0, tiled=True),
            lax.all_gather(w_down, ("head", "blk"), axis=0, tiled=True),
            lax.all_gather(gain_one, ("head", "blk"), axis=0, tiled=True),
            lax.all_gather(gain_two, ("head", "blk"), axis=0, tiled=True),
        )
        mixed, grad_tokens, gradients = micro_step(
            tokens[batch_index],
            segments[batch_index],
            cotangent[batch_index],
            weights_full,
            query_pos,
        )
        mixed_list.append(mixed)
        token_grad_list.append(grad_tokens)
        grad_terms.append(
            (
                lax.psum_scatter(gradients[0], ("head", "blk"), scatter_dimension=0, tiled=True),
                lax.psum_scatter(gradients[1], ("head", "blk"), scatter_dimension=0, tiled=True),
                lax.psum_scatter(gradients[2], ("head", "blk"), scatter_dimension=0, tiled=True),
                lax.psum_scatter(gradients[3], ("head", "blk"), scatter_dimension=0, tiled=True),
                lax.psum_scatter(gradients[4], ("head", "blk"), scatter_dimension=0, tiled=True),
                lax.psum_scatter(gradients[5], ("head", "blk"), scatter_dimension=0, tiled=True),
            )
        )
    summed = grad_terms[0]
    for later_terms in grad_terms[1:]:
        summed = tuple((first + second for first, second in zip(summed, later_terms)))
    mixed_all = jnp.stack(mixed_list, axis=0)
    token_grads = jnp.stack(token_grad_list, axis=0)
    return (
        mixed_all,
        token_grads,
        summed[0],
        summed[1],
        summed[2],
        summed[3],
        summed[4],
        summed[5],
    )


CORE, AXIS_X, AXIS_Z_NEAR, AXIS_Z_FAR, AXIS_Y = 1, 2, 4, 8, 16
DEVICES = 32
WIDTH = 768
HALF = 384
UNITS = 1536
ROWS = 256
POSITIONS = 1024
MIB = 1024 * 1024


def swap(array, bit, keep=lambda source: True):
    pairs = [(i, i ^ bit) for i in range(DEVICES) if keep(i)]
    return lax.ppermute(array, ("head", "blk"), pairs)


def upward(bit):
    return lambda source: source & bit == 0


def downward(bit):
    return lambda source: source & bit != 0


def dot(a, b):
    return lax.dot_general(a, b, (((1,), (0,)), ((), ())), preferred_element_type=jnp.float32)


def dot_nt(a, b):
    return lax.dot_general(a, b, (((1,), (1,)), ((), ())), preferred_element_type=jnp.float32)


def dot_tn(a, b):
    return lax.dot_general(a, b, (((0,), (0,)), ((), ())), preferred_element_type=jnp.float32)


def lanes(rows):
    return lax.broadcasted_iota(jnp.int32, (rows, WIDTH), 1)


def norm_rows(values, lane):
    inner = jnp.where(lane < WIDTH - 1, values, 0.0)
    total = jnp.sum(inner, axis=-1, keepdims=True)
    full = jnp.where(lane == WIDTH - 1, -total, inner)
    factor = lax.rsqrt(jnp.mean(full * full, axis=-1, keepdims=True) + 1e-05)
    return full * factor, factor


def norm_rows_back(d_normed, normed, factor, lane):
    inner = jnp.mean(d_normed * normed, axis=-1, keepdims=True)
    d_full = factor * (d_normed - normed * inner)
    last = jnp.sum(jnp.where(lane == WIDTH - 1, d_full, 0.0), axis=-1, keepdims=True)
    return jnp.where(lane < WIDTH - 1, d_full - last, 0.0)


def piece_chip(which, pair, entry):
    z_bits = (entry & 3) << 1
    other = entry >> 2
    return z_bits | ((other | pair << 3) if which == 0 else (other << 3 | pair))


def gather_z(block):
    near = swap(block, AXIS_Z_NEAR)
    far = swap(block, AXIS_Z_FAR)
    end = swap(block, AXIS_Z_NEAR | AXIS_Z_FAR)
    return block, near, far, end


def gather_z_twice(block):
    near = swap(block, AXIS_Z_NEAR)
    far = swap(jnp.stack([block, near]), AXIS_Z_FAR)
    return block, near, far[0], far[1]


def gather_first(four, cut):
    four_a = jnp.stack([array[:, :cut] for array in four])
    four_b = jnp.stack([array[:, cut:] for array in four])
    return four_a, swap(four_a, AXIS_X), four_b, swap(four_b, AXIS_Y)


def gather_second(four_a, got_a, four_b, got_b):
    eight_a = jnp.concatenate([four_a, got_a], axis=0)
    eight_b = jnp.concatenate([four_b, got_b], axis=0)
    return eight_a, swap(eight_a, AXIS_Y), eight_b, swap(eight_b, AXIS_X)


def add(first, *others):
    total = first.astype(jnp.float32)
    for other in others:
        total = total + other.astype(jnp.float32)
    return total


def reduce_start(pieces):
    keep_a, send_a, keep_b, send_b = pieces
    return keep_a, swap(send_a, AXIS_Y), keep_b, swap(send_b, AXIS_X)


def reduce_middle(keep_a, got_a, keep_b, got_b):
    send_a = add(keep_a[4:], got_a[4:]).astype(jnp.bfloat16)
    send_b = add(keep_b[4:], got_b[4:]).astype(jnp.bfloat16)
    left_a = (keep_a[:4], got_a[:4], swap(send_a, AXIS_X))
    left_b = (keep_b[:4], got_b[:4], swap(send_b, AXIS_Y))
    return left_a, left_b


def along_z(four):
    near = swap(four[1], AXIS_Z_NEAR)
    far = swap(four[2], AXIS_Z_FAR)
    end = swap(four[3], AXIS_Z_NEAR | AXIS_Z_FAR)
    return near, far, end


def reduce_z(left_a, left_b):
    four = jnp.concatenate([add(*left_a), add(*left_b)], axis=-1).astype(jnp.bfloat16)
    return (four[0], *along_z(four))


def fence(*arrays):
    return lax.optimization_barrier(arrays)


def after(arrays, *others):
    return fence(*arrays, *others)[: len(arrays)]


def piece_rows(chip, which, pair, entry):
    return pl.ds(pl.multiple_of((chip ^ piece_chip(which, pair, entry)) * 48, 16), 48)


def take_pieces(pieces, target, chip, which):
    def move(entry, carry):
        for pair in range(2):
            target[piece_rows(chip, which, pair, entry), :] = pieces[pair][entry]
        return carry

    lax.fori_loop(0, 8, move, 0)


def give_pieces(pieces, source, chip, which):
    def move(entry, carry):
        for pair in range(2):
            pieces[pair][entry] = source[piece_rows(chip, which, pair, entry), :]
        return carry

    lax.fori_loop(0, 8, move, 0)


def row_block(entry, place, core):
    rel = (entry & 3) << 1 | entry >> 2
    return pl.ds(pl.multiple_of(((place ^ rel) * 2 + core) * 64, 64), 64)


def split_heads(both):
    small = lax.broadcasted_iota(jnp.int32, both.shape, 1) < HEAD_DIM
    zero = jnp.zeros_like(both)
    return jnp.concatenate([jnp.where(small, both, zero), jnp.where(small, zero, both)], axis=0)


def join_heads(stacked):
    rows = stacked.shape[0] // 2
    small = lax.broadcasted_iota(jnp.int32, (rows, stacked.shape[1]), 1) < HEAD_DIM
    return jnp.where(small, stacked[:rows], stacked[rows:])


def forward_kernel(
    ids, tok_mine, tok_other, w0, w1, w2, w3,
    attn_out, query_out, own_out, gains_out, kv, normed, soft, wqkv, wout,
    tok, bias,
):
    chip, core = ids[0], ids[1]
    place = lax.rem(chip, 8)
    take_pieces((w0, w1), wqkv, chip, 0)
    take_pieces((w2, w3), wout, chip, 1)
    first_row = pl.multiple_of(place * 128, 128)
    lane = lanes(ROWS)
    picks = lax.broadcasted_iota(jnp.int32, (8, 128), 0) == lax.broadcasted_iota(
        jnp.int32, (8, 128), 1
    )
    gains_out[...] = dot_nt(picks.astype(jnp.bfloat16), wqkv[:, 3 * HALF :])
    gain = gains_out[0:1, :]
    for micro in range(2):
        def move(entry, carry, micro=micro):
            tok[micro, row_block(entry, place, core), :] = tok_mine[entry, micro]
            tok[micro, row_block(entry, place, 1 - core), :] = tok_other[entry, micro]
            return carry

        lax.fori_loop(0, 8, move, 0)

        def norm_chunk(chunk, carry, micro=micro):
            rows = pl.ds(pl.multiple_of(chunk * ROWS, ROWS), ROWS)
            values = tok[micro, rows, :].astype(jnp.float32)
            rows_normed = (norm_rows(values, lane)[0] * gain).astype(jnp.bfloat16)
            normed[micro, rows, :] = rows_normed
            kv[micro, rows, :] = dot(rows_normed, wqkv[:, HALF : 3 * HALF]).astype(jnp.bfloat16)
            return carry

        lax.fori_loop(0, POSITIONS // ROWS, norm_chunk, 0)
    hot = (lax.broadcasted_iota(jnp.int32, (8, WIDTH), 1) == WIDTH - 1).astype(jnp.bfloat16)
    for micro in range(2):
        here = slice(micro * 128, micro * 128 + 128)
        own = tok[micro, pl.ds(first_row, 128), :]
        own_out[here, :] = own
        query = dot(normed[micro, pl.ds(first_row, 128), :], wqkv[:, :HALF])
        query = query.astype(jnp.bfloat16) * jnp.bfloat16(0.125)
        query_out[here, :] = query
        query_seg = dot_nt(hot, own)[0:1, :]
        key_seg = tok[micro, :, WIDTH - 1 :].astype(jnp.float32)
        key_pos = lax.broadcasted_iota(jnp.int32, (POSITIONS, 128), 0)
        query_pos = first_row + lax.broadcasted_iota(jnp.int32, (POSITIONS, 128), 1)
        seen = (key_pos <= query_pos) & ((key_seg == 0.0) | (key_seg == query_seg))
        one = jnp.where(seen, 0.0, -1e30)
        bias[:, :128] = one
        bias[:, 128:] = one
        for pair in range(3):
            cols = slice(pair * 128, pair * 128 + 128)
            stacked = split_heads(query[:, cols])
            scores = dot_nt(kv[micro, :, cols], stacked) + bias[...]
            top = jnp.max(scores, axis=0, keepdims=True)
            terms = jnp.exp(scores - top)
            total = jnp.sum(terms, axis=0, keepdims=True)
            weights = (terms * (1.0 / total)).astype(jnp.bfloat16)
            soft[micro * 3 + pair] = weights
            value = kv[micro, :, HALF + pair * 128 : HALF + pair * 128 + 128]
            mixed = dot_tn(value, weights)
            attn_out[here, cols] = join_heads(mixed.T).astype(jnp.bfloat16)


def feed_half(normed, cot, up, down, g_up, g_down):
    slope = math.sqrt(2.0 / math.pi)
    hidden = dot(normed, up[...])
    square = hidden * hidden
    wave = jnp.tanh(slope * hidden * (1.0 + 0.044715 * square))
    active = (0.5 * hidden * (1.0 + wave)).astype(jnp.bfloat16)
    grow = 0.5 * (1.0 + wave) + 0.5 * hidden * (1.0 - wave * wave) * slope * (
        1.0 + 3.0 * 0.044715 * square
    )
    d_hidden = (dot_nt(cot, down[...]) * grow).astype(jnp.bfloat16)
    g_up[...] = dot_tn(normed, d_hidden).astype(jnp.bfloat16)
    g_down[...] = dot_tn(active, cot).astype(jnp.bfloat16)
    return dot(active, down[...]), dot_nt(d_hidden, up[...])


def feed_first_kernel(
    ids, gains, attn_mine, attn_other, own, wout_mine, wout_other, cot_mine, cot_other,
    w0, w1, w2, w3,
    attn_out, cot_out, res_out, normed_out, sum_mix, sum_norm, g0, g1, g2, g3,
    up, down, g_up, g_down,
):
    chip, core = ids[0], ids[1]
    take_pieces((w0, w1), up, chip, 0)
    take_pieces((w2, w3), down, chip, 1)
    mine_at = pl.multiple_of(core * HALF, 128)
    other_at = pl.multiple_of((1 - core) * HALF, 128)
    attn_out[:, pl.ds(mine_at, HALF)] = attn_mine[...]
    attn_out[:, pl.ds(other_at, HALF)] = attn_other[...]
    for micro in range(2):
        for side, source in ((core, cot_mine), (1 - core, cot_other)):
            at = pl.multiple_of(micro * 128 + side * 64, 64)
            cot_out[pl.ds(at, 64), :] = source[micro]
    lane = lanes(ROWS)
    attn = attn_out[...]
    res_out[:, pl.ds(mine_at, HALF)] = dot(attn, wout_mine[...])
    res_out[:, pl.ds(other_at, HALF)] = dot(attn, wout_other[...])
    own_values = jnp.where(lane < WIDTH - 1, own[...].astype(jnp.float32), 0.0)
    residual = res_out[...] + own_values
    res_out[...] = residual
    normed = (norm_rows(residual, lane)[0] * gains[1:2, :]).astype(jnp.bfloat16)
    normed_out[...] = normed
    mix, norm = feed_half(normed, cot_out[...], up, down, g_up, g_down)
    sum_mix[...] = mix
    sum_norm[...] = norm
    give_pieces((g0, g1), g_up, chip, 0)
    give_pieces((g2, g3), g_down, chip, 1)


def feed_second_kernel(
    ids, normed, cot, mix_in, norm_in, w0, w1, w2, w3,
    part_out, g0, g1, g2, g3,
    up, down, g_up, g_down,
):
    chip = ids[0]
    take_pieces((w0, w1), up, chip, 0)
    take_pieces((w2, w3), down, chip, 1)
    mix, norm = feed_half(normed[...], cot[...], up, down, g_up, g_down)
    part_out[:ROWS, :] = (mix_in[...] + mix).astype(jnp.bfloat16)
    part_out[ROWS:, :] = (norm_in[...] + norm).astype(jnp.bfloat16)
    give_pieces((g0, g1), g_up, chip, 0)
    give_pieces((g2, g3), g_down, chip, 1)


def backward_kernel(
    ids, gains, residual, part_mine, part_other, cot, wout_mine, wout_other, query,
    wqkv, kv, soft,
    mixed_out, dres_out, d_query, d_sum_half, keep_rows, send_rows, d_kv,
    d_attn, d_rows, d_sum_ref, hold,
):
    chip, core = ids[0], ids[1]
    place = lax.rem(chip, 8)
    first_row = pl.multiple_of(place * 128, 128)
    mine_at = pl.multiple_of(core * HALF, 128)
    other_at = pl.multiple_of((1 - core) * HALF, 128)
    lane = lanes(ROWS)
    res = residual[...]
    hold[...] = add(res, part_mine[:ROWS, :], part_other[:ROWS, :])
    for micro in range(2):
        at = pl.multiple_of(micro * 128 + core * 64, 64)
        mixed_out[micro] = hold[pl.ds(at, 64), : WIDTH - 1].astype(jnp.bfloat16)
    d_normed = add(part_mine[ROWS:, :], part_other[ROWS:, :]) * gains[1:2, :]
    normed_two, factor = norm_rows(res, lane)
    d_res = cot[...].astype(jnp.float32) + norm_rows_back(d_normed, normed_two, factor, lane)
    hold[...] = d_res
    for micro in range(2):
        at = pl.multiple_of(micro * 128 + core * 64, 64)
        dres_out[micro] = hold[pl.ds(at, 64), :]
    d_sum_ref[...] = d_res.astype(jnp.bfloat16)
    d_mine = d_sum_ref[:, pl.ds(mine_at, HALF)]
    d_other = d_sum_ref[:, pl.ds(other_at, HALF)]
    d_sum_half[...] = d_mine
    d_heads = dot_nt(d_mine, wout_mine[pl.ds(mine_at, HALF), :]) + dot_nt(
        d_other, wout_other[pl.ds(mine_at, HALF), :]
    )
    d_attn[...] = d_heads.astype(jnp.bfloat16)
    for micro in range(2):
        here = slice(micro * 128, micro * 128 + 128)
        for pair in range(3):
            cols = slice(pair * 128, pair * 128 + 128)
            value_cols = slice(HALF + pair * 128, HALF + pair * 128 + 128)
            d_out = split_heads(d_attn[here, cols])
            weights = soft[micro * 3 + pair]
            d_soft = dot_nt(kv[micro, :, value_cols], d_out)
            weights_f = weights.astype(jnp.float32)
            delta = jnp.sum(weights_f * d_soft, axis=0, keepdims=True)
            d_scores = (weights_f * (d_soft - delta)).astype(jnp.bfloat16)
            d_q = dot_tn(kv[micro, :, cols], d_scores) * 0.125
            d_query[here, cols] = join_heads(d_q.T).astype(jnp.bfloat16)
            d_kv[micro, :, cols] = dot(d_scores, split_heads(query[here, cols])).astype(
                jnp.bfloat16
            )
            d_kv[micro, :, value_cols] = dot(weights, d_out).astype(jnp.bfloat16)
        def row_chunk(chunk, carry, micro=micro):
            at = pl.ds(pl.multiple_of(chunk * ROWS, ROWS), ROWS)
            rows = dot_nt(d_kv[micro, at, :], wqkv[:, HALF : 3 * HALF])
            d_rows[micro, at, :] = rows.astype(jnp.bfloat16)
            return carry

        lax.fori_loop(0, POSITIONS // ROWS, row_chunk, 0, unroll=4)
        own = d_rows[micro, pl.ds(first_row, 128), :].astype(jnp.float32)
        own = own + dot_nt(d_query[here, :], wqkv[:, :HALF])
        d_rows[micro, pl.ds(first_row, 128), :] = own.astype(jnp.bfloat16)
        def part_rows(entry, carry, micro=micro):
            keep_rows[entry, micro] = d_rows[micro, row_block(entry, place, core), :]
            send_rows[entry, micro] = d_rows[micro, row_block(entry, place, 1 - core), :]
            return carry

        lax.fori_loop(0, 8, part_rows, 0)


def gradient_kernel(
    ids, attn, d_sum_half, d_query, d_kv, normed, g0, g1, g2, g3, g_a, g_b
):
    chip = ids[0]
    first_row = pl.multiple_of(lax.rem(chip, 8) * 128, 128)
    g_b[...] = dot_tn(attn[...], d_sum_half[...]).astype(jnp.bfloat16)
    own_0 = normed[0, pl.ds(first_row, 128), :]
    own_1 = normed[1, pl.ds(first_row, 128), :]
    g_a[:, :HALF] = (dot_tn(own_0, d_query[:128, :]) + dot_tn(own_1, d_query[128:, :])).astype(
        jnp.bfloat16
    )
    g_a[:, HALF:] = (dot_tn(normed[0], d_kv[0]) + dot_tn(normed[1], d_kv[1])).astype(jnp.bfloat16)
    give_pieces((g0, g1), g_a, chip, 0)
    give_pieces((g2, g3), g_b, chip, 1)


def tail_kernel(gains, tokens, d_0, d_1, d_2, d_3, d_residual, grad_out):
    lane = lanes(128)
    rows = (128, WIDTH)
    values = tokens[...].reshape(rows).astype(jnp.float32)
    normed, factor = norm_rows(values, lane)
    d_normed = add(d_0[...], d_1[...], d_2[...], d_3[...]).reshape(rows) * gains[0:1, :]
    out = d_residual[...].reshape(rows) + norm_rows_back(d_normed, normed, factor, lane)
    grad_out[...] = out[:, : WIDTH - 1].reshape(2, 64, WIDTH - 1)


VMEM = pl.BlockSpec(memory_space=pltpu.VMEM)
SMEM = pl.BlockSpec(memory_space=pltpu.SMEM)


def shaped(shape, dtype=jnp.bfloat16):
    return jax.ShapeDtypeStruct(shape, dtype)


def call(kernel, ins, outs, scratch, name, mib, flops=0, bytes_accessed=0):
    return pl.pallas_call(
        kernel,
        in_specs=[spec for spec in ins],
        out_specs=[spec for spec, _ in outs],
        out_shape=[shape for _, shape in outs],
        scratch_shapes=scratch,
        name=name,
        cost_estimate=pl.CostEstimate(
            flops=flops, transcendentals=0, bytes_accessed=bytes_accessed
        ),
        compiler_params=pltpu.CompilerParams(vmem_limit_bytes=mib * MIB),
    )


def pick(core, zero, one):
    return jnp.where(core == 0, zero, one)


def chip_block(core, for_zero, for_one):
    mine = pick(core, for_zero, for_one)
    other = swap(pick(core, for_one, for_zero), CORE)
    return jnp.concatenate([pick(core, mine, other), pick(core, other, mine)], axis=0)


def core_rows(core, block):
    rows = block.shape[0] // 2
    mine = pick(core, block[:rows], block[rows:])
    other = swap(pick(core, block[rows:], block[:rows]), CORE)
    return pick(core, mine, other), pick(core, other, mine)


def split_units(w_up, blocks):
    rows = w_up.shape[0]
    parts = w_up.reshape(rows, blocks, 2, 2, -1)
    return [parts[:, :, k].swapaxes(1, 2).reshape(rows, -1) for k in range(2)]


def join_units(first, second, blocks):
    rows = first.shape[0]
    parts = [half.reshape(rows, 2, blocks, -1).swapaxes(1, 2) for half in (first, second)]
    return jnp.stack(parts, axis=2).reshape(rows, -1)


def on_chip_pair(tokens, segments, cotangent, w_qkv, w_out, w_up, w_down, gain_one, gain_two):
    bf, f32 = jnp.bfloat16, jnp.float32
    device = lax.axis_index("head") * 16 + lax.axis_index("blk")
    core = device % 2
    ids = jnp.stack([device // 2, core]).astype(jnp.int32)
    own = jnp.concatenate([tokens[:, 0], segments[:, 0, :, None].astype(bf)], axis=-1)
    cot = jnp.pad(cotangent[:, 0], ((0, 0), (0, 0), (0, 1)))
    four = jnp.stack(
        [
            own,
            swap(own, AXIS_Z_NEAR, upward(AXIS_Z_NEAR)),
            swap(own, AXIS_Z_FAR, upward(AXIS_Z_FAR)),
            swap(own, AXIS_Z_NEAR | AXIS_Z_FAR, upward(AXIS_Z_FAR)),
        ]
    )
    got_x = swap(four, AXIS_X)
    eight = jnp.concatenate([four, got_x], axis=0)
    eight_other = swap(eight, CORE)
    gain_cols = jnp.pad(jnp.stack([gain_one, gain_two], axis=-1), ((0, 0), (0, 126)))
    out_wide = jnp.pad(w_out, ((0, 0), (0, 1)))
    down_wide = jnp.pad(w_down, ((0, 0), (0, 1)))
    qkv_parts = w_qkv.reshape(-1, 3, 2, HALF)
    attn_halves = [
        jnp.concatenate(
            [qkv_parts[:, 0, k], qkv_parts[:, 1, k], qkv_parts[:, 2, k], gain_cols]
            + [out_wide[:, k * HALF : k * HALF + HALF]],
            axis=-1,
        )
        for k in range(2)
    ]
    wide = 3 * HALF + 128
    attn_four = gather_z(chip_block(core, *attn_halves))
    attn_first = gather_first(attn_four, wide)
    up_block = chip_block(core, *split_units(w_up, 16))
    feed_blocks = [
        jnp.concatenate(
            [up_block[:, half * WIDTH :][:, :WIDTH], down_wide[half * 48 : half * 48 + 48]], axis=-1
        )
        for half in range(2)
    ]
    four_0 = gather_z_twice(*after((feed_blocks[0],), four))
    four_1 = gather_z_twice(*after((feed_blocks[1],), *four_0[1:]))
    attn_pieces = gather_second(*after(attn_first, *four_0))
    first_0 = gather_first(after(four_0, got_x), WIDTH)
    pieces_0 = gather_second(*after(first_0, *attn_pieces))
    first_1 = gather_first(after(four_1, *first_0), WIDTH)
    cot_other = swap(cot, CORE)
    rows_shape = shaped((2, POSITIONS, WIDTH))
    attn, query, own_rows, gains, kv, normed_all, soft, wqkv, wout = call(
        forward_kernel,
        [SMEM] + [VMEM] * 6,
        [
            (VMEM, shaped((ROWS, HALF))),
            (VMEM, shaped((ROWS, HALF))),
            (VMEM, shaped((ROWS, WIDTH))),
            (VMEM, shaped((8, WIDTH), f32)),
            (VMEM, rows_shape),
            (VMEM, rows_shape),
            (VMEM, shaped((6, POSITIONS, ROWS))),
            (VMEM, shaped((WIDTH, wide))),
            (VMEM, shaped((WIDTH, HALF))),
        ],
        [
            pltpu.VMEM((2, POSITIONS, WIDTH), bf),
            pltpu.VMEM((POSITIONS, ROWS), f32),
        ],
        "attention_forward",
        30,
    )(ids, eight, eight_other, *attn_pieces)
    attn_other = swap(attn, CORE)
    wout_other = swap(wout, CORE)
    pieces_1 = gather_second(*first_1)
    weight_scratch = [pltpu.VMEM((WIDTH, WIDTH), bf)] * 4
    piece_shapes = [(VMEM, shaped((8, 48, WIDTH)))] * 4
    outs = call(
        feed_first_kernel,
        [SMEM] + [VMEM] * 8 + [VMEM] * 4,
        [
            (VMEM, shaped((ROWS, WIDTH))),
            (VMEM, shaped((ROWS, WIDTH))),
            (VMEM, shaped((ROWS, WIDTH), f32)),
            (VMEM, shaped((ROWS, WIDTH))),
            (VMEM, shaped((ROWS, WIDTH), f32)),
            (VMEM, shaped((ROWS, WIDTH), f32)),
        ]
        + piece_shapes,
        weight_scratch,
        "feed_forward_and_back_first",
        20,
        2 * 10**9,
        10**6,
    )(
        ids, gains, attn, attn_other, own_rows, wout, wout_other, cot, cot_other, *pieces_0
    )
    attn_all, cot_all, residual, normed_two, sum_mix, sum_norm = outs[:6]
    feed_0 = reduce_start(outs[6:])
    part, *grads_1 = call(
        feed_second_kernel,
        [SMEM] + [VMEM] * 4 + [VMEM] * 4,
        [(VMEM, shaped((2 * ROWS, WIDTH)))] + piece_shapes,
        weight_scratch,
        "feed_forward_and_back_second",
        20,
        2 * 10**9,
        10**6,
    )(ids, normed_two, cot_all, sum_mix, sum_norm, *pieces_1)
    part_other = swap(part, CORE)
    feed_0 = reduce_middle(*feed_0)
    feed_1 = reduce_start(grads_1)
    outs = call(
        backward_kernel,
        [SMEM] + [VMEM] * 11,
        [
            (VMEM, shaped((2, 64, WIDTH - 1))),
            (VMEM, shaped((2, 64, WIDTH), f32)),
            (VMEM, shaped((ROWS, HALF))),
            (VMEM, shaped((ROWS, HALF))),
            (VMEM, shaped((8, 2, 64, WIDTH))),
            (VMEM, shaped((8, 2, 64, WIDTH))),
            (VMEM, rows_shape),
        ],
        [
            pltpu.VMEM((ROWS, HALF), bf),
            pltpu.VMEM((2, POSITIONS, WIDTH), bf),
            pltpu.VMEM((ROWS, WIDTH), bf),
            pltpu.VMEM((ROWS, WIDTH), f32),
        ],
        "attention_backward",
        30,
    )(
        ids, gains, residual, part, part_other, cot_all, wout, wout_other, query,
        wqkv, kv, soft,
    )
    mixed, d_residual, *outs = outs
    outs, feed_1 = fence(outs, feed_1)
    d_query, d_sum_half, keep_rows, send_rows, d_kv = outs
    feed_0 = reduce_z(*feed_0)
    feed_1 = reduce_middle(*feed_1)
    got_rows = swap(send_rows, CORE)
    grad_attn_pieces = call(
        gradient_kernel,
        [SMEM] + [VMEM] * 5,
        [(VMEM, shaped((8, 48, 3 * HALF)))] * 2 + [(VMEM, shaped((8, 48, HALF)))] * 2,
        [
            pltpu.VMEM((WIDTH, 3 * HALF), bf),
            pltpu.VMEM((WIDTH, HALF), bf),
        ],
        "attention_weight_gradients",
        20,
        2 * 10**10,
        10**8,
    )(ids, attn_all, d_sum_half, d_query, d_kv, normed_all)
    keep_rows, got_rows, grad_attn_pieces, feed_1 = fence(
        keep_rows, got_rows, grad_attn_pieces, feed_1
    )
    crossed = swap(add(keep_rows[4:], got_rows[4:]).astype(bf), AXIS_X)
    attn_first = reduce_start(grad_attn_pieces)
    feed_1 = reduce_z(*feed_1)
    feed_0, feed_1, crossed = fence(feed_0, feed_1, crossed)
    rows_4 = add(keep_rows[:4], got_rows[:4], crossed).astype(bf)
    to_near = swap(rows_4[1], AXIS_Z_NEAR, downward(AXIS_Z_NEAR))
    to_far = swap(rows_4[2], AXIS_Z_FAR, downward(AXIS_Z_FAR))
    to_end = swap(rows_4[3], AXIS_Z_NEAR | AXIS_Z_FAR, downward(AXIS_Z_FAR))
    attn_last = reduce_z(*reduce_middle(*attn_first))
    sum_0, sum_1, attn_sum = add(*feed_0), add(*feed_1), add(*attn_last)
    (grad_tokens,) = call(
        tail_kernel,
        [VMEM] * 7,
        [(VMEM, shaped((2, 64, WIDTH - 1), f32))],
        [],
        "token_gradient",
        8,
        2 * 10**10,
        10**8,
    )(gains, own, rows_4[0], to_near, to_far, to_end, d_residual)
    attn_0, attn_1 = core_rows(core, attn_sum)
    up_sum = jnp.concatenate([sum_0[:, :WIDTH], sum_1[:, :WIDTH]], axis=-1)
    up_0, up_1 = core_rows(core, up_sum)
    grad_qkv = jnp.concatenate(
        [half[:, k * HALF : k * HALF + HALF] for k in range(3) for half in (attn_0, attn_1)],
        axis=-1,
    )
    grad_out = jnp.concatenate([attn_0[:, 3 * HALF :], attn_1[:, 3 * HALF : 4 * HALF - 1]], axis=-1)
    grad_up = join_units(up_0, up_1, 16)
    grad_down = jnp.concatenate([sum_0[:, WIDTH:], sum_1[:, WIDTH:]], axis=0)
    grad_gain_one = jnp.sum(grad_qkv * w_qkv.astype(f32), axis=-1) / gain_one.astype(f32)
    grad_gain_two = jnp.sum(grad_up * w_up.astype(f32), axis=-1) / gain_two.astype(f32)
    return (
        mixed[:, None],
        grad_tokens[:, None],
        grad_qkv,
        grad_out,
        grad_up,
        grad_down[:, : WIDTH - 1],
        grad_gain_one,
        grad_gain_two,
    )


def solution(mesh):
    small_slice = (mesh.shape["head"], mesh.shape["blk"]) == (2, 16)
    placed = (
        P(None, "head", "blk", None),
        P(None, "head", "blk"),
        P(None, "head", "blk", None),
        P(("head", "blk"), None),
        P(("head", "blk"), None),
        P(("head", "blk"), None),
        P(("head", "blk"), None),
        P(("head", "blk")),
        P(("head", "blk")),
    )
    return jax.shard_map(
        on_chip_pair if small_slice else on_device,
        mesh=mesh,
        in_specs=placed,
        out_specs=(
            P(None, "head", "blk", None),
            P(None, "head", "blk", None),
            P(("head", "blk"), None),
            P(("head", "blk"), None),
            P(("head", "blk"), None),
            P(("head", "blk"), None),
            P(("head", "blk")),
            P(("head", "blk")),
        ),
        check_vma=False,
    )
```
